32 devices in a mesh: groups: 2 (over x), mp: 4 (over y, core), dp: 4 (over z).
Axes of the slice: x: 2, y: 2, z: 4, core: 2. Of those that a mesh axis runs over, the one named last changes fastest.
Arguments:
- grid_feat: bfloat16 [8, 512, 1024], P(('groups', 'dp'), 'mp'), parts along dimension 0, may hold values from -6 to 6
- node_feat: bfloat16 [8, 256, 1024], P(('groups', 'dp'), 'mp'), parts along dimension 0, may hold values from -6 to 6
- cotangent: bfloat16 [8, 512, 1024], P(('groups', 'dp'), 'mp'), parts along dimension 0, may hold values from -6 to 6
- w_query: bfloat16 [1024, 1024], replicated, may hold values from -2 to 2, as said below
- w_keyval: bfloat16 [1024, 2048], replicated, may hold values from -2 to 2, as said below
- neighbours: int32 [512, 12], P('mp'), may hold values from 0 to 127, as said below
- send_rows: int32 [4, 4, 16], P('mp'), may hold values from 0 to 63, as said below
Outputs:
- d_grid: bfloat16 [8, 512, 1024], P(('groups', 'dp'), 'mp'), parts along dimension 0
- d_nodes: bfloat16 [8, 256, 1024], P(('groups', 'dp'), 'mp'), parts along dimension 0
- dw_query: float32 [2048, 1024], P(('groups', 'mp', 'dp')), parts along dimension 0
- dw_keyval: float32 [2048, 2048], P(('groups', 'mp', 'dp')), parts along dimension 0
The draws below stay inside these ranges and needn't reach their ends.
There are 2 independent parts, one for each index of `groups`. The reference program is written for one: setup_inputs(seed, part) draws one part's arguments, and reference() takes and returns one part's arrays. A program takes and returns all parts, laid end to end along the dimension named above; an argument that names none is the same for every part. Nothing has to cross between parts.
Inputs may be any that keep to these rules, and one draw needn't show every extreme that they name: `neighbours`: an entry under 4 * 16 names slot r % 16 of the block that index r // 16 of mp sends to the grid point's own index; larger entries name the own index's nodes. The slots that are named in a block form a leading run; every index names all 16 slots of the blocks from the indices one below and one above it on mp (wrapping around), some of every other index's block, and none of its own block. `send_rows`: the 16 rows of one block are distinct local node rows of the sending index. `w_query`: projection weights. `w_keyval`: projection weights.
All inputs are finite; a program needn't handle non-finite values.
Results may differ from the reference program's by a relative error of at most 0.018.
The reference program's roundings to bfloat16 on the way count: a program that leaves them out, or rounds other values in their place, can miss the bound.
Values may be sent and summed in bfloat16 or wider, within the bound.
A program may use at most 128 MiB of HBM per device.

```python
import jax
import jax.numpy as jnp
from jax import lax

D = 1024
HEADS = 16
NBR = 12
GRID_DEV = 128
NODE_DEV = 64
CAP = 16
SAMPLES = 4
GRID = 512
NODES = 256
N_MP = 4


def plan_counts(key):
    sender = jnp.arange(N_MP)[:, None]
    target = jnp.arange(N_MP)[None, :]
    counts = jax.random.randint(jax.random.fold_in(key, 7), (N_MP, N_MP), max(1, CAP // 4), CAP + 1)
    beside = ((target - sender) % N_MP == 1) | ((sender - target) % N_MP == 1)
    counts = jnp.where(beside, CAP, counts)
    return jnp.where(sender == target, 0, counts).astype(jnp.int32)


def draw_neighbours(key, part):
    counts = plan_counts(key)
    ends = jnp.cumsum(counts, axis=0)
    starts = ends - counts
    total = ends[-1]
    device = jnp.arange(GRID) // GRID_DEV
    total_rows = total[device][:, None]
    pick = jax.random.randint(jax.random.fold_in(key, 11), (GRID, NBR), 0, NODE_DEV + total_rows)
    ends_rows = ends[:, device].T
    source = jnp.sum(ends_rows[:, None, :] <= pick[:, :, None], axis=2)
    source_cl = jnp.minimum(source, N_MP - 1)
    begin = starts[source_cl, device[:, None]]
    remote = source_cl * CAP + (pick - begin)
    local = N_MP * CAP + (pick - total_rows)
    value = jnp.where(pick < total_rows, remote, local)
    first = jnp.arange(GRID) % GRID_DEV
    column = jnp.where(first == 0, N_MP * CAP + NODE_DEV - 1, jnp.where((first == 1) & (device > 0), 0, value[:, 0]))
    value = value.at[:, 0].set(column)
    return value.astype(jnp.int32)


def pin_value(perm, slot, target):
    current = perm[slot]
    perm = jnp.where(perm == target, current, perm)
    return perm.at[slot].set(target)


def draw_send_rows(key, part):
    base = jax.random.fold_in(key, 23)

    def one_block(index):
        perm = jax.random.permutation(jax.random.fold_in(base, index), NODE_DEV)
        pinned = pin_value(pin_value(perm, 0, NODE_DEV - 1), 1, 0)
        return jnp.where(index == 1, pinned, perm)[:CAP]
    rows = jax.vmap(one_block)(jnp.arange(N_MP * N_MP))
    return rows.reshape(N_MP, N_MP, CAP).astype(jnp.int32)


def draw_w_query(key, part):
    base = jnp.clip(jax.random.normal(jax.random.fold_in(key, 31), (D, D), jnp.float32), -4.0, 4.0) * D ** (-0.5)
    return base.astype(jnp.bfloat16)


def draw_w_keyval(key, part):
    base = jnp.clip(jax.random.normal(jax.random.fold_in(key, 37), (D, 2 * D), jnp.float32), -4.0, 4.0) * D ** (-0.5)
    return base.astype(jnp.bfloat16)


def strengthened(values, own_key, source, target, shards_of, factor):
    def block_of(dim):
        return (jnp.arange(values.shape[dim]) // (values.shape[dim] // shards_of)).reshape((-1,) + (1,) * (values.ndim - 1 - dim))

    near = jax.random.permutation(own_key, shards_of)[block_of(target)]
    far = (block_of(target) + shards_of // 2) % shards_of
    return jnp.where((block_of(source) == near) | (block_of(source) == far), factor * values, values)


def block_levels(key, extent, shards, low, high):
    def one(position, blocks):
        heights = jax.random.uniform(jax.random.fold_in(jax.random.fold_in(key, 6), position), (blocks,), jnp.float32, low / len(shards), high / len(shards))
        return jnp.repeat(jnp.exp(heights), extent[position] // blocks).reshape((-1,) + (1,) * (len(extent) - position - 1))

    loudness = one(*shards[0])
    for cut in shards[1:]:
        loudness = loudness * one(*cut)
    return loudness


def bell_draw(own_key, shape, scale, bound, shards=(), held_as=jnp.bfloat16):
    array = jax.random.normal(own_key, shape, jnp.float32) * scale
    if len(shards) > 0:
        array = block_levels(own_key, shape, shards, -0.22, 0.18) * array
    return jnp.clip(array, min=-bound, max=bound).astype(held_as)


def noise_with(rng, extent, scale, limit, shards, heavy, held_as=jnp.bfloat16):
    entries = scale * jax.random.normal(rng, extent, jnp.float32)
    if shards:
        entries = entries * block_levels(rng, extent, shards, -0.22, 0.18)
    return jnp.clip(strengthened(entries, jax.random.fold_in(rng, 3), *heavy), -limit, limit).astype(held_as)


def setup_inputs(seed: int = 0, part: int = 0) -> dict:
    seeds = jax.random.split(jax.random.key(seed), 8)
    part_keys = jax.random.split(jax.random.fold_in(seeds[7], part), 8)
    return {
        "grid_feat": noise_with(part_keys[0], (SAMPLES, GRID, D), 1.0, 6.0, ((0, 4), (1, 4)), (1, 2, 4, 2.0)),
        "node_feat": noise_with(part_keys[1], (SAMPLES, NODES, D), 1.0, 6.0, ((0, 4), (1, 4)), (1, 2, 4, 2.0)),
        "cotangent": bell_draw(part_keys[2], (SAMPLES, GRID, D), 1.0, 6.0, ((0, 4), (1, 4))),
        "w_query": draw_w_query(jax.random.fold_in(seeds[7], 71), part),
        "w_keyval": draw_w_keyval(jax.random.fold_in(seeds[7], 71), part),
        "neighbours": draw_neighbours(jax.random.fold_in(seeds[7], 71), part),
        "send_rows": draw_send_rows(jax.random.fold_in(seeds[7], 71), part),
    }


def edge_grads(query_rows, cot_rows, edges):
    count = query_rows.shape[0]
    width = query_rows.shape[1]
    nbrs = edges.shape[1]
    scale = (width // HEADS) ** -0.5
    query = query_rows.astype(jnp.float32).reshape(count, HEADS, -1)
    cot = cot_rows.astype(jnp.float32).reshape(count, HEADS, -1)
    keys = edges[:, :, :width].astype(jnp.float32).reshape(count, nbrs, HEADS, -1)
    values = edges[:, :, width:].astype(jnp.float32).reshape(count, nbrs, HEADS, -1)
    scores = jnp.einsum('ghe,gkhe->gkh', query, keys) * scale
    attn = jax.nn.softmax(scores, axis=1)
    d_attn = jnp.einsum('ghe,gkhe->gkh', cot, values)
    d_scores = attn * (d_attn - jnp.sum(attn * d_attn, axis=1, keepdims=True))
    d_query = (jnp.einsum('gkh,gkhe->ghe', d_scores, keys) * scale).reshape(count, width).astype(jnp.bfloat16)
    d_keys = d_scores[..., None] * query[:, None] * scale
    d_values = attn[..., None] * cot[:, None]
    contrib = jnp.concatenate([d_keys.reshape(count, nbrs, width), d_values.reshape(count, nbrs, width)], axis=-1)
    return d_query, contrib


def reference(grid_feat, node_feat, cotangent, w_query, w_keyval, neighbours, send_rows):
    shard = (jnp.arange(GRID) // GRID_DEV).astype(jnp.int32)
    remote = neighbours < N_MP * CAP
    source = jnp.minimum(neighbours // CAP, N_MP - 1).astype(jnp.int32)
    slot = (neighbours % CAP).astype(jnp.int32)
    remote_node = source * NODE_DEV + send_rows[source, shard[:, None], slot]
    local_node = shard[:, None] * NODE_DEV + neighbours - N_MP * CAP
    node_id = jnp.where(remote, remote_node, local_node).astype(jnp.int32)
    wscale = 1.0 / (SAMPLES * GRID) ** 0.5
    dims_t = (((0,), (0,)), ((), ()))

    def one_sample(carry, inputs):
        grid_x, node_x, cot = inputs
        query = jnp.dot(grid_x, w_query, preferred_element_type=jnp.float32).astype(jnp.bfloat16)
        keyval = jnp.dot(node_x, w_keyval, preferred_element_type=jnp.float32).astype(jnp.bfloat16)

        def shard_step(acc, index):
            start = (index * GRID_DEV).astype(jnp.int32)
            query_rows = lax.dynamic_slice_in_dim(query, start, GRID_DEV, 0)
            cot_rows = lax.dynamic_slice_in_dim(cot, start, GRID_DEV, 0)
            ids = lax.dynamic_slice_in_dim(node_id, start, GRID_DEV, 0)
            d_query, contrib = edge_grads(query_rows, cot_rows, keyval[ids])
            partial_value = jax.ops.segment_sum(contrib.reshape(-1, 2 * D), ids.reshape(-1), num_segments=NODES)
            partial_value = lax.optimization_barrier(partial_value.astype(jnp.bfloat16))
            return acc + partial_value.astype(jnp.float32), d_query

        dkv_sum, d_query = lax.scan(shard_step, jnp.zeros((NODES, 2 * D), jnp.float32), jnp.arange(N_MP, dtype=jnp.int32))
        d_query = d_query.reshape(GRID, D)
        dkv = dkv_sum.astype(jnp.bfloat16)
        d_grid = jnp.dot(d_query, w_query.T, preferred_element_type=jnp.float32).astype(jnp.bfloat16)
        d_nodes = jnp.dot(dkv, w_keyval.T, preferred_element_type=jnp.float32).astype(jnp.bfloat16)
        grad_q = carry[0] + lax.dot_general(grid_x, d_query, dims_t, preferred_element_type=jnp.float32) * wscale
        grad_kv = carry[1] + lax.dot_general(node_x, dkv, dims_t, preferred_element_type=jnp.float32) * wscale
        return (grad_q, grad_kv), (d_grid, d_nodes)

    start = (jnp.zeros((D, D), jnp.float32), jnp.zeros((D, 2 * D), jnp.float32))
    (grad_q, grad_kv), (d_grid, d_nodes) = lax.scan(one_sample, start, (grid_feat, node_feat, cotangent))
    return d_grid, d_nodes, grad_q, grad_kv
```

```python
import functools
import math

import jax
import jax.numpy as jnp
from jax import lax
from jax.experimental import pallas as pl
from jax.experimental.pallas import tpu as pltpu
from jax.sharding import PartitionSpec as P

HEADS = 16
LANES = 128
MESH = pl.DeviceIdType.MESH
F32 = jnp.float32
BF16 = jnp.bfloat16


def dot_nn(x, y):
    return lax.dot_general(x, y, (((1,), (0,)), ((), ())), preferred_element_type=F32)


def dot_nt(x, y):
    return lax.dot_general(x, y, (((1,), (1,)), ((), ())), preferred_element_type=F32)


def dot_tn(x, y):
    return lax.dot_general(x, y, (((0,), (0,)), ((), ())), preferred_element_type=F32)


def kernel(
    n, nd, wscale,
    gf, nf, cot, wq_h, wkv_h, nbr, sr_col, sr_row,
    dgrid, dnodes, dwq, dwkv,
    wq, wkv, out_feat, tab, q_s, kv_s, count_s, gf_all, nf_all, dq_s, dq_all,
    part_s, ret_s, dkv_s, dkv_all, tq, tkv, rq, rkv, oq, okv, swq, swkv,
    local_sem, feat_ss, feat_rs, half_ss, half_rs, dq_ss, dq_rs, ret_ss, ret_rs,
    dkv_ss, dkv_rs, z_ss, z_rs, sw_ss, sw_rs,
):
    grid_dev, width = gf.shape
    nodes = nf.shape[0]
    slots = sr_col.shape[0]
    rows = slots + nodes
    cap = slots // n
    nbrs = nbr.shape[1]
    a = width // gf_all.shape[2]
    b = n // a
    high = width // a
    wide = width // b
    out_rows = dwq.shape[0]
    head = width // HEADS
    per = LANES // head
    scale = head ** (-0.5)
    me = lax.axis_index("mp")
    zd = lax.axis_index("dp")
    mine_i = me // b
    mine_j = lax.rem(me, b)

    def to_mp(src, dst, ssem, rsem, peer):
        return pltpu.make_async_remote_copy(
            src_ref=src, dst_ref=dst, send_sem=ssem, recv_sem=rsem,
            device_id={"mp": peer}, device_id_type=MESH,
        )

    def to_dp(src, dst, ssem, rsem, peer):
        return pltpu.make_async_remote_copy(
            src_ref=src, dst_ref=dst, send_sem=ssem, recv_sem=rsem,
            device_id={"dp": peer}, device_id_type=MESH,
        )

    def peer_of(o):
        return lax.rem(me + o, n)

    load_q = pltpu.make_async_copy(wq_h, wq, local_sem.at[0])
    load_kv = pltpu.make_async_copy(wkv_h, wkv, local_sem.at[1])
    load_q.start()
    load_kv.start()
    barrier = pltpu.get_barrier_semaphore()
    for o in range(1, n):
        pl.semaphore_signal(barrier, inc=1, device_id={"mp": peer_of(o)}, device_id_type=MESH)
    for o in range(1, nd):
        pl.semaphore_signal(
            barrier, inc=1, device_id={"dp": lax.rem(zd + o, nd)}, device_id_type=MESH
        )
    pick = (sr_col[...] == lax.broadcasted_iota(jnp.int32, (slots, nodes), 1)).astype(BF16)
    out_feat[...] = dot_nn(pick, nf[...]).astype(BF16)
    tab[pl.ds(slots, nodes), :] = nf[...]
    own_slots = pl.ds(pl.multiple_of(me * cap, cap), cap)
    tab[own_slots, :] = jnp.zeros((cap, width), BF16)
    for jb in range(b):
        ret_s[jb, own_slots, :] = jnp.zeros((cap, 2 * wide), BF16)
    pl.semaphore_wait(barrier, n - 1 + nd - 1)

    feat = []
    for o in range(1, n):
        there = pl.ds(pl.multiple_of(peer_of(o) * cap, cap), cap)
        feat.append(
            to_mp(out_feat.at[there], tab.at[own_slots], feat_ss.at[o], feat_rs.at[o], peer_of(o))
        )
        feat[-1].start()

    ids = nbr[...]
    row_id = lax.broadcasted_iota(jnp.int32, (grid_dev, rows), 1)
    count = jnp.zeros((grid_dev, rows), F32)
    for k in range(nbrs):
        count += (ids[:, k : k + 1] == row_id).astype(F32)
    for s in range(per):
        count_s[s * grid_dev : (s + 1) * grid_dev, :] = count
    half_cols = pl.ds(pl.multiple_of(mine_i * high, high), high)
    gf_all[me] = gf[:, half_cols]
    nf_all[me] = nf[:, half_cols]
    load_q.wait()
    q_s[...] = dot_nn(gf[...], wq[...]).astype(BF16)
    for c in feat:
        c.wait_recv()
    half = []
    for o in range(1, n):
        there = pl.ds(pl.multiple_of((peer_of(o) // b) * high, high), high)
        half.append(
            to_mp(nf.at[:, there], nf_all.at[me], half_ss.at[0, o], half_rs.at[0, o], peer_of(o))
        )
        half.append(
            to_mp(gf.at[:, there], gf_all.at[me], half_ss.at[1, o], half_rs.at[1, o], peer_of(o))
        )
    for c in half:
        c.start()
    load_kv.wait()
    kv_s[...] = dot_nn(tab[...], wkv[...]).astype(BF16)

    lane = lax.broadcasted_iota(jnp.int32, (1, LANES), 1)
    keep = [(lane // head) == s for s in range(per)]

    def spread(x):
        return jnp.concatenate([jnp.where(m, x, jnp.zeros_like(x)) for m in keep], axis=0)

    dq_copies = []
    ret_copies = []
    for jb in range(b):

        def one(blk, carry):
            off = pl.multiple_of(jb * wide + blk * LANES, LANES)
            at = pl.ds(off, LANES)
            at_v = pl.ds(pl.multiple_of(width + off, LANES), LANES)
            here = pl.ds(pl.multiple_of(blk * LANES, LANES), LANES)
            here_v = pl.ds(pl.multiple_of(wide + blk * LANES, LANES), LANES)
            qs = spread(q_s[:, at])
            cs = spread(cot[:, at])
            keys = kv_s[:, at]
            values = kv_s[:, at_v]
            times = count_s[...]
            scores = dot_nt(qs, keys) * scale
            d_attn = dot_nt(cs, values)
            top = jnp.max(
                jnp.where(times > 0, scores, -jnp.inf), axis=1, keepdims=True
            )
            e = jnp.where(times > 0, times * jnp.exp(jnp.minimum(scores - top, 0.0)), 0.0)
            attn = e / jnp.sum(e, axis=1, keepdims=True)
            ds = attn * (d_attn - jnp.sum(attn * d_attn, axis=1, keepdims=True)) * scale
            ds = ds.astype(BF16)
            attn = attn.astype(BF16)
            dq = None
            for s in range(per):
                term = dot_nn(
                    ds[s * grid_dev : (s + 1) * grid_dev],
                    jnp.where(keep[s], keys, jnp.zeros_like(keys)),
                )
                dq = term if dq is None else dq + term
            dq_s[jb, :, here] = dq.astype(BF16)
            part_s[jb, :, here] = dot_tn(ds, qs).astype(BF16)
            part_s[jb, :, here_v] = dot_tn(attn, cs).astype(BF16)
            return carry

        lax.fori_loop(0, wide // LANES, one, 0)
        for o in range(1, n):
            peer = peer_of(o)
            c = to_mp(dq_s.at[jb], dq_all.at[me], dq_ss.at[o], dq_rs.at[o], peer)

            @pl.when(lax.rem(peer, b) == jb)
            def _():
                c.start()

        for o in range(1, n):
            there = pl.ds(pl.multiple_of(peer_of(o) * cap, cap), cap)
            c = to_mp(
                part_s.at[jb, there], ret_s.at[jb, own_slots],
                ret_ss.at[jb, o], ret_rs.at[jb, o], peer_of(o),
            )
            c.start()
            ret_copies.append(c)

    dq_all[me] = dq_s[mine_j]
    acc = None
    for jb in range(b):
        term = dot_nt(dq_s[jb], wq[:, jb * wide : (jb + 1) * wide])
        acc = term if acc is None else acc + term
    dgrid[...] = acc.astype(BF16)

    place = (sr_row[...] == lax.broadcasted_iota(jnp.int32, (nodes, slots), 0)).astype(BF16)
    for jb in range(b):
        for o in range(1, n):
            ret_copies[jb * (n - 1) + o - 1].wait_recv()
        dkv = part_s[jb, slots:, :].astype(F32) + dot_nn(place, ret_s[jb])
        dkv_s[jb] = dkv.astype(BF16)
        for o in range(1, n):
            peer = peer_of(o)
            c = to_mp(dkv_s.at[jb], dkv_all.at[me], dkv_ss.at[o], dkv_rs.at[o], peer)

            @pl.when(lax.rem(peer, b) == jb)
            def _():
                c.start()

    dkv_all[me] = dkv_s[mine_j]

    def got(src, dst, ssem, rsem):
        return to_mp(src, dst, ssem, rsem, peer_of(1))

    for c in half:
        c.wait_recv()
    for o in range(1, n):
        got(dq_s.at[0], dq_all.at[me], dq_ss.at[o], dq_rs.at[o]).wait_recv()
    term_q = dot_tn(
        gf_all[...].reshape(n * grid_dev, high), dq_all[...].reshape(n * grid_dev, wide)
    ) * wscale
    term_q = term_q.astype(BF16).reshape(b, nd, out_rows, wide)
    for d in range(nd):
        tq[d] = term_q[:, d]
    z_copies = []
    for o in range(1, nd):
        peer = lax.rem(zd + o, nd)
        z_copies.append(to_dp(tq.at[peer], rq.at[o], z_ss.at[0, o], z_rs.at[0, o], peer))
        z_copies[-1].start()

    acc = None
    for jb in range(b):
        for k in range(2):
            term = dot_nt(
                dkv_s[jb, :, k * wide : (k + 1) * wide],
                wkv[:, k * width + jb * wide : k * width + (jb + 1) * wide],
            )
            acc = term if acc is None else acc + term
    dnodes[...] = acc.astype(BF16)

    for o in range(1, n):
        got(dkv_s.at[0], dkv_all.at[me], dkv_ss.at[o], dkv_rs.at[o]).wait_recv()
    term_kv = dot_tn(
        nf_all[...].reshape(n * nodes, high), dkv_all[...].reshape(n * nodes, 2 * wide)
    ) * wscale
    term_kv = term_kv.astype(BF16).reshape(b, nd, out_rows, 2 * wide)
    for d in range(nd):
        tkv[d] = term_kv[:, d]
    for o in range(1, nd):
        peer = lax.rem(zd + o, nd)
        z_copies.append(to_dp(tkv.at[peer], rkv.at[o], z_ss.at[1, o], z_rs.at[1, o], peer))
        z_copies[-1].start()

    def finish(which, t, r, out, sw, width_out):
        total = t[zd].astype(F32)
        for o in range(1, nd):
            z_copies[which * (nd - 1) + o - 1].wait_recv()
            total += r[o].astype(F32)
        out[...] = total.astype(BF16)
        sent = []
        for o in range(1, b):
            mate = lax.rem(mine_j + o, b)
            c = to_mp(
                out.at[mate], sw.at[o], sw_ss.at[which, o], sw_rs.at[which, o],
                mine_i * b + mate,
            )
            c.start()
            sent.append(c)
        return sent

    sent_q = finish(0, tq, rq, oq, swq, wide)
    sent_kv = finish(1, tkv, rkv, okv, swkv, 2 * wide)

    def columns(j, k):
        return pl.ds(pl.multiple_of(k * width + j * wide, LANES), wide)

    dwq[:, columns(mine_j, 0)] = oq[mine_j].astype(F32)
    for o in range(1, b):
        source = lax.rem(mine_j + b - o, b)
        sent_q[o - 1].wait_recv()
        dwq[:, columns(source, 0)] = swq[o].astype(F32)
    for k in range(2):
        dwkv[:, columns(mine_j, k)] = okv[mine_j][:, k * wide : (k + 1) * wide].astype(F32)
    for o in range(1, b):
        source = lax.rem(mine_j + b - o, b)
        sent_kv[o - 1].wait_recv()
        for k in range(2):
            dwkv[:, columns(source, k)] = swkv[o][:, k * wide : (k + 1) * wide].astype(F32)

    for c in feat + half + ret_copies + z_copies + sent_q + sent_kv:
        c.wait_send()
    for o in range(1, n):
        got(dq_s.at[0], dq_all.at[me], dq_ss.at[o], dq_rs.at[o]).wait_send()
        got(dkv_s.at[0], dkv_all.at[me], dkv_ss.at[o], dkv_rs.at[o]).wait_send()


def rows_apart(grid_feat, node_feat, cotangent, w_query, w_keyval, neighbours, send_rows):
    n = lax.axis_size("mp")
    nd = lax.axis_size("dp")
    samples_dev, grid_dev, width = grid_feat.shape
    nodes = node_feat.shape[1]
    cap = send_rows.shape[2]
    slots = n * cap
    rows = slots + nodes
    a = 2
    b = n // a
    high = width // a
    wide = width // b
    out_rows = width // (n * nd)
    per = LANES * HEADS // width
    wscale = 1.0 / math.sqrt(samples_dev * nd * grid_dev * n)
    vmem = pl.BlockSpec(memory_space=pltpu.VMEM)
    anywhere = pl.BlockSpec(memory_space=pl.ANY)
    dma = pltpu.SemaphoreType.DMA
    d_grid, d_nodes, dw_query, dw_keyval = pl.pallas_call(
        functools.partial(kernel, n, nd, wscale),
        out_shape=(
            jax.ShapeDtypeStruct((grid_dev, width), BF16),
            jax.ShapeDtypeStruct((nodes, width), BF16),
            jax.ShapeDtypeStruct((out_rows, width), F32),
            jax.ShapeDtypeStruct((out_rows, 2 * width), F32),
        ),
        in_specs=[vmem, vmem, vmem, anywhere, anywhere, vmem, vmem, vmem],
        out_specs=(vmem, vmem, vmem, vmem),
        scratch_shapes=[
            pltpu.VMEM((width, width), BF16),
            pltpu.VMEM((width, 2 * width), BF16),
            pltpu.VMEM((slots, width), BF16),
            pltpu.VMEM((rows, width), BF16),
            pltpu.VMEM((grid_dev, width), BF16),
            pltpu.VMEM((rows, 2 * width), BF16),
            pltpu.VMEM((per * grid_dev, rows), F32),
            pltpu.VMEM((n, grid_dev, high), BF16),
            pltpu.VMEM((n, nodes, high), BF16),
            pltpu.VMEM((b, grid_dev, wide), BF16),
            pltpu.VMEM((n, grid_dev, wide), BF16),
            pltpu.VMEM((b, rows, 2 * wide), BF16),
            pltpu.VMEM((b, slots, 2 * wide), BF16),
            pltpu.VMEM((b, nodes, 2 * wide), BF16),
            pltpu.VMEM((n, nodes, 2 * wide), BF16),
            pltpu.VMEM((nd, b, out_rows, wide), BF16),
            pltpu.VMEM((nd, b, out_rows, 2 * wide), BF16),
            pltpu.VMEM((nd, b, out_rows, wide), BF16),
            pltpu.VMEM((nd, b, out_rows, 2 * wide), BF16),
            pltpu.VMEM((b, out_rows, wide), BF16),
            pltpu.VMEM((b, out_rows, 2 * wide), BF16),
            pltpu.VMEM((b, out_rows, wide), BF16),
            pltpu.VMEM((b, out_rows, 2 * wide), BF16),
            dma((2,)),
            dma((n,)), dma((n,)),
            dma((2, n)), dma((2, n)),
            dma((n,)), dma((n,)),
            dma((b, n)), dma((b, n)),
            dma((n,)), dma((n,)),
            dma((2, nd)), dma((2, nd)),
            dma((2, b)), dma((2, b)),
        ],
        compiler_params=pltpu.CompilerParams(
            collective_id=0, has_side_effects=True, vmem_limit_bytes=56 * 1024 * 1024
        ),
        name="graph_attention_grads",
    )(
        grid_feat[0], node_feat[0], cotangent[0], w_query, w_keyval, neighbours,
        send_rows.reshape(slots, 1), send_rows.reshape(1, slots),
    )
    return d_grid[None], d_nodes[None], dw_query, dw_keyval


def heads_kernel(
    n, nd, wscale,
    gf, nf, cot, wq_h, wkv_h, nbr_t, sr,
    dgrid, dnodes, dwq, dwkv,
    wq, wkv, idx_all, nf_all, gf_all, q_s, q_all, cot_all, kv_s, dkv_acc, dq_s, dq_rows,
    dkv_s, dkv_all, ret_kv, dkv_rows, fin_s, fin_q, tkv, fin_kv, *rest,
):
    steps = nd.bit_length() - 1
    halves, rest = rest[: steps], rest[steps:]
    gots, rest = rest[: steps], rest[steps:]
    (
        local_sem, idx_ss, idx_rs, nf_ss, nfy_ss, nf_rs, cot_ss, cot_rs, q_ss, q_rs,
        gfy_ss, gfm_ss, gf_rs, sc_ss, sc_rs, rq_ss, rq_rs, rkv_ss, rkv_rs,
        h_ss, h_rs, fq_ss, fq_rs, fk_ss, fk_rs,
    ) = rest
    grid_dev, width = gf.shape
    nodes = nf.shape[0]
    nbrs = nbr_t.shape[0]
    cap = sr.shape[1]
    slots = n * cap
    rows = slots + nodes
    all_nodes = n * nodes
    hc = width // n
    zc = 2 * hc // nd
    per_half = nd // 2
    out_rows = dwq.shape[0]
    head = width // HEADS
    per = LANES // head
    scale = head ** (-0.5)
    ny = n // 2
    sr_at = idx_all.shape[1] - n
    me = lax.axis_index("mp")
    zd = lax.axis_index("dp")
    core = lax.rem(me, 2)
    chip = lax.div(me, 2)
    mate = me + 1 - 2 * core

    def place_of(m):
        return lax.rem(m, 2) * ny + lax.div(m, 2)

    mine = place_of(me)
    sent = []

    def send(src, dst, ssem, rsem, mp=None, dp=None, when=None):
        device = {}
        if mp is not None:
            device["mp"] = mp
        if dp is not None:
            device["dp"] = dp
        c = pltpu.make_async_remote_copy(
            src_ref=src, dst_ref=dst, send_sem=ssem, recv_sem=rsem,
            device_id=device, device_id_type=MESH,
        )
        if when is None:
            c.start()
        else:
            pl.when(when)(c.start)
        sent.append((c, when))

    def arrived(dst, rsem):
        pltpu.make_async_remote_copy(
            src_ref=dst, dst_ref=dst, send_sem=rsem, recv_sem=rsem,
            device_id={"mp": mate}, device_id_type=MESH,
        ).wait_recv()

    def peer_of(o):
        return lax.rem(me + o, n)

    load_q = pltpu.make_async_copy(wq_h, wq, local_sem.at[0])
    load_kv = pltpu.make_async_copy(wkv_h, wkv, local_sem.at[1])
    load_q.start()
    load_kv.start()
    barrier = pltpu.get_barrier_semaphore()
    for o in range(n):
        for k in range(nd):
            if o or k:
                pl.semaphore_signal(
                    barrier, inc=1,
                    device_id={"mp": peer_of(o), "dp": lax.rem(zd + k, nd)}, device_id_type=MESH,
                )

    lane_slot = lax.broadcasted_iota(jnp.int32, (cap, rows), 1)
    tile = (lax.rem(lane_slot, cap) == lax.broadcasted_iota(jnp.int32, (cap, rows), 0)).astype(BF16)
    spread_rows = dot_nn(sr[...].astype(F32).astype(BF16), tile).astype(jnp.int32) + mine * nodes
    lane_row = lax.broadcasted_iota(jnp.int32, (n, rows), 1)
    own_lane = (lane_row >= me * cap) & (lane_row < me * cap + cap)
    idx_all[me] = jnp.zeros(idx_all.shape[1:], jnp.int32)
    idx_all[me, 0:nbrs, 0:grid_dev] = nbr_t[...]
    idx_all[me, sr_at : sr_at + n, 0:rows] = jnp.where(own_lane, spread_rows, 0)
    nf_all[zd, mine] = nf[...]
    pl.semaphore_wait(barrier, n * nd - 1)

    for o in range(1, n):
        send(idx_all.at[me], idx_all.at[me], idx_ss.at[o], idx_rs.at[me], mp=peer_of(o))

    def right_of(src, ssem, rsem, when):
        send(src, src, ssem, rsem, dp=lax.rem(zd + 1, nd), when=when)

    def left_of(src, ssem, rsem, when):
        send(src, src, ssem, rsem, dp=lax.rem(zd + nd - 1, nd), when=when)

    has_right = zd + 1 < nd
    has_left = zd > 0

    def pass_on(sample, p, to_right, to_left, to_mate=True, when=None):
        block = nf_all.at[sample, p]
        rsem = nf_rs.at[sample, p]
        if to_right is not None:
            right_of(block, nf_ss.at[1, sample, p], rsem, to_right)
        if to_left is not None:
            left_of(block, nf_ss.at[2, sample, p], rsem, to_left)
        if to_mate:
            send(block, block, nf_ss.at[0, sample, p], rsem, mp=mate, when=when)

    for o in range(1, ny):
        there = lax.rem(chip + o, ny) * 2 + core
        send(
            nf_all.at[zd, mine], nf_all.at[zd, mine], nfy_ss.at[o], nf_rs.at[zd, mine], mp=there
        )
    pass_on(zd, mine, has_right, has_left)
    order = [1 + o for o in range(n - 1)]
    for o in order:
        there = peer_of(o)
        cols = pl.ds(pl.multiple_of(there * hc, hc), hc)
        send(cot.at[:, cols], cot_all.at[me], cot_ss.at[o], cot_rs.at[me], mp=there)
    own_cols = pl.ds(pl.multiple_of(me * hc, hc), hc)
    cot_all[me] = cot[:, own_cols]
    gf_all[mine] = gf[...]

    load_q.wait()
    query = dot_nn(gf[...], wq[...]).astype(BF16)
    for k in range(n):
        q_s[k] = query[:, k * hc : (k + 1) * hc]
    for o in order:
        there = peer_of(o)
        send(q_s.at[there], q_all.at[me], q_ss.at[o], q_rs.at[me], mp=there)
    q_all[me] = q_s[me]
    for o in range(1, ny):
        there = lax.rem(chip + o, ny) * 2 + core
        send(gf_all.at[mine], gf_all.at[mine], gfy_ss.at[o], gf_rs.at[mine], mp=there)
    send(gf_all.at[mine], gf_all.at[mine], gfm_ss.at[0], gf_rs.at[mine], mp=mate)

    for o in range(1, ny):
        p = core * ny + lax.rem(chip + ny - o, ny)
        arrived(nf_all.at[zd, p], nf_rs.at[zd, p])
        pass_on(zd, p, has_right, has_left)
    for o in range(ny):
        p = (1 - core) * ny + lax.rem(chip + o, ny)
        arrived(nf_all.at[zd, p], nf_rs.at[zd, p])
    load_kv.wait()
    node_rows = nf_all[zd].reshape(all_nodes, width)
    for k in range(2):
        cols = pl.ds(pl.multiple_of(k * width + me * hc, LANES), hc)
        kv_s[k] = dot_nn(node_rows, wkv[:, cols]).astype(BF16)
    for o in range(1, n):
        there = peer_of(o)
        arrived(idx_all.at[there], idx_rs.at[there])

    def chain(o, y):
        p = core * ny + lax.rem(chip + y, ny)
        from_left = zd >= o
        from_right = zd + o < nd
        left_sample = lax.rem(zd + nd - o, nd)
        right_sample = lax.rem(zd + o, nd)

        @pl.when(from_left)
        def _():
            arrived(nf_all.at[left_sample, p], nf_rs.at[left_sample, p])

        pass_on(left_sample, p, from_left & has_right, None, when=from_left)

        @pl.when(from_right)
        def _():
            arrived(nf_all.at[right_sample, p], nf_rs.at[right_sample, p])

        pass_on(right_sample, p, None, from_right & has_left, when=from_right)

    plan = None
    for m in range(n):
        part = idx_all[m, sr_at : sr_at + n, 0:rows]
        plan = part if plan is None else plan + part
    own_rows = lax.broadcasted_iota(jnp.int32, (1, rows), 1)
    node_iota = lax.broadcasted_iota(jnp.int32, (all_nodes, rows), 0)
    row_iota = lax.broadcasted_iota(jnp.int32, (rows, grid_dev), 0)
    reader = lax.broadcasted_iota(jnp.int32, (n, rows), 0)
    lane = lax.broadcasted_iota(jnp.int32, (1, LANES), 1)
    keep = [(lane // head) == s for s in range(per)]

    def spread(x):
        return jnp.concatenate([jnp.where(m, x, jnp.zeros_like(x)) for m in keep], axis=0)

    dkv_acc[...] = jnp.zeros_like(dkv_acc)

    def shard(d):
        ids = idx_all[d, 0:nbrs, 0:grid_dev]
        count = jnp.zeros((rows, grid_dev), F32)
        for k in range(nbrs):
            count += (ids[k : k + 1, :] == row_iota).astype(F32)
        remote = jnp.sum(jnp.where(reader == d, plan, 0), axis=0, keepdims=True)
        target = jnp.where(own_rows < slots, remote, place_of(d) * nodes + own_rows - slots)
        named = (node_iota == target).astype(BF16)
        times = dot_nn(named, count.astype(BF16))
        times = jnp.concatenate([times] * per, axis=1)

        def pair(j, carry):
            at = pl.ds(pl.multiple_of(j * LANES, LANES), LANES)
            qs = spread(q_all[d, :, at])
            cs = spread(cot_all[d, :, at])
            keys = kv_s[0, :, at]
            values = kv_s[1, :, at]
            scores = dot_nt(keys, qs) * scale
            d_attn = dot_nt(values, cs)
            top = jnp.max(jnp.where(times > 0, scores, -jnp.inf), axis=0, keepdims=True)
            e = jnp.where(times > 0, times * jnp.exp(jnp.minimum(scores - top, 0.0)), 0.0)
            attn = e * (1.0 / jnp.sum(e, axis=0, keepdims=True))
            ds = attn * (d_attn - jnp.sum(attn * d_attn, axis=0, keepdims=True)) * scale
            ds = ds.astype(BF16)
            attn = attn.astype(BF16)
            both = dot_tn(ds, keys)
            dq = both[:grid_dev]
            for s in range(1, per):
                dq = jnp.where(keep[s], both[s * grid_dev : (s + 1) * grid_dev], dq)
            dq_s[d, :, at] = dq.astype(BF16)
            dkv_acc[0, :, at] += dot_nn(ds, qs).astype(BF16).astype(F32)
            dkv_acc[1, :, at] += dot_nn(attn, cs).astype(BF16).astype(F32)
            return carry

        lax.fori_loop(0, hc // LANES, pair, 0)

    def await_shard(d):
        arrived(cot_all.at[d], cot_rs.at[d])
        arrived(q_all.at[d], q_rs.at[d])

    shard(me)
    await_shard(mate)
    shard(mate)
    for y in range(ny):
        chain(1, y)
    for o in range(1, ny):
        for k in range(2):
            d = lax.rem(chip + ny - o, ny) * 2 + lax.rem(core + k, 2)
            await_shard(d)
            shard(d)

    for k in range(nd):
        half, off = k // per_half, (k % per_half) * zc
        dkv_s[k] = dkv_acc[half, :, off : off + zc].astype(BF16).reshape(n, nodes, zc)
    for o in range(1, nd):
        there = lax.rem(zd + o, nd)
        send(dkv_s.at[there], dkv_all.at[zd], sc_ss.at[o], sc_rs.at[zd], dp=there)
    dkv_all[zd] = dkv_s[zd]
    for o in range(1, n):
        there = peer_of(o)
        send(dq_s.at[there], dq_rows.at[:, own_cols], rq_ss.at[o], rq_rs.at[me], mp=there)
        send(dkv_s.at[:, place_of(there)], ret_kv.at[me], rkv_ss.at[o], rkv_rs.at[me], mp=there)
    dq_rows[:, own_cols] = dq_s[me]
    ret_kv[me] = dkv_s[:, mine]

    for o in range(1, ny):
        p = core * ny + lax.rem(chip + ny - o, ny)
        arrived(gf_all.at[p], gf_rs.at[p])
        send(gf_all.at[p], gf_all.at[p], gfm_ss.at[o], gf_rs.at[p], mp=mate)
    for y in range(ny):
        chain(2, y) if nd > 2 else None
    for o in range(ny):
        p = (1 - core) * ny + lax.rem(chip + o, ny)
        arrived(gf_all.at[p], gf_rs.at[p])

    bits = [lax.rem(lax.div(zd, 1 << b), 2) for b in range(steps)]
    mates = [zd + (1 << b) * (1 - 2 * bits[b]) for b in range(steps)]
    targets = [peer_of(o + 1) for o in range(n)]

    def give(b, t):
        send(
            halves[b].at[t, :, 1 - bits[b]], gots[b].at[t], h_ss.at[b, t], h_rs.at[b, t],
            dp=mates[b],
        )

    dq_all = jnp.concatenate([dq_s[lax.rem(p, ny) * 2 + p // ny] for p in range(n)], axis=0)
    for t in targets:
        cols = pl.ds(pl.multiple_of(t * (hc), LANES), hc)
        term = dot_tn(gf_all[:, :, cols].reshape(n * grid_dev, hc), dq_all) * wscale
        halves[0][t] = term.astype(BF16).reshape(per_half, 2, out_rows, hc)
        give(0, t)

    for o in range(1, n):
        there = peer_of(o)
        arrived(dq_rows.at[:, pl.ds(pl.multiple_of(there * hc, hc), hc)], rq_rs.at[there])
    dgrid[...] = dot_nt(dq_rows[...], wq[...]).astype(BF16)

    def column(m, k):
        return (k // per_half) * width + m * hc + (k % per_half) * zc

    for o in range(1, n):
        there = peer_of(o)
        arrived(ret_kv.at[there], rkv_rs.at[there])
    for m in range(n):
        for k in range(nd):
            dkv_rows[:, column(m, k) : column(m, k) + zc] = ret_kv[m, k]
    dnodes[...] = dot_nt(dkv_rows[...], wkv[...]).astype(BF16)

    def halve(b):
        for t in targets:
            arrived(gots[b].at[t], h_rs.at[b, t])
            total = halves[b][t, :, bits[b]].astype(F32) + gots[b][t].astype(F32)
            total = total.astype(BF16)
            if b + 1 < steps:
                halves[b + 1][t] = total.reshape(halves[b + 1].shape[1:])
                give(b + 1, t)
            else:
                fin_s[t] = total.reshape(out_rows, hc)

    for b in range(steps - 1):
        halve(b)
    for o in range(3, nd):
        for y in range(ny):
            chain(o, y)

    for o in range(1, nd):
        there = lax.rem(zd + o, nd)
        arrived(dkv_all.at[there], sc_rs.at[there])
        for y in range(ny):
            p = (1 - core) * ny + lax.rem(chip + y, ny)
            arrived(nf_all.at[there, p], nf_rs.at[there, p])
    dkv_cols = dkv_all[...].reshape(nd * all_nodes, zc)
    for i, t in enumerate(targets):
        cols = pl.ds(pl.multiple_of(t * hc, LANES), hc)
        term = dot_tn(nf_all[:, :, :, cols].reshape(nd * all_nodes, hc), dkv_cols) * wscale
        tkv[t] = term.astype(BF16).reshape(nd, out_rows, zc)
        for k in range(nd):
            if i == n - 1 and k == nd - 1:
                continue
            there = lax.rem(zd + 1 + k, nd)
            send(
                tkv.at[t, there], fin_kv.at[me, zd], fk_ss.at[t, there], fk_rs.at[me, zd],
                mp=t, dp=there,
            )
    fin_kv[me, zd] = tkv[me, zd]

    halve(steps - 1)
    for o in range(1, n):
        there = peer_of(o)
        send(fin_s.at[there], fin_q.at[me], fq_ss.at[o], fq_rs.at[me], mp=there)
    fin_q[me] = fin_s[me]
    for o in range(1, n):
        there = peer_of(o)
        arrived(fin_q.at[there], fq_rs.at[there])
    for m in range(n):
        dwq[:, m * hc : (m + 1) * hc] = fin_q[m].astype(F32)
    for o in range(n):
        for k in range(nd):
            if o or k:
                m, s = peer_of(o), lax.rem(zd + k, nd)
                arrived(fin_kv.at[m, s], fk_rs.at[m, s])
    for m in range(n):
        for k in range(nd):
            dwkv[:, column(m, k) : column(m, k) + zc] = fin_kv[m, k].astype(F32)
    for c, when in sent:
        if when is None:
            c.wait_send()
        else:
            pl.when(when)(c.wait_send)


def copy_kernel(*refs):
    for i in range(len(refs) // 2):
        refs[len(refs) // 2 + i][...] = refs[i][...]


def heads_apart(grid_feat, node_feat, cotangent, w_query, w_keyval, neighbours, send_rows):
    n = lax.axis_size("mp")
    nd = lax.axis_size("dp")
    grid_dev, width = grid_feat.shape[1:]
    nodes = node_feat.shape[1]
    nbrs = neighbours.shape[1]
    cap = send_rows.shape[2]
    rows = n * cap + nodes
    hc = width // n
    zc = 2 * hc // nd
    ny = n // 2
    steps = nd.bit_length() - 1
    out_rows = width // (n * nd)
    wscale = 1.0 / math.sqrt(nd * grid_dev * n)
    idx_rows = -(-nbrs // 8) * 8 + n
    idx_lanes = max(grid_dev, rows)
    vmem = pl.BlockSpec(memory_space=pltpu.VMEM)
    anywhere = pl.BlockSpec(memory_space=pl.ANY)
    dma = pltpu.SemaphoreType.DMA
    outs = (
        jax.ShapeDtypeStruct((grid_dev, width), BF16),
        jax.ShapeDtypeStruct((nodes, width), BF16),
        jax.ShapeDtypeStruct((out_rows, width), F32),
        jax.ShapeDtypeStruct((out_rows, 2 * width), F32),
    )
    held = pl.pallas_call(
        functools.partial(heads_kernel, n, nd, wscale),
        out_shape=outs,
        in_specs=[vmem, vmem, vmem, anywhere, anywhere, vmem, vmem],
        out_specs=(vmem, vmem, vmem, vmem),
        scratch_shapes=[
            pltpu.VMEM((width, width), BF16),
            pltpu.VMEM((width, 2 * width), BF16),
            pltpu.VMEM((n, -(-idx_rows // 8) * 8, idx_lanes), jnp.int32),
            pltpu.VMEM((nd, n, nodes, width), BF16),
            pltpu.VMEM((n, grid_dev, width), BF16),
            pltpu.VMEM((n, grid_dev, hc), BF16),
            pltpu.VMEM((n, grid_dev, hc), BF16),
            pltpu.VMEM((n, grid_dev, hc), BF16),
            pltpu.VMEM((2, n * nodes, hc), BF16),
            pltpu.VMEM((2, n * nodes, hc), F32),
            pltpu.VMEM((n, grid_dev, hc), BF16),
            pltpu.VMEM((grid_dev, width), BF16),
            pltpu.VMEM((nd, n, nodes, zc), BF16),
            pltpu.VMEM((nd, n, nodes, zc), BF16),
            pltpu.VMEM((n, nd, nodes, zc), BF16),
            pltpu.VMEM((nodes, 2 * width), BF16),
            pltpu.VMEM((n, out_rows, hc), BF16),
            pltpu.VMEM((n, out_rows, hc), BF16),
            pltpu.VMEM((n, nd, out_rows, zc), BF16),
            pltpu.VMEM((n, nd, out_rows, zc), BF16),
        ] + [
            pltpu.VMEM((n, nd >> (b + 1), 2, out_rows, hc), BF16) for b in range(steps)
        ] + [
            pltpu.VMEM((n, nd >> (b + 1), out_rows, hc), BF16) for b in range(steps)
        ] + [
            dma((2,)),
            dma((n,)), dma((n,)),
            dma((3, nd, n)), dma((ny,)), dma((nd, n)),
            dma((n,)), dma((n,)),
            dma((n,)), dma((n,)),
            dma((ny,)), dma((ny,)), dma((n,)),
            dma((nd,)), dma((nd,)),
            dma((n,)), dma((n,)),
            dma((n,)), dma((n,)),
            dma((steps, n)), dma((steps, n)),
            dma((n,)), dma((n,)),
            dma((n, nd)), dma((n, nd)),
        ],
        compiler_params=pltpu.CompilerParams(
            collective_id=0, has_side_effects=True, vmem_limit_bytes=56 * 1024 * 1024
        ),
        name="heads_apart_grads",
    )(
        grid_feat[0], node_feat[0], cotangent[0], w_query, w_keyval,
        neighbours.T, send_rows[0],
    )
    d_grid, d_nodes, dw_query, dw_keyval = pl.pallas_call(
        copy_kernel, out_shape=outs, in_specs=[vmem] * 4, out_specs=(vmem,) * 4,
        name="results",
    )(*held)
    return d_grid[None], d_nodes[None], dw_query, dw_keyval


def per_device(*args):
    n = lax.axis_size("mp")
    nd = lax.axis_size("dp")
    samples_dev, grid_dev, width = args[0].shape
    hc = width // n
    apart = (
        samples_dev == 1
        and n % 2 == 0
        and nd >= 2
        and nd & (nd - 1) == 0
        and hc % LANES == 0
        and 2 * hc % (nd * LANES) == 0
        and grid_dev % LANES == 0
        and width % (HEADS * n) == 0
        and LANES % (width // HEADS) == 0
        and width % (n * nd * 16) == 0
        and args[6].shape[2] * n <= 256
        and args[1].shape[1] * n <= 256
    )
    return heads_apart(*args) if apart else rows_apart(*args)


def solution(mesh):
    in_specs = (
        P(("groups", "dp"), "mp", None),
        P(("groups", "dp"), "mp", None),
        P(("groups", "dp"), "mp", None),
        P(),
        P(),
        P("mp", None),
        P("mp", None, None),
    )
    out_specs = (
        P(("groups", "dp"), "mp", None),
        P(("groups", "dp"), "mp", None),
        P(("groups", "mp", "dp"), None),
        P(("groups", "mp", "dp"), None),
    )
    return jax.shard_map(
        per_device, mesh=mesh, in_specs=in_specs, out_specs=out_specs, check_vma=False
    )
```

```python
import functools
import math

import jax
import jax.numpy as jnp
from jax import lax
from jax.experimental import pallas as pl
from jax.experimental.pallas import tpu as pltpu
from jax.sharding import PartitionSpec as P

HEADS = 16
LANES = 128
MESH = pl.DeviceIdType.MESH
F32 = jnp.float32
BF16 = jnp.bfloat16


def dot_nn(x, y):
    return lax.dot_general(x, y, (((1,), (0,)), ((), ())), preferred_element_type=F32)


def dot_nt(x, y):
    return lax.dot_general(x, y, (((1,), (1,)), ((), ())), preferred_element_type=F32)


def dot_tn(x, y):
    return lax.dot_general(x, y, (((0,), (0,)), ((), ())), preferred_element_type=F32)


def kernel(
    n, nd, wscale,
    gf, nf, cot, wq_h, wkv_h, nbr, sr_col, sr_row,
    dgrid, dnodes, dwq, dwkv,
    wq, wkv, out_feat, tab, q_s, kv_s, count_s, gf_all, nf_all, dq_s, dq_all,
    part_s, ret_s, dkv_s, dkv_all, tq, tkv, rq, rkv, oq, okv, swq, swkv,
    local_sem, feat_ss, feat_rs, half_ss, half_rs, dq_ss, dq_rs, ret_ss, ret_rs,
    dkv_ss, dkv_rs, z_ss, z_rs, sw_ss, sw_rs,
):
    grid_dev, width = gf.shape
    nodes = nf.shape[0]
    slots = sr_col.shape[0]
    rows = slots + nodes
    cap = slots // n
    nbrs = nbr.shape[1]
    a = width // gf_all.shape[2]
    b = n // a
    high = width // a
    wide = width // b
    out_rows = dwq.shape[0]
    head = width // HEADS
    per = LANES // head
    scale = head ** (-0.5)
    me = lax.axis_index("mp")
    zd = lax.axis_index("dp")
    mine_i = me // b
    mine_j = lax.rem(me, b)

    def to_mp(src, dst, ssem, rsem, peer):
        return pltpu.make_async_remote_copy(
            src_ref=src, dst_ref=dst, send_sem=ssem, recv_sem=rsem,
            device_id={"mp": peer}, device_id_type=MESH,
        )

    def to_dp(src, dst, ssem, rsem, peer):
        return pltpu.make_async_remote_copy(
            src_ref=src, dst_ref=dst, send_sem=ssem, recv_sem=rsem,
            device_id={"dp": peer}, device_id_type=MESH,
        )

    def peer_of(o):
        return lax.rem(me + o, n)

    load_q = pltpu.make_async_copy(wq_h, wq, local_sem.at[0])
    load_kv = pltpu.make_async_copy(wkv_h, wkv, local_sem.at[1])
    load_q.start()
    load_kv.start()
    barrier = pltpu.get_barrier_semaphore()
    for o in range(1, n):
        pl.semaphore_signal(barrier, inc=1, device_id={"mp": peer_of(o)}, device_id_type=MESH)
    for o in range(1, nd):
        pl.semaphore_signal(
            barrier, inc=1, device_id={"dp": lax.rem(zd + o, nd)}, device_id_type=MESH
        )
    pick = (sr_col[...] == lax.broadcasted_iota(jnp.int32, (slots, nodes), 1)).astype(BF16)
    out_feat[...] = dot_nn(pick, nf[...]).astype(BF16)
    tab[pl.ds(slots, nodes), :] = nf[...]
    own_slots = pl.ds(pl.multiple_of(me * cap, cap), cap)
    tab[own_slots, :] = jnp.zeros((cap, width), BF16)
    for jb in range(b):
        ret_s[jb, own_slots, :] = jnp.zeros((cap, 2 * wide), BF16)
    pl.semaphore_wait(barrier, n - 1 + nd - 1)

    feat = []
    for o in range(1, n):
        there = pl.ds(pl.multiple_of(peer_of(o) * cap, cap), cap)
        feat.append(
            to_mp(out_feat.at[there], tab.at[own_slots], feat_ss.at[o], feat_rs.at[o], peer_of(o))
        )
        feat[-1].start()

    ids = nbr[...]
    row_id = lax.broadcasted_iota(jnp.int32, (grid_dev, rows), 1)
    count = jnp.zeros((grid_dev, rows), F32)
    for k in range(nbrs):
        count += (ids[:, k : k + 1] == row_id).astype(F32)
    for s in range(per):
        count_s[s * grid_dev : (s + 1) * grid_dev, :] = count
    half_cols = pl.ds(pl.multiple_of(mine_i * high, high), high)
    gf_all[me] = gf[:, half_cols]
    nf_all[me] = nf[:, half_cols]
    load_q.wait()
    q_s[...] = dot_nn(gf[...], wq[...]).astype(BF16)
    for c in feat:
        c.wait_recv()
    half = []
    for o in range(1, n):
        there = pl.ds(pl.multiple_of((peer_of(o) // b) * high, high), high)
        half.append(
            to_mp(nf.at[:, there], nf_all.at[me], half_ss.at[0, o], half_rs.at[0, o], peer_of(o))
        )
        half.append(
            to_mp(gf.at[:, there], gf_all.at[me], half_ss.at[1, o], half_rs.at[1, o], peer_of(o))
        )
    for c in half:
        c.start()
    load_kv.wait()
    kv_s[...] = dot_nn(tab[...], wkv[...]).astype(BF16)

    lane = lax.broadcasted_iota(jnp.int32, (1, LANES), 1)
    keep = [(lane // head) == s for s in range(per)]

    def spread(x):
        return jnp.concatenate([jnp.where(m, x, jnp.zeros_like(x)) for m in keep], axis=0)

    dq_copies = []
    ret_copies = []
    for jb in range(b):

        def one(blk, carry):
            off = pl.multiple_of(jb * wide + blk * LANES, LANES)
            at = pl.ds(off, LANES)
            at_v = pl.ds(pl.multiple_of(width + off, LANES), LANES)
            here = pl.ds(pl.multiple_of(blk * LANES, LANES), LANES)
            here_v = pl.ds(pl.multiple_of(wide + blk * LANES, LANES), LANES)
            qs = spread(q_s[:, at])
            cs = spread(cot[:, at])
            keys = kv_s[:, at]
            values = kv_s[:, at_v]
            times = count_s[...]
            scores = dot_nt(qs, keys) * scale
            d_attn = dot_nt(cs, values)
            top = jnp.max(
                jnp.where(times > 0, scores, -jnp.inf), axis=1, keepdims=True
            )
            e = jnp.where(times > 0, times * jnp.exp(jnp.minimum(scores - top, 0.0)), 0.0)
            attn = e / jnp.sum(e, axis=1, keepdims=True)
            ds = attn * (d_attn - jnp.sum(attn * d_attn, axis=1, keepdims=True)) * scale
            ds = ds.astype(BF16)
            attn = attn.astype(BF16)
            dq = None
            for s in range(per):
                term = dot_nn(
                    ds[s * grid_dev : (s + 1) * grid_dev],
                    jnp.where(keep[s], keys, jnp.zeros_like(keys)),
                )
                dq = term if dq is None else dq + term
            dq_s[jb, :, here] = dq.astype(BF16)
            part_s[jb, :, here] = dot_tn(ds, qs).astype(BF16)
            part_s[jb, :, here_v] = dot_tn(attn, cs).astype(BF16)
            return carry

        lax.fori_loop(0, wide // LANES, one, 0)
        for o in range(1, n):
            peer = peer_of(o)
            c = to_mp(dq_s.at[jb], dq_all.at[me], dq_ss.at[o], dq_rs.at[o], peer)

            @pl.when(lax.rem(peer, b) == jb)
            def _():
                c.start()

        for o in range(1, n):
            there = pl.ds(pl.multiple_of(peer_of(o) * cap, cap), cap)
            c = to_mp(
                part_s.at[jb, there], ret_s.at[jb, own_slots],
                ret_ss.at[jb, o], ret_rs.at[jb, o], peer_of(o),
            )
            c.start()
            ret_copies.append(c)

    dq_all[me] = dq_s[mine_j]
    acc = None
    for jb in range(b):
        term = dot_nt(dq_s[jb], wq[:, jb * wide : (jb + 1) * wide])
        acc = term if acc is None else acc + term
    dgrid[...] = acc.astype(BF16)

    place = (sr_row[...] == lax.broadcasted_iota(jnp.int32, (nodes, slots), 0)).astype(BF16)
    for jb in range(b):
        for o in range(1, n):
            ret_copies[jb * (n - 1) + o - 1].wait_recv()
        dkv = part_s[jb, slots:, :].astype(F32) + dot_nn(place, ret_s[jb])
        dkv_s[jb] = dkv.astype(BF16)
        for o in range(1, n):
            peer = peer_of(o)
            c = to_mp(dkv_s.at[jb], dkv_all.at[me], dkv_ss.at[o], dkv_rs.at[o], peer)

            @pl.when(lax.rem(peer, b) == jb)
            def _():
                c.start()

    dkv_all[me] = dkv_s[mine_j]

    def got(src, dst, ssem, rsem):
        return to_mp(src, dst, ssem, rsem, peer_of(1))

    for c in half:
        c.wait_recv()
    for o in range(1, n):
        got(dq_s.at[0], dq_all.at[me], dq_ss.at[o], dq_rs.at[o]).wait_recv()
    term_q = dot_tn(
        gf_all[...].reshape(n * grid_dev, high), dq_all[...].reshape(n * grid_dev, wide)
    ) * wscale
    term_q = term_q.astype(BF16).reshape(b, nd, out_rows, wide)
    for d in range(nd):
        tq[d] = term_q[:, d]
    z_copies = []
    for o in range(1, nd):
        peer = lax.rem(zd + o, nd)
        z_copies.append(to_dp(tq.at[peer], rq.at[o], z_ss.at[0, o], z_rs.at[0, o], peer))
        z_copies[-1].start()

    acc = None
    for jb in range(b):
        for k in range(2):
            term = dot_nt(
                dkv_s[jb, :, k * wide : (k + 1) * wide],
                wkv[:, k * width + jb * wide : k * width + (jb + 1) * wide],
            )
            acc = term if acc is None else acc + term
    dnodes[...] = acc.astype(BF16)

    for o in range(1, n):
        got(dkv_s.at[0], dkv_all.at[me], dkv_ss.at[o], dkv_rs.at[o]).wait_recv()
    term_kv = dot_tn(
        nf_all[...].reshape(n * nodes, high), dkv_all[...].reshape(n * nodes, 2 * wide)
    ) * wscale
    term_kv = term_kv.astype(BF16).reshape(b, nd, out_rows, 2 * wide)
    for d in range(nd):
        tkv[d] = term_kv[:, d]
    for o in range(1, nd):
        peer = lax.rem(zd + o, nd)
        z_copies.append(to_dp(tkv.at[peer], rkv.at[o], z_ss.at[1, o], z_rs.at[1, o], peer))
        z_copies[-1].start()

    def finish(which, t, r, out, sw, width_out):
        total = t[zd].astype(F32)
        for o in range(1, nd):
            z_copies[which * (nd - 1) + o - 1].wait_recv()
            total += r[o].astype(F32)
        out[...] = total.astype(BF16)
        sent = []
        for o in range(1, b):
            mate = lax.rem(mine_j + o, b)
            c = to_mp(
                out.at[mate], sw.at[o], sw_ss.at[which, o], sw_rs.at[which, o],
                mine_i * b + mate,
            )
            c.start()
            sent.append(c)
        return sent

    sent_q = finish(0, tq, rq, oq, swq, wide)
    sent_kv = finish(1, tkv, rkv, okv, swkv, 2 * wide)

    def columns(j, k):
        return pl.ds(pl.multiple_of(k * width + j * wide, LANES), wide)

    dwq[:, columns(mine_j, 0)] = oq[mine_j].astype(F32)
    for o in range(1, b):
        source = lax.rem(mine_j + b - o, b)
        sent_q[o - 1].wait_recv()
        dwq[:, columns(source, 0)] = swq[o].astype(F32)
    for k in range(2):
        dwkv[:, columns(mine_j, k)] = okv[mine_j][:, k * wide : (k + 1) * wide].astype(F32)
    for o in range(1, b):
        source = lax.rem(mine_j + b - o, b)
        sent_kv[o - 1].wait_recv()
        for k in range(2):
            dwkv[:, columns(source, k)] = swkv[o][:, k * wide : (k + 1) * wide].astype(F32)

    for c in feat + half + ret_copies + z_copies + sent_q + sent_kv:
        c.wait_send()
    for o in range(1, n):
        got(dq_s.at[0], dq_all.at[me], dq_ss.at[o], dq_rs.at[o]).wait_send()
        got(dkv_s.at[0], dkv_all.at[me], dkv_ss.at[o], dkv_rs.at[o]).wait_send()


def rows_apart(grid_feat, node_feat, cotangent, w_query, w_keyval, neighbours, send_rows):
    n = lax.axis_size("mp")
    nd = lax.axis_size("dp")
    samples_dev, grid_dev, width = grid_feat.shape
    nodes = node_feat.shape[1]
    cap = send_rows.shape[2]
    slots = n * cap
    rows = slots + nodes
    a = 2
    b = n // a
    high = width // a
    wide = width // b
    out_rows = width // (n * nd)
    per = LANES * HEADS // width
    wscale = 1.0 / math.sqrt(samples_dev * nd * grid_dev * n)
    vmem = pl.BlockSpec(memory_space=pltpu.VMEM)
    anywhere = pl.BlockSpec(memory_space=pl.ANY)
    dma = pltpu.SemaphoreType.DMA
    d_grid, d_nodes, dw_query, dw_keyval = pl.pallas_call(
        functools.partial(kernel, n, nd, wscale),
        out_shape=(
            jax.ShapeDtypeStruct((grid_dev, width), BF16),
            jax.ShapeDtypeStruct((nodes, width), BF16),
            jax.ShapeDtypeStruct((out_rows, width), F32),
            jax.ShapeDtypeStruct((out_rows, 2 * width), F32),
        ),
        in_specs=[vmem, vmem, vmem, anywhere, anywhere, vmem, vmem, vmem],
        out_specs=(vmem, vmem, vmem, vmem),
        scratch_shapes=[
            pltpu.VMEM((width, width), BF16),
            pltpu.VMEM((width, 2 * width), BF16),
            pltpu.VMEM((slots, width), BF16),
            pltpu.VMEM((rows, width), BF16),
            pltpu.VMEM((grid_dev, width), BF16),
            pltpu.VMEM((rows, 2 * width), BF16),
            pltpu.VMEM((per * grid_dev, rows), F32),
            pltpu.VMEM((n, grid_dev, high), BF16),
            pltpu.VMEM((n, nodes, high), BF16),
            pltpu.VMEM((b, grid_dev, wide), BF16),
            pltpu.VMEM((n, grid_dev, wide), BF16),
            pltpu.VMEM((b, rows, 2 * wide), BF16),
            pltpu.VMEM((b, slots, 2 * wide), BF16),
            pltpu.VMEM((b, nodes, 2 * wide), BF16),
            pltpu.VMEM((n, nodes, 2 * wide), BF16),
            pltpu.VMEM((nd, b, out_rows, wide), BF16),
            pltpu.VMEM((nd, b, out_rows, 2 * wide), BF16),
            pltpu.VMEM((nd, b, out_rows, wide), BF16),
            pltpu.VMEM((nd, b, out_rows, 2 * wide), BF16),
            pltpu.VMEM((b, out_rows, wide), BF16),
            pltpu.VMEM((b, out_rows, 2 * wide), BF16),
            pltpu.VMEM((b, out_rows, wide), BF16),
            pltpu.VMEM((b, out_rows, 2 * wide), BF16),
            dma((2,)),
            dma((n,)), dma((n,)),
            dma((2, n)), dma((2, n)),
            dma((n,)), dma((n,)),
            dma((b, n)), dma((b, n)),
            dma((n,)), dma((n,)),
            dma((2, nd)), dma((2, nd)),
            dma((2, b)), dma((2, b)),
        ],
        compiler_params=pltpu.CompilerParams(
            collective_id=0, has_side_effects=True, vmem_limit_bytes=56 * 1024 * 1024
        ),
        name="graph_attention_grads",
    )(
        grid_feat[0], node_feat[0], cotangent[0], w_query, w_keyval, neighbours,
        send_rows.reshape(slots, 1), send_rows.reshape(1, slots),
    )
    return d_grid[None], d_nodes[None], dw_query, dw_keyval


def heads_kernel(
    n, nd, wscale,
    gf, nf, cot, wq_h, wkv_h, nbr_t, sr,
    dgrid, dnodes, dwq, dwkv,
    wq, wkv, idx_all, nf_all, nf_part, gf_all, q_s, q_all, cot_all, kv_s, dkv_acc, dq_s, dq_rows,
    dkv_s, dkv_all, ret_kv, dkv_rows, fin_s, fin_q, tkv, fin_kv, *rest,
):
    steps = nd.bit_length() - 1
    halves, rest = rest[: steps], rest[steps:]
    gots, rest = rest[: steps], rest[steps:]
    (
        local_sem, idx_ss, idx_rs, nfy_ss, nfm_ss, nf_rs, part_ss, part_rs, cot_ss, cot_rs, q_ss, q_rs,
        gfy_ss, gfm_ss, gf_rs, sc_ss, scy_ss, sc_rs, rq_ss, rq_rs, rkv_ss, rkv_rs,
        h_ss, h_rs, fq_ss, fq_rs, fk_ss, fk_rs,
    ) = rest
    grid_dev, width = gf.shape
    nodes = nf.shape[0]
    nbrs = nbr_t.shape[0]
    cap = sr.shape[1]
    slots = n * cap
    rows = slots + nodes
    all_nodes = n * nodes
    hc = width // n
    zc = 2 * hc // nd
    per_half = nd // 2
    out_rows = dwq.shape[0]
    head = width // HEADS
    per = LANES // head
    scale = head ** (-0.5)
    ny = n // 2
    wy = width // ny
    sr_at = idx_all.shape[1] - n
    me = lax.axis_index("mp")
    zd = lax.axis_index("dp")
    core = lax.rem(me, 2)
    chip = lax.div(me, 2)
    mate = me + 1 - 2 * core

    def place_of(m):
        return lax.rem(m, 2) * ny + lax.div(m, 2)

    mine = place_of(me)
    sent = []

    def send(src, dst, ssem, rsem, mp=None, dp=None, when=None):
        device = {}
        if mp is not None:
            device["mp"] = mp
        if dp is not None:
            device["dp"] = dp
        c = pltpu.make_async_remote_copy(
            src_ref=src, dst_ref=dst, send_sem=ssem, recv_sem=rsem,
            device_id=device, device_id_type=MESH,
        )
        if when is None:
            c.start()
        else:
            pl.when(when)(c.start)
        sent.append((c, when))

    def arrived(dst, rsem):
        pltpu.make_async_remote_copy(
            src_ref=dst, dst_ref=dst, send_sem=rsem, recv_sem=rsem,
            device_id={"mp": mate}, device_id_type=MESH,
        ).wait_recv()

    def peer_of(o):
        return lax.rem(me + o, n)

    load_q = pltpu.make_async_copy(wq_h, wq, local_sem.at[0])
    load_kv = pltpu.make_async_copy(wkv_h, wkv, local_sem.at[1])
    load_q.start()
    load_kv.start()
    barrier = pltpu.get_barrier_semaphore()
    for o in range(n):
        for k in range(nd):
            if o or k:
                pl.semaphore_signal(
                    barrier, inc=1,
                    device_id={"mp": peer_of(o), "dp": lax.rem(zd + k, nd)}, device_id_type=MESH,
                )

    lane_slot = lax.broadcasted_iota(jnp.int32, (cap, rows), 1)
    tile = (lax.rem(lane_slot, cap) == lax.broadcasted_iota(jnp.int32, (cap, rows), 0)).astype(BF16)
    spread_rows = dot_nn(sr[...].astype(F32).astype(BF16), tile).astype(jnp.int32) + mine * nodes
    lane_row = lax.broadcasted_iota(jnp.int32, (n, rows), 1)
    own_lane = (lane_row >= me * cap) & (lane_row < me * cap + cap)
    idx_all[me] = jnp.zeros(idx_all.shape[1:], jnp.int32)
    idx_all[me, 0:nbrs, 0:grid_dev] = nbr_t[...]
    idx_all[me, sr_at : sr_at + n, 0:rows] = jnp.where(own_lane, spread_rows, 0)
    half_cols = pl.ds(pl.multiple_of(chip * wy, LANES), wy)
    nf_all[mine] = nf[...]
    nf_part[zd, mine] = nf[:, half_cols]
    pl.semaphore_wait(barrier, n * nd - 1)

    for o in range(1, n):
        send(idx_all.at[me], idx_all.at[me], idx_ss.at[o], idx_rs.at[me], mp=peer_of(o))

    def right_of(src, ssem, rsem, when):
        send(src, src, ssem, rsem, dp=lax.rem(zd + 1, nd), when=when)

    def left_of(src, ssem, rsem, when):
        send(src, src, ssem, rsem, dp=lax.rem(zd + nd - 1, nd), when=when)

    has_right = zd + 1 < nd
    has_left = zd > 0

    def pass_on(sample, p, to_right, to_left, when):
        block = nf_part.at[sample, p]
        rsem = part_rs.at[sample, p]
        if to_right is not None:
            right_of(block, part_ss.at[1, sample, p], rsem, to_right)
        if to_left is not None:
            left_of(block, part_ss.at[2, sample, p], rsem, to_left)
        if when is not None:
            send(block, block, part_ss.at[0, sample, p], rsem, mp=mate, when=when)

    for o in range(1, ny):
        there = lax.rem(chip + o, ny) * 2 + core
        send(nf_all.at[mine], nf_all.at[mine], nfy_ss.at[o], nf_rs.at[mine], mp=there)
    send(nf_all.at[mine], nf_all.at[mine], nfm_ss.at[0], nf_rs.at[mine], mp=mate)
    pass_on(zd, mine, has_right, has_left, None)
    order = [1 + o for o in range(n - 1)]
    for o in order:
        there = peer_of(o)
        cols = pl.ds(pl.multiple_of(there * hc, hc), hc)
        send(cot.at[:, cols], cot_all.at[me], cot_ss.at[o], cot_rs.at[me], mp=there)
    own_cols = pl.ds(pl.multiple_of(me * hc, hc), hc)
    cot_all[me] = cot[:, own_cols]
    gf_all[mine] = gf[...]

    load_q.wait()
    query = dot_nn(gf[...], wq[...]).astype(BF16)
    for k in range(n):
        q_s[k] = query[:, k * hc : (k + 1) * hc]
    for o in order:
        there = peer_of(o)
        send(q_s.at[there], q_all.at[me], q_ss.at[o], q_rs.at[me], mp=there)
    q_all[me] = q_s[me]
    for o in range(1, ny):
        there = lax.rem(chip + o, ny) * 2 + core
        send(gf_all.at[mine], gf_all.at[mine], gfy_ss.at[o], gf_rs.at[mine], mp=there)
    send(gf_all.at[mine], gf_all.at[mine], gfm_ss.at[0], gf_rs.at[mine], mp=mate)

    for o in range(1, ny):
        p = core * ny + lax.rem(chip + ny - o, ny)
        arrived(nf_all.at[p], nf_rs.at[p])
        send(nf_all.at[p], nf_all.at[p], nfm_ss.at[o], nf_rs.at[p], mp=mate)
        nf_part[zd, p] = nf_all[p, :, half_cols]
        pass_on(zd, p, has_right, has_left, None)
    for o in range(ny):
        p = (1 - core) * ny + lax.rem(chip + o, ny)
        arrived(nf_all.at[p], nf_rs.at[p])
        nf_part[zd, p] = nf_all[p, :, half_cols]
    load_kv.wait()
    node_rows = nf_all[...].reshape(all_nodes, width)
    for k in range(2):
        cols = pl.ds(pl.multiple_of(k * width + me * hc, LANES), hc)
        kv_s[k] = dot_nn(node_rows, wkv[:, cols]).astype(BF16)
    for o in range(1, n):
        there = peer_of(o)
        arrived(idx_all.at[there], idx_rs.at[there])

    def chain(o, y):
        p = core * ny + lax.rem(chip + y, ny)
        from_left = zd >= o
        from_right = zd + o < nd
        left_sample = lax.rem(zd + nd - o, nd)
        right_sample = lax.rem(zd + o, nd)

        @pl.when(from_left)
        def _():
            arrived(nf_part.at[left_sample, p], part_rs.at[left_sample, p])

        pass_on(left_sample, p, from_left & has_right, None, from_left)

        @pl.when(from_right)
        def _():
            arrived(nf_part.at[right_sample, p], part_rs.at[right_sample, p])

        pass_on(right_sample, p, None, from_right & has_left, from_right)

    plan = None
    for m in range(n):
        part = idx_all[m, sr_at : sr_at + n, 0:rows]
        plan = part if plan is None else plan + part
    own_rows = lax.broadcasted_iota(jnp.int32, (1, rows), 1)
    node_iota = lax.broadcasted_iota(jnp.int32, (all_nodes, rows), 0)
    row_iota = lax.broadcasted_iota(jnp.int32, (rows, grid_dev), 0)
    reader = lax.broadcasted_iota(jnp.int32, (n, rows), 0)
    lane = lax.broadcasted_iota(jnp.int32, (1, LANES), 1)
    keep = [(lane // head) == s for s in range(per)]

    def spread(x):
        return jnp.concatenate([jnp.where(m, x, jnp.zeros_like(x)) for m in keep], axis=0)

    dkv_acc[...] = jnp.zeros_like(dkv_acc)

    def shard(d):
        ids = idx_all[d, 0:nbrs, 0:grid_dev]
        count = jnp.zeros((rows, grid_dev), F32)
        for k in range(nbrs):
            count += (ids[k : k + 1, :] == row_iota).astype(F32)
        remote = jnp.sum(jnp.where(reader == d, plan, 0), axis=0, keepdims=True)
        target = jnp.where(own_rows < slots, remote, place_of(d) * nodes + own_rows - slots)
        named = (node_iota == target).astype(BF16)
        times = dot_nn(named, count.astype(BF16))
        times = jnp.concatenate([times] * per, axis=1)

        def pair(j, carry):
            at = pl.ds(pl.multiple_of(j * LANES, LANES), LANES)
            qs = spread(q_all[d, :, at])
            cs = spread(cot_all[d, :, at])
            keys = kv_s[0, :, at]
            values = kv_s[1, :, at]
            scores = dot_nt(keys, qs) * scale
            d_attn = dot_nt(values, cs)
            top = jnp.max(jnp.where(times > 0, scores, -jnp.inf), axis=0, keepdims=True)
            e = jnp.where(times > 0, times * jnp.exp(jnp.minimum(scores - top, 0.0)), 0.0)
            attn = e * (1.0 / jnp.sum(e, axis=0, keepdims=True))
            ds = attn * (d_attn - jnp.sum(attn * d_attn, axis=0, keepdims=True)) * scale
            ds = ds.astype(BF16)
            attn = attn.astype(BF16)
            both = dot_tn(ds, keys)
            dq = both[:grid_dev]
            for s in range(1, per):
                dq = jnp.where(keep[s], both[s * grid_dev : (s + 1) * grid_dev], dq)
            dq_s[d, :, at] = dq.astype(BF16)
            dkv_acc[0, :, at] += dot_nn(ds, qs).astype(BF16).astype(F32)
            dkv_acc[1, :, at] += dot_nn(attn, cs).astype(BF16).astype(F32)
            return carry

        lax.fori_loop(0, hc // LANES, pair, 0)

    def await_shard(d):
        arrived(cot_all.at[d], cot_rs.at[d])
        arrived(q_all.at[d], q_rs.at[d])

    links = [(o, y) for o in range(1, nd) for y in range(ny)]

    def poll():
        if links:
            chain(*links.pop(0))

    poll()
    shard(me)
    await_shard(mate)
    shard(mate)
    poll()
    for o in range(1, ny):
        for k in range(2):
            d = lax.rem(chip + ny - o, ny) * 2 + lax.rem(core + k, 2)
            await_shard(d)
            shard(d)
            if k == 0:
                poll()

    for k in range(nd):
        half, off = k // per_half, (k % per_half) * zc
        dkv_s[k] = dkv_acc[half, :, off : off + zc].astype(BF16)
    for o in range(1, nd):
        there = lax.rem(zd + o, nd)
        send(dkv_s.at[there], dkv_all.at[zd, chip], sc_ss.at[o], sc_rs.at[zd, chip], dp=there)
    dkv_all[zd, chip] = dkv_s[zd]

    def across(sample, when):
        block = dkv_all.at[sample, chip]
        for o in range(1, ny):
            there = lax.rem(chip + o, ny) * 2 + core
            send(block, block, scy_ss.at[sample, o], sc_rs.at[sample, chip], mp=there, when=when)

    def gather_across(o):
        for sample, here in ((lax.rem(zd + nd - o, nd), zd >= o), (lax.rem(zd + o, nd), zd + o < nd)):

            @pl.when(here)
            def _():
                arrived(dkv_all.at[sample, chip], sc_rs.at[sample, chip])

            across(sample, here)

    across(zd, None)
    for o in range(1, n):
        there = peer_of(o)
        send(dq_s.at[there], dq_rows.at[:, own_cols], rq_ss.at[o], rq_rs.at[me], mp=there)
    dq_rows[:, own_cols] = dq_s[me]
    ret_kv[me] = dkv_s[:, pl.ds(pl.multiple_of(mine * nodes, nodes), nodes)]

    poll()
    for o in range(1, ny):
        p = core * ny + lax.rem(chip + ny - o, ny)
        arrived(gf_all.at[p], gf_rs.at[p])
        send(gf_all.at[p], gf_all.at[p], gfm_ss.at[o], gf_rs.at[p], mp=mate)
    poll()
    for o in range(ny):
        p = (1 - core) * ny + lax.rem(chip + o, ny)
        arrived(gf_all.at[p], gf_rs.at[p])

    bits = [lax.rem(lax.div(zd, 1 << b), 2) for b in range(steps)]
    mates = [zd + (1 << b) * (1 - 2 * bits[b]) for b in range(steps)]
    targets = [peer_of(o + 1) for o in range(n)]

    def give(b, t):
        send(
            halves[b].at[t, :, 1 - bits[b]], gots[b].at[t], h_ss.at[b, t], h_rs.at[b, t],
            dp=mates[b],
        )

    dq_all = jnp.concatenate([dq_s[lax.rem(p, ny) * 2 + p // ny] for p in range(n)], axis=0)
    for t in targets:
        cols = pl.ds(pl.multiple_of(t * (hc), LANES), hc)
        term = dot_tn(gf_all[:, :, cols].reshape(n * grid_dev, hc), dq_all) * wscale
        halves[0][t] = term.astype(BF16).reshape(per_half, 2, out_rows, hc)
        give(0, t)

    for o in range(1, n):
        there = peer_of(o)
        arrived(dq_rows.at[:, pl.ds(pl.multiple_of(there * hc, hc), hc)], rq_rs.at[there])
    dgrid[...] = dot_nt(dq_rows[...], wq[...]).astype(BF16)

    def column(m, k):
        return (k // per_half) * width + m * hc + (k % per_half) * zc

    def halve(b, i):
        t = targets[i]
        arrived(gots[b].at[t], h_rs.at[b, t])
        total = halves[b][t, :, bits[b]].astype(F32) + gots[b][t].astype(F32)
        total = total.astype(BF16)
        if b + 1 < steps:
            halves[b + 1][t] = total.reshape(halves[b + 1].shape[1:])
            give(b + 1, t)
        elif i < n - 1:
            fin_s[t] = total.reshape(out_rows, hc)
            send(fin_s.at[t], fin_q.at[me], fq_ss.at[i], fq_rs.at[me], mp=t)
        else:
            fin_q[me] = total.reshape(out_rows, hc)

    while links:
        poll()
    for o in range(1, nd):
        gather_across(o)
    for o in range(1, n):
        there = peer_of(o)
        node_block = pl.ds(pl.multiple_of(place_of(there) * nodes, nodes), nodes)
        send(dkv_s.at[:, node_block], ret_kv.at[me], rkv_ss.at[o], rkv_rs.at[me], mp=there)

    def keyval_block(i, dkv_cols):
        k = lax.rem(core + 1 + i, 2)
        cols = pl.ds(pl.multiple_of(k * hc, LANES), hc)
        term = dot_tn(nf_part[:, :, :, cols].reshape(nd * all_nodes, hc), dkv_cols) * wscale
        tkv[k] = term.astype(BF16).reshape(nd, out_rows, ny * zc)
        for o in range(nd):
            if i == 1 and o == nd - 1:
                continue
            there = lax.rem(zd + 1 + o, nd)
            send(
                tkv.at[k, there], fin_kv.at[core, zd], fk_ss.at[k, there], fk_rs.at[core, zd],
                mp=chip * 2 + k, dp=there,
            )

    for i in range(n - 1):
        halve(0, i)
    for s in range(nd):
        for o in range(1, ny):
            there = lax.rem(chip + o, ny)
            arrived(dkv_all.at[s, there], sc_rs.at[s, there])
    for o in range(1, nd):
        there = lax.rem(zd + o, nd)
        for y in range(ny):
            p = (1 - core) * ny + y
            arrived(nf_part.at[there, p], part_rs.at[there, p])
    dkv_cols = jnp.concatenate(
        [dkv_all[:, y].reshape(nd * all_nodes, zc) for y in range(ny)], axis=1
    )
    keyval_block(0, dkv_cols)
    halve(0, n - 1)
    keyval_block(1, dkv_cols)
    fin_kv[core, zd] = tkv[core, zd]
    for b in range(1, steps):
        for i in range(n):
            halve(b, i)

    for o in range(1, n):
        there = peer_of(o)
        arrived(ret_kv.at[there], rkv_rs.at[there])
    for m in range(n):
        for k in range(nd):
            dkv_rows[:, column(m, k) : column(m, k) + zc] = ret_kv[m, k]
    dnodes[...] = dot_nt(dkv_rows[...], wkv[...]).astype(BF16)

    for o in range(1, n):
        there = peer_of(o)
        arrived(fin_q.at[there], fq_rs.at[there])
    for m in range(n):
        dwq[:, m * hc : (m + 1) * hc] = fin_q[m].astype(F32)
    for o in range(2):
        for k in range(nd):
            if o or k:
                c, s = lax.rem(core + o, 2), lax.rem(zd + k, nd)
                arrived(fin_kv.at[c, s], fk_rs.at[c, s])
    for c in range(2):
        for k in range(nd):
            for y in range(ny):
                at = column(y * 2 + c, k)
                dwkv[:, at : at + zc] = fin_kv[c, k, :, y * zc : (y + 1) * zc].astype(F32)
    for c, when in sent:
        if when is None:
            c.wait_send()
        else:
            pl.when(when)(c.wait_send)


def copy_kernel(*refs):
    for i in range(len(refs) // 2):
        refs[len(refs) // 2 + i][...] = refs[i][...]


def heads_apart(grid_feat, node_feat, cotangent, w_query, w_keyval, neighbours, send_rows):
    n = lax.axis_size("mp")
    nd = lax.axis_size("dp")
    grid_dev, width = grid_feat.shape[1:]
    nodes = node_feat.shape[1]
    nbrs = neighbours.shape[1]
    cap = send_rows.shape[2]
    rows = n * cap + nodes
    hc = width // n
    zc = 2 * hc // nd
    ny = n // 2
    steps = nd.bit_length() - 1
    out_rows = width // (n * nd)
    wscale = 1.0 / math.sqrt(nd * grid_dev * n)
    idx_rows = -(-nbrs // 8) * 8 + n
    idx_lanes = max(grid_dev, rows)
    vmem = pl.BlockSpec(memory_space=pltpu.VMEM)
    anywhere = pl.BlockSpec(memory_space=pl.ANY)
    dma = pltpu.SemaphoreType.DMA
    outs = (
        jax.ShapeDtypeStruct((grid_dev, width), BF16),
        jax.ShapeDtypeStruct((nodes, width), BF16),
        jax.ShapeDtypeStruct((out_rows, width), F32),
        jax.ShapeDtypeStruct((out_rows, 2 * width), F32),
    )
    held = pl.pallas_call(
        functools.partial(heads_kernel, n, nd, wscale),
        out_shape=outs,
        in_specs=[vmem, vmem, vmem, anywhere, anywhere, vmem, vmem],
        out_specs=(vmem, vmem, vmem, vmem),
        scratch_shapes=[
            pltpu.VMEM((width, width), BF16),
            pltpu.VMEM((width, 2 * width), BF16),
            pltpu.VMEM((n, -(-idx_rows // 8) * 8, idx_lanes), jnp.int32),
            pltpu.VMEM((n, nodes, width), BF16),
            pltpu.VMEM((nd, n, nodes, width // ny), BF16),
            pltpu.VMEM((n, grid_dev, width), BF16),
            pltpu.VMEM((n, grid_dev, hc), BF16),
            pltpu.VMEM((n, grid_dev, hc), BF16),
            pltpu.VMEM((n, grid_dev, hc), BF16),
            pltpu.VMEM((2, n * nodes, hc), BF16),
            pltpu.VMEM((2, n * nodes, hc), F32),
            pltpu.VMEM((n, grid_dev, hc), BF16),
            pltpu.VMEM((grid_dev, width), BF16),
            pltpu.VMEM((nd, n * nodes, zc), BF16),
            pltpu.VMEM((nd, ny, n * nodes, zc), BF16),
            pltpu.VMEM((n, nd, nodes, zc), BF16),
            pltpu.VMEM((nodes, 2 * width), BF16),
            pltpu.VMEM((n, out_rows, hc), BF16),
            pltpu.VMEM((n, out_rows, hc), BF16),
            pltpu.VMEM((2, nd, out_rows, ny * zc), BF16),
            pltpu.VMEM((2, nd, out_rows, ny * zc), BF16),
        ] + [
            pltpu.VMEM((n, nd >> (b + 1), 2, out_rows, hc), BF16) for b in range(steps)
        ] + [
            pltpu.VMEM((n, nd >> (b + 1), out_rows, hc), BF16) for b in range(steps)
        ] + [
            dma((2,)),
            dma((n,)), dma((n,)),
            dma((ny,)), dma((ny,)), dma((n,)), dma((3, nd, n)), dma((nd, n)),
            dma((n,)), dma((n,)),
            dma((n,)), dma((n,)),
            dma((ny,)), dma((ny,)), dma((n,)),
            dma((nd,)), dma((nd, ny)), dma((nd, ny)),
            dma((n,)), dma((n,)),
            dma((n,)), dma((n,)),
            dma((steps, n)), dma((steps, n)),
            dma((n,)), dma((n,)),
            dma((2, nd)), dma((2, nd)),
        ],
        compiler_params=pltpu.CompilerParams(
            collective_id=0, has_side_effects=True, vmem_limit_bytes=56 * 1024 * 1024
        ),
        name="heads_apart_grads",
    )(
        grid_feat[0], node_feat[0], cotangent[0], w_query, w_keyval,
        neighbours.T, send_rows[0],
    )
    d_grid, d_nodes, dw_query, dw_keyval = pl.pallas_call(
        copy_kernel, out_shape=outs, in_specs=[vmem] * 4, out_specs=(vmem,) * 4,
        name="results",
    )(*held)
    return d_grid[None], d_nodes[None], dw_query, dw_keyval


def per_device(*args):
    n = lax.axis_size("mp")
    nd = lax.axis_size("dp")
    samples_dev, grid_dev, width = args[0].shape
    hc = width // n
    apart = (
        samples_dev == 1
        and n % 2 == 0
        and nd >= 4
        and nd & (nd - 1) == 0
        and hc % LANES == 0
        and 2 * hc % (nd * LANES) == 0
        and grid_dev % LANES == 0
        and width % (HEADS * n) == 0
        and LANES % (width // HEADS) == 0
        and width % (n * nd * 16) == 0
        and args[6].shape[2] * n <= 256
        and args[1].shape[1] * n <= 256
    )
    return heads_apart(*args) if apart else rows_apart(*args)


def solution(mesh):
    in_specs = (
        P(("groups", "dp"), "mp", None),
        P(("groups", "dp"), "mp", None),
        P(("groups", "dp"), "mp", None),
        P(),
        P(),
        P("mp", None),
        P("mp", None, None),
    )
    out_specs = (
        P(("groups", "dp"), "mp", None),
        P(("groups", "dp"), "mp", None),
        P(("groups", "mp", "dp"), None),
        P(("groups", "mp", "dp"), None),
    )
    return jax.shard_map(
        per_device, mesh=mesh, in_specs=in_specs, out_specs=out_specs, check_vma=False
    )
```

```python
import functools
import math

import jax
import jax.numpy as jnp
from jax import lax
from jax.experimental import pallas as pl
from jax.experimental.pallas import tpu as pltpu
from jax.sharding import PartitionSpec as P

HEADS = 16
LANES = 128
MESH = pl.DeviceIdType.MESH
F32 = jnp.float32
BF16 = jnp.bfloat16


def dot_nn(x, y):
    return lax.dot_general(x, y, (((1,), (0,)), ((), ())), preferred_element_type=F32)


def dot_nt(x, y):
    return lax.dot_general(x, y, (((1,), (1,)), ((), ())), preferred_element_type=F32)


def dot_tn(x, y):
    return lax.dot_general(x, y, (((0,), (0,)), ((), ())), preferred_element_type=F32)


def kernel(
    n, nd, wscale,
    gf, nf, cot, wq_h, wkv_h, nbr, sr_col, sr_row,
    dgrid, dnodes, dwq, dwkv,
    wq, wkv, out_feat, tab, q_s, kv_s, count_s, gf_all, nf_all, dq_s, dq_all,
    part_s, ret_s, dkv_s, dkv_all, tq, tkv, rq, rkv, oq, okv, swq, swkv,
    local_sem, feat_ss, feat_rs, half_ss, half_rs, dq_ss, dq_rs, ret_ss, ret_rs,
    dkv_ss, dkv_rs, z_ss, z_rs, sw_ss, sw_rs,
):
    grid_dev, width = gf.shape
    nodes = nf.shape[0]
    slots = sr_col.shape[0]
    rows = slots + nodes
    cap = slots // n
    nbrs = nbr.shape[1]
    a = width // gf_all.shape[2]
    b = n // a
    high = width // a
    wide = width // b
    out_rows = dwq.shape[0]
    head = width // HEADS
    per = LANES // head
    scale = head ** (-0.5)
    me = lax.axis_index("mp")
    zd = lax.axis_index("dp")
    mine_i = me // b
    mine_j = lax.rem(me, b)

    def to_mp(src, dst, ssem, rsem, peer):
        return pltpu.make_async_remote_copy(
            src_ref=src, dst_ref=dst, send_sem=ssem, recv_sem=rsem,
            device_id={"mp": peer}, device_id_type=MESH,
        )

    def to_dp(src, dst, ssem, rsem, peer):
        return pltpu.make_async_remote_copy(
            src_ref=src, dst_ref=dst, send_sem=ssem, recv_sem=rsem,
            device_id={"dp": peer}, device_id_type=MESH,
        )

    def peer_of(o):
        return lax.rem(me + o, n)

    load_q = pltpu.make_async_copy(wq_h, wq, local_sem.at[0])
    load_kv = pltpu.make_async_copy(wkv_h, wkv, local_sem.at[1])
    load_q.start()
    load_kv.start()
    barrier = pltpu.get_barrier_semaphore()
    for o in range(1, n):
        pl.semaphore_signal(barrier, inc=1, device_id={"mp": peer_of(o)}, device_id_type=MESH)
    for o in range(1, nd):
        pl.semaphore_signal(
            barrier, inc=1, device_id={"dp": lax.rem(zd + o, nd)}, device_id_type=MESH
        )
    pick = (sr_col[...] == lax.broadcasted_iota(jnp.int32, (slots, nodes), 1)).astype(BF16)
    out_feat[...] = dot_nn(pick, nf[...]).astype(BF16)
    tab[pl.ds(slots, nodes), :] = nf[...]
    own_slots = pl.ds(pl.multiple_of(me * cap, cap), cap)
    tab[own_slots, :] = jnp.zeros((cap, width), BF16)
    for jb in range(b):
        ret_s[jb, own_slots, :] = jnp.zeros((cap, 2 * wide), BF16)
    pl.semaphore_wait(barrier, n - 1 + nd - 1)

    feat = []
    for o in range(1, n):
        there = pl.ds(pl.multiple_of(peer_of(o) * cap, cap), cap)
        feat.append(
            to_mp(out_feat.at[there], tab.at[own_slots], feat_ss.at[o], feat_rs.at[o], peer_of(o))
        )
        feat[-1].start()

    ids = nbr[...]
    row_id = lax.broadcasted_iota(jnp.int32, (grid_dev, rows), 1)
    count = jnp.zeros((grid_dev, rows), F32)
    for k in range(nbrs):
        count += (ids[:, k : k + 1] == row_id).astype(F32)
    for s in range(per):
        count_s[s * grid_dev : (s + 1) * grid_dev, :] = count
    half_cols = pl.ds(pl.multiple_of(mine_i * high, high), high)
    gf_all[me] = gf[:, half_cols]
    nf_all[me] = nf[:, half_cols]
    load_q.wait()
    q_s[...] = dot_nn(gf[...], wq[...]).astype(BF16)
    for c in feat:
        c.wait_recv()
    half = []
    for o in range(1, n):
        there = pl.ds(pl.multiple_of((peer_of(o) // b) * high, high), high)
        half.append(
            to_mp(nf.at[:, there], nf_all.at[me], half_ss.at[0, o], half_rs.at[0, o], peer_of(o))
        )
        half.append(
            to_mp(gf.at[:, there], gf_all.at[me], half_ss.at[1, o], half_rs.at[1, o], peer_of(o))
        )
    for c in half:
        c.start()
    load_kv.wait()
    kv_s[...] = dot_nn(tab[...], wkv[...]).astype(BF16)

    lane = lax.broadcasted_iota(jnp.int32, (1, LANES), 1)
    keep = [(lane // head) == s for s in range(per)]

    def spread(x):
        return jnp.concatenate([jnp.where(m, x, jnp.zeros_like(x)) for m in keep], axis=0)

    dq_copies = []
    ret_copies = []
    for jb in range(b):

        def one(blk, carry):
            off = pl.multiple_of(jb * wide + blk * LANES, LANES)
            at = pl.ds(off, LANES)
            at_v = pl.ds(pl.multiple_of(width + off, LANES), LANES)
            here = pl.ds(pl.multiple_of(blk * LANES, LANES), LANES)
            here_v = pl.ds(pl.multiple_of(wide + blk * LANES, LANES), LANES)
            qs = spread(q_s[:, at])
            cs = spread(cot[:, at])
            keys = kv_s[:, at]
            values = kv_s[:, at_v]
            times = count_s[...]
            scores = dot_nt(qs, keys) * scale
            d_attn = dot_nt(cs, values)
            top = jnp.max(
                jnp.where(times > 0, scores, -jnp.inf), axis=1, keepdims=True
            )
            e = jnp.where(times > 0, times * jnp.exp(jnp.minimum(scores - top, 0.0)), 0.0)
            attn = e / jnp.sum(e, axis=1, keepdims=True)
            ds = attn * (d_attn - jnp.sum(attn * d_attn, axis=1, keepdims=True)) * scale
            ds = ds.astype(BF16)
            attn = attn.astype(BF16)
            dq = None
            for s in range(per):
                term = dot_nn(
                    ds[s * grid_dev : (s + 1) * grid_dev],
                    jnp.where(keep[s], keys, jnp.zeros_like(keys)),
                )
                dq = term if dq is None else dq + term
            dq_s[jb, :, here] = dq.astype(BF16)
            part_s[jb, :, here] = dot_tn(ds, qs).astype(BF16)
            part_s[jb, :, here_v] = dot_tn(attn, cs).astype(BF16)
            return carry

        lax.fori_loop(0, wide // LANES, one, 0)
        for o in range(1, n):
            peer = peer_of(o)
            c = to_mp(dq_s.at[jb], dq_all.at[me], dq_ss.at[o], dq_rs.at[o], peer)

            @pl.when(lax.rem(peer, b) == jb)
            def _():
                c.start()

        for o in range(1, n):
            there = pl.ds(pl.multiple_of(peer_of(o) * cap, cap), cap)
            c = to_mp(
                part_s.at[jb, there], ret_s.at[jb, own_slots],
                ret_ss.at[jb, o], ret_rs.at[jb, o], peer_of(o),
            )
            c.start()
            ret_copies.append(c)

    dq_all[me] = dq_s[mine_j]
    acc = None
    for jb in range(b):
        term = dot_nt(dq_s[jb], wq[:, jb * wide : (jb + 1) * wide])
        acc = term if acc is None else acc + term
    dgrid[...] = acc.astype(BF16)

    place = (sr_row[...] == lax.broadcasted_iota(jnp.int32, (nodes, slots), 0)).astype(BF16)
    for jb in range(b):
        for o in range(1, n):
            ret_copies[jb * (n - 1) + o - 1].wait_recv()
        dkv = part_s[jb, slots:, :].astype(F32) + dot_nn(place, ret_s[jb])
        dkv_s[jb] = dkv.astype(BF16)
        for o in range(1, n):
            peer = peer_of(o)
            c = to_mp(dkv_s.at[jb], dkv_all.at[me], dkv_ss.at[o], dkv_rs.at[o], peer)

            @pl.when(lax.rem(peer, b) == jb)
            def _():
                c.start()

    dkv_all[me] = dkv_s[mine_j]

    def got(src, dst, ssem, rsem):
        return to_mp(src, dst, ssem, rsem, peer_of(1))

    for c in half:
        c.wait_recv()
    for o in range(1, n):
        got(dq_s.at[0], dq_all.at[me], dq_ss.at[o], dq_rs.at[o]).wait_recv()
    term_q = dot_tn(
        gf_all[...].reshape(n * grid_dev, high), dq_all[...].reshape(n * grid_dev, wide)
    ) * wscale
    term_q = term_q.astype(BF16).reshape(b, nd, out_rows, wide)
    for d in range(nd):
        tq[d] = term_q[:, d]
    z_copies = []
    for o in range(1, nd):
        peer = lax.rem(zd + o, nd)
        z_copies.append(to_dp(tq.at[peer], rq.at[o], z_ss.at[0, o], z_rs.at[0, o], peer))
        z_copies[-1].start()

    acc = None
    for jb in range(b):
        for k in range(2):
            term = dot_nt(
                dkv_s[jb, :, k * wide : (k + 1) * wide],
                wkv[:, k * width + jb * wide : k * width + (jb + 1) * wide],
            )
            acc = term if acc is None else acc + term
    dnodes[...] = acc.astype(BF16)

    for o in range(1, n):
        got(dkv_s.at[0], dkv_all.at[me], dkv_ss.at[o], dkv_rs.at[o]).wait_recv()
    term_kv = dot_tn(
        nf_all[...].reshape(n * nodes, high), dkv_all[...].reshape(n * nodes, 2 * wide)
    ) * wscale
    term_kv = term_kv.astype(BF16).reshape(b, nd, out_rows, 2 * wide)
    for d in range(nd):
        tkv[d] = term_kv[:, d]
    for o in range(1, nd):
        peer = lax.rem(zd + o, nd)
        z_copies.append(to_dp(tkv.at[peer], rkv.at[o], z_ss.at[1, o], z_rs.at[1, o], peer))
        z_copies[-1].start()

    def finish(which, t, r, out, sw, width_out):
        total = t[zd].astype(F32)
        for o in range(1, nd):
            z_copies[which * (nd - 1) + o - 1].wait_recv()
            total += r[o].astype(F32)
        out[...] = total.astype(BF16)
        sent = []
        for o in range(1, b):
            mate = lax.rem(mine_j + o, b)
            c = to_mp(
                out.at[mate], sw.at[o], sw_ss.at[which, o], sw_rs.at[which, o],
                mine_i * b + mate,
            )
            c.start()
            sent.append(c)
        return sent

    sent_q = finish(0, tq, rq, oq, swq, wide)
    sent_kv = finish(1, tkv, rkv, okv, swkv, 2 * wide)

    def columns(j, k):
        return pl.ds(pl.multiple_of(k * width + j * wide, LANES), wide)

    dwq[:, columns(mine_j, 0)] = oq[mine_j].astype(F32)
    for o in range(1, b):
        source = lax.rem(mine_j + b - o, b)
        sent_q[o - 1].wait_recv()
        dwq[:, columns(source, 0)] = swq[o].astype(F32)
    for k in range(2):
        dwkv[:, columns(mine_j, k)] = okv[mine_j][:, k * wide : (k + 1) * wide].astype(F32)
    for o in range(1, b):
        source = lax.rem(mine_j + b - o, b)
        sent_kv[o - 1].wait_recv()
        for k in range(2):
            dwkv[:, columns(source, k)] = swkv[o][:, k * wide : (k + 1) * wide].astype(F32)

    for c in feat + half + ret_copies + z_copies + sent_q + sent_kv:
        c.wait_send()
    for o in range(1, n):
        got(dq_s.at[0], dq_all.at[me], dq_ss.at[o], dq_rs.at[o]).wait_send()
        got(dkv_s.at[0], dkv_all.at[me], dkv_ss.at[o], dkv_rs.at[o]).wait_send()


def rows_apart(grid_feat, node_feat, cotangent, w_query, w_keyval, neighbours, send_rows):
    n = lax.axis_size("mp")
    nd = lax.axis_size("dp")
    samples_dev, grid_dev, width = grid_feat.shape
    nodes = node_feat.shape[1]
    cap = send_rows.shape[2]
    slots = n * cap
    rows = slots + nodes
    a = 2
    b = n // a
    high = width // a
    wide = width // b
    out_rows = width // (n * nd)
    per = LANES * HEADS // width
    wscale = 1.0 / math.sqrt(samples_dev * nd * grid_dev * n)
    vmem = pl.BlockSpec(memory_space=pltpu.VMEM)
    anywhere = pl.BlockSpec(memory_space=pl.ANY)
    dma = pltpu.SemaphoreType.DMA
    d_grid, d_nodes, dw_query, dw_keyval = pl.pallas_call(
        functools.partial(kernel, n, nd, wscale),
        out_shape=(
            jax.ShapeDtypeStruct((grid_dev, width), BF16),
            jax.ShapeDtypeStruct((nodes, width), BF16),
            jax.ShapeDtypeStruct((out_rows, width), F32),
            jax.ShapeDtypeStruct((out_rows, 2 * width), F32),
        ),
        in_specs=[vmem, vmem, vmem, anywhere, anywhere, vmem, vmem, vmem],
        out_specs=(vmem, vmem, vmem, vmem),
        scratch_shapes=[
            pltpu.VMEM((width, width), BF16),
            pltpu.VMEM((width, 2 * width), BF16),
            pltpu.VMEM((slots, width), BF16),
            pltpu.VMEM((rows, width), BF16),
            pltpu.VMEM((grid_dev, width), BF16),
            pltpu.VMEM((rows, 2 * width), BF16),
            pltpu.VMEM((per * grid_dev, rows), F32),
            pltpu.VMEM((n, grid_dev, high), BF16),
            pltpu.VMEM((n, nodes, high), BF16),
            pltpu.VMEM((b, grid_dev, wide), BF16),
            pltpu.VMEM((n, grid_dev, wide), BF16),
            pltpu.VMEM((b, rows, 2 * wide), BF16),
            pltpu.VMEM((b, slots, 2 * wide), BF16),
            pltpu.VMEM((b, nodes, 2 * wide), BF16),
            pltpu.VMEM((n, nodes, 2 * wide), BF16),
            pltpu.VMEM((nd, b, out_rows, wide), BF16),
            pltpu.VMEM((nd, b, out_rows, 2 * wide), BF16),
            pltpu.VMEM((nd, b, out_rows, wide), BF16),
            pltpu.VMEM((nd, b, out_rows, 2 * wide), BF16),
            pltpu.VMEM((b, out_rows, wide), BF16),
            pltpu.VMEM((b, out_rows, 2 * wide), BF16),
            pltpu.VMEM((b, out_rows, wide), BF16),
            pltpu.VMEM((b, out_rows, 2 * wide), BF16),
            dma((2,)),
            dma((n,)), dma((n,)),
            dma((2, n)), dma((2, n)),
            dma((n,)), dma((n,)),
            dma((b, n)), dma((b, n)),
            dma((n,)), dma((n,)),
            dma((2, nd)), dma((2, nd)),
            dma((2, b)), dma((2, b)),
        ],
        compiler_params=pltpu.CompilerParams(
            collective_id=0, has_side_effects=True, vmem_limit_bytes=56 * 1024 * 1024
        ),
        name="graph_attention_grads",
    )(
        grid_feat[0], node_feat[0], cotangent[0], w_query, w_keyval, neighbours,
        send_rows.reshape(slots, 1), send_rows.reshape(1, slots),
    )
    return d_grid[None], d_nodes[None], dw_query, dw_keyval


def heads_kernel(
    n, nd, wscale,
    gf_h, nf_h, cot_h, wq_h, wkv_h, nbr_h, sr_h,
    dgrid, dnodes, dwq, dwkv,
    wq, wkv, cot, own_term, nbr_t, sr, times_all, idx_all, nf_all, nf_part, gf_all, q_s, q_all, cot_all, kv_s, dkv_acc, dq_s, dq_rows,
    dkv_s, dkv_all, ret_kv, dkv_rows, fin_s, fin_q, tkv, fin_kv, *rest,
):
    steps = nd.bit_length() - 1
    halves, rest = rest[: steps], rest[steps:]
    gots, rest = rest[: steps], rest[steps:]
    (
        local_sem, idx_ss, idx_rs, nfy_ss, nfm_ss, nf_rs, part_ss, part_rs, cot_ss, cot_rs, q_ss, q_rs,
        gfy_ss, gfm_ss, gf_rs, sc_ss, scy_ss, sc_rs, rq_ss, rq_rs, rkv_ss, rkv_rs,
        h_ss, h_rs, fq_ss, fq_rs, fk_ss, fk_rs,
    ) = rest
    grid_dev, width = gf_h.shape
    nodes = nf_h.shape[0]
    nbrs = nbr_t.shape[0]
    cap = sr.shape[1]
    slots = n * cap
    rows = slots + nodes
    all_nodes = n * nodes
    hc = width // n
    zc = 2 * hc // nd
    per_half = nd // 2
    out_rows = dwq.shape[0]
    head = width // HEADS
    per = LANES // head
    scale = head ** (-0.5)
    ny = n // 2
    wy = width // ny
    sr_at = idx_all.shape[1] - n
    me = lax.axis_index("mp")
    zd = lax.axis_index("dp")
    core = lax.rem(me, 2)
    chip = lax.div(me, 2)
    mate = me + 1 - 2 * core

    def place_of(m):
        return lax.rem(m, 2) * ny + lax.div(m, 2)

    mine = place_of(me)
    sent = []

    def send(src, dst, ssem, rsem, mp=None, dp=None, when=None):
        device = {}
        if mp is not None:
            device["mp"] = mp
        if dp is not None:
            device["dp"] = dp
        c = pltpu.make_async_remote_copy(
            src_ref=src, dst_ref=dst, send_sem=ssem, recv_sem=rsem,
            device_id=device, device_id_type=MESH,
        )
        if when is None:
            c.start()
        else:
            pl.when(when)(c.start)
        sent.append((c, when))

    def arrived(dst, rsem):
        pltpu.make_async_remote_copy(
            src_ref=dst, dst_ref=dst, send_sem=rsem, recv_sem=rsem,
            device_id={"mp": mate}, device_id_type=MESH,
        ).wait_recv()

    def peer_of(o):
        return lax.rem(me + o, n)

    barrier = pltpu.get_barrier_semaphore()
    for o in range(n):
        for k in range(nd):
            if o or k:
                pl.semaphore_signal(
                    barrier, inc=1,
                    device_id={"mp": peer_of(o), "dp": lax.rem(zd + k, nd)}, device_id_type=MESH,
                )
    own_cols = pl.ds(pl.multiple_of(me * hc, hc), hc)
    half_cols = pl.ds(pl.multiple_of(chip * wy, LANES), wy)

    def load(i, src, dst):
        c = pltpu.make_async_copy(src, dst, local_sem.at[i])
        c.start()
        return c

    load_nbr = load(0, nbr_h, nbr_t)
    load_sr = load(1, sr_h, sr)
    load_nf = load(2, nf_h, nf_all.at[mine])
    load_part = load(3, nf_h.at[:, half_cols], nf_part.at[zd, mine])
    load_gf = load(5, gf_h, gf_all.at[mine])
    load_q = load(6, wq_h, wq)
    load_cot = load(4, cot_h, cot)
    load_kv = load(7, wkv_h, wkv)

    load_nbr.wait()
    load_sr.wait()
    lane_slot = lax.broadcasted_iota(jnp.int32, (cap, rows), 1)
    tile = (lax.rem(lane_slot, cap) == lax.broadcasted_iota(jnp.int32, (cap, rows), 0)).astype(BF16)
    spread_rows = dot_nn(sr[...].astype(F32).astype(BF16), tile).astype(jnp.int32) + mine * nodes
    lane_row = lax.broadcasted_iota(jnp.int32, (n, rows), 1)
    own_lane = (lane_row >= me * cap) & (lane_row < me * cap + cap)
    idx_all[me] = jnp.zeros(idx_all.shape[1:], jnp.int32)
    idx_all[me, 0:nbrs, 0:grid_dev] = nbr_t[...]
    idx_all[me, sr_at : sr_at + n, 0:rows] = jnp.where(own_lane, spread_rows, 0)
    load_nf.wait()
    load_part.wait()
    pl.semaphore_wait(barrier, n * nd - 1)

    for o in range(1, n):
        send(idx_all.at[me], idx_all.at[me], idx_ss.at[o], idx_rs.at[me], mp=peer_of(o))

    def right_of(src, ssem, rsem, when):
        send(src, src, ssem, rsem, dp=lax.rem(zd + 1, nd), when=when)

    def left_of(src, ssem, rsem, when):
        send(src, src, ssem, rsem, dp=lax.rem(zd + nd - 1, nd), when=when)

    has_right = zd + 1 < nd
    has_left = zd > 0

    def pass_on(sample, p, to_right, to_left, when):
        block = nf_part.at[sample, p]
        rsem = part_rs.at[sample, p]
        if to_right is not None:
            right_of(block, part_ss.at[1, sample, p], rsem, to_right)
        if to_left is not None:
            left_of(block, part_ss.at[2, sample, p], rsem, to_left)
        if when is not None:
            send(block, block, part_ss.at[0, sample, p], rsem, mp=mate, when=when)

    for o in range(1, ny):
        there = lax.rem(chip + o, ny) * 2 + core
        send(nf_all.at[mine], nf_all.at[mine], nfy_ss.at[o], nf_rs.at[mine], mp=there)
    send(nf_all.at[mine], nf_all.at[mine], nfm_ss.at[0], nf_rs.at[mine], mp=mate)
    pass_on(zd, mine, has_right, has_left, None)
    readers = [lax.rem(chip + o, ny) * 2 + lax.rem(core + k, 2) for k in range(2) for o in range(ny)]
    readers = readers[1:ny] + [readers[ny]] + readers[ny + 1 :]

    def send_cot(i):
        there = readers[i]
        cols = pl.ds(pl.multiple_of(there * hc, hc), hc)
        send(cot.at[:, cols], cot_all.at[me], cot_ss.at[i], cot_rs.at[me], mp=there)

    load_cot.wait()
    for i in range(ny):
        send_cot(i)
    cot_all[me] = cot[:, own_cols]
    load_gf.wait()
    load_q.wait()
    query = dot_nn(gf_all[mine], wq[...]).astype(BF16)
    for k in range(n):
        q_s[k] = query[:, k * hc : (k + 1) * hc]
    for i in range(n - 1):
        there = readers[i]
        if i >= ny:
            send_cot(i)
        send(q_s.at[there], q_all.at[me], q_ss.at[i], q_rs.at[me], mp=there)
    q_all[me] = q_s[me]
    for o in range(1, ny):
        there = lax.rem(chip + o, ny) * 2 + core
        send(gf_all.at[mine], gf_all.at[mine], gfy_ss.at[o], gf_rs.at[mine], mp=there)
    send(gf_all.at[mine], gf_all.at[mine], gfm_ss.at[0], gf_rs.at[mine], mp=mate)

    for o in range(1, n):
        there = peer_of(o)
        arrived(idx_all.at[there], idx_rs.at[there])
    plan = None
    for m in range(n):
        part = idx_all[m, sr_at : sr_at + n, 0:rows]
        plan = part if plan is None else plan + part
    own_rows = lax.broadcasted_iota(jnp.int32, (1, rows), 1)
    node_iota = lax.broadcasted_iota(jnp.int32, (all_nodes, rows), 0)
    row_iota = lax.broadcasted_iota(jnp.int32, (rows, grid_dev), 0)
    reader = lax.broadcasted_iota(jnp.int32, (n, rows), 0)

    def count_shard(d, carry):
        ids = idx_all[d, 0:nbrs, 0:grid_dev]
        count = jnp.zeros((rows, grid_dev), F32)
        for k in range(nbrs):
            count += (ids[k : k + 1, :] == row_iota).astype(F32)
        remote = jnp.sum(jnp.where(reader == d, plan, 0), axis=0, keepdims=True)
        target = jnp.where(own_rows < slots, remote, place_of(d) * nodes + own_rows - slots)
        named = (node_iota == target).astype(BF16)
        times_all[d] = dot_nn(named, count.astype(BF16))
        return carry

    lax.fori_loop(0, n, count_shard, 0)
    dkv_acc[...] = jnp.zeros_like(dkv_acc)
    for o in range(1, ny):
        p = core * ny + lax.rem(chip + ny - o, ny)
        arrived(nf_all.at[p], nf_rs.at[p])
        send(nf_all.at[p], nf_all.at[p], nfm_ss.at[o], nf_rs.at[p], mp=mate)
        nf_part[zd, p] = nf_all[p, :, half_cols]
        pass_on(zd, p, has_right, has_left, None)
    for o in range(ny):
        p = (1 - core) * ny + lax.rem(chip + o, ny)
        arrived(nf_all.at[p], nf_rs.at[p])
        nf_part[zd, p] = nf_all[p, :, half_cols]
    load_kv.wait()
    node_rows = nf_all[...].reshape(all_nodes, width)
    for k in range(2):
        cols = pl.ds(pl.multiple_of(k * width + me * hc, LANES), hc)
        kv_s[k] = dot_nn(node_rows, wkv[:, cols]).astype(BF16)
    def chain(o, y):
        p = core * ny + lax.rem(chip + y, ny)
        from_left = zd >= o
        from_right = zd + o < nd
        left_sample = lax.rem(zd + nd - o, nd)
        right_sample = lax.rem(zd + o, nd)

        @pl.when(from_left)
        def _():
            arrived(nf_part.at[left_sample, p], part_rs.at[left_sample, p])

        pass_on(left_sample, p, from_left & has_right, None, from_left)

        @pl.when(from_right)
        def _():
            arrived(nf_part.at[right_sample, p], part_rs.at[right_sample, p])

        pass_on(right_sample, p, None, from_right & has_left, from_right)

    lane = lax.broadcasted_iota(jnp.int32, (1, LANES), 1)
    keep = [(lane // head) == s for s in range(per)]

    def spread(x):
        return jnp.concatenate([jnp.where(m, x, jnp.zeros_like(x)) for m in keep], axis=0)

    def shard(d):
        times = times_all[d]
        times = jnp.concatenate([times] * per, axis=1)

        def pair(j, carry):
            at = pl.ds(pl.multiple_of(j * LANES, LANES), LANES)
            qs = spread(q_all[d, :, at])
            cs = spread(cot_all[d, :, at])
            keys = kv_s[0, :, at]
            values = kv_s[1, :, at]
            scores = dot_nt(keys, qs) * scale
            d_attn = dot_nt(values, cs)
            scores = jnp.where(times > 0, scores, -jnp.inf)
            e = times * jnp.exp(scores - jnp.max(scores, axis=0, keepdims=True))
            attn = e * (1.0 / jnp.sum(e, axis=0, keepdims=True))
            ds = attn * (d_attn - jnp.sum(attn * d_attn, axis=0, keepdims=True)) * scale
            ds = ds.astype(BF16)
            attn = attn.astype(BF16)
            both = dot_tn(ds, keys)
            dq = both[:grid_dev]
            for s in range(1, per):
                dq = jnp.where(keep[s], both[s * grid_dev : (s + 1) * grid_dev], dq)
            dq_s[d, :, at] = dq.astype(BF16)
            dkv_acc[0, :, at] += dot_nn(ds, qs).astype(BF16).astype(F32)
            dkv_acc[1, :, at] += dot_nn(attn, cs).astype(BF16).astype(F32)
            return carry

        lax.fori_loop(0, hc // LANES, pair, 0, unroll=True)

    def await_shard(d):
        arrived(cot_all.at[d], cot_rs.at[d])
        arrived(q_all.at[d], q_rs.at[d])

    links = [(o, y) for o in range(1, nd) for y in range(ny)]

    def poll():
        if links:
            chain(*links.pop(0))

    poll()
    shard(me)
    await_shard(mate)
    shard(mate)
    poll()
    for o in range(1, ny):
        for k in range(2):
            d = lax.rem(chip + ny - o, ny) * 2 + lax.rem(core + k, 2)
            await_shard(d)
            shard(d)
            if k == 0:
                poll()

    for k in range(nd):
        half, off = k // per_half, (k % per_half) * zc
        dkv_s[k] = dkv_acc[half, :, off : off + zc].astype(BF16)
    far_first = []
    for o in range(nd - 1, 0, -1):
        far_first.append((lax.rem(zd + nd - o, nd), zd >= o, 2 * o - 1))
        far_first.append((lax.rem(zd + o, nd), zd + o < nd, 2 * o - 2))
    for there, here, i in far_first:
        send(
            dkv_s.at[there], dkv_all.at[zd, chip], sc_ss.at[i], sc_rs.at[zd, chip],
            dp=there, when=here,
        )
    dkv_all[zd, chip] = dkv_s[zd]

    def across(sample, when):
        block = dkv_all.at[sample, chip]
        for o in range(1, ny):
            there = lax.rem(chip + o, ny) * 2 + core
            send(block, block, scy_ss.at[sample, o], sc_rs.at[sample, chip], mp=there, when=when)

    def gather_across(o):
        for sample, here in ((lax.rem(zd + nd - o, nd), zd >= o), (lax.rem(zd + o, nd), zd + o < nd)):

            @pl.when(here)
            def _():
                arrived(dkv_all.at[sample, chip], sc_rs.at[sample, chip])

            across(sample, here)

    across(zd, None)
    for o in range(1, n):
        there = peer_of(o)
        send(dq_s.at[there], dq_rows.at[:, own_cols], rq_ss.at[o], rq_rs.at[me], mp=there)
    dq_rows[:, own_cols] = dq_s[me]
    ret_kv[me] = dkv_s[:, pl.ds(pl.multiple_of(mine * nodes, nodes), nodes)]

    targets = [peer_of(o + 1) for o in range(n)]
    theirs = (1 - core) * ny + chip
    arrived(gf_all.at[theirs], gf_rs.at[theirs])

    def query_term(t, chips):
        cols = pl.ds(pl.multiple_of(t * hc, LANES), hc)
        left = [gf_all[c * ny + y, :, cols] for y in chips for c in range(2)]
        right = [dq_s[y * 2 + c] for y in chips for c in range(2)]
        return dot_tn(jnp.concatenate(left, axis=0), jnp.concatenate(right, axis=0))

    for t in targets:
        own_term[t] = query_term(t, [chip])
    poll()
    for o in range(1, ny):
        p = core * ny + lax.rem(chip + ny - o, ny)
        arrived(gf_all.at[p], gf_rs.at[p])
        send(gf_all.at[p], gf_all.at[p], gfm_ss.at[o], gf_rs.at[p], mp=mate)
    poll()
    for o in range(1, ny):
        p = (1 - core) * ny + lax.rem(chip + o, ny)
        arrived(gf_all.at[p], gf_rs.at[p])

    bits = [lax.rem(lax.div(zd, 1 << b), 2) for b in range(steps)]
    mates = [zd + (1 << b) * (1 - 2 * bits[b]) for b in range(steps)]

    def give(b, t):
        send(
            halves[b].at[t, :, 1 - bits[b]], gots[b].at[t], h_ss.at[b, t], h_rs.at[b, t],
            dp=mates[b],
        )

    others = [lax.rem(chip + o, ny) for o in range(1, ny)]
    for t in targets:
        term = (own_term[t] + query_term(t, others)) * wscale
        halves[0][t] = term.astype(BF16).reshape(per_half, 2, out_rows, hc)
        give(0, t)

    def column(m, k):
        return (k // per_half) * width + m * hc + (k % per_half) * zc

    def halve(b, i):
        t = targets[i]
        arrived(gots[b].at[t], h_rs.at[b, t])
        total = halves[b][t, :, bits[b]].astype(F32) + gots[b][t].astype(F32)
        total = total.astype(BF16)
        if b + 1 < steps:
            halves[b + 1][t] = total.reshape(halves[b + 1].shape[1:])
            give(b + 1, t)
        elif i < n - 1:
            fin_s[t] = total.reshape(out_rows, hc)
            send(fin_s.at[t], fin_q.at[me], fq_ss.at[i], fq_rs.at[me], mp=t)
        else:
            fin_q[me] = total.reshape(out_rows, hc)

    for o in range(1, nd):
        gather_across(o)
        poll()
    while links:
        poll()
    def keyval_block(i, y):
        k = lax.rem(core + 1 + i, 2)
        cols = pl.ds(pl.multiple_of(k * hc, LANES), hc)
        term = dot_tn(
            nf_part[:, :, :, cols].reshape(nd * all_nodes, hc),
            dkv_all[:, y].reshape(nd * all_nodes, zc),
        ) * wscale
        tkv[k, y] = term.astype(BF16).reshape(nd, out_rows, zc)

        def block_to(there, when):
            send(
                tkv.at[k, y, there], fin_kv.at[core, zd, y], fk_ss.at[k, y, there],
                fk_rs.at[core, zd, y], mp=chip * 2 + k, dp=there, when=when,
            )

        for there, here, _ in far_first:
            block_to(there, here)
        if i == 0:
            block_to(zd, None)
        else:
            fin_kv[core, zd, y] = tkv[k, y, zd]

    for o in range(1, nd):
        there = lax.rem(zd + o, nd)
        for y in range(ny):
            p = (1 - core) * ny + y
            arrived(nf_part.at[there, p], part_rs.at[there, p])
    keyval_block(0, chip)
    keyval_block(1, chip)
    for i in range(n // 2):
        halve(0, i)
    for o in range(1, n):
        there = peer_of(o)
        arrived(dq_rows.at[:, pl.ds(pl.multiple_of(there * hc, hc), hc)], rq_rs.at[there])
    dgrid[...] = dot_nt(dq_rows[...], wq[...]).astype(BF16)
    for i in range(n // 2, n - 1):
        halve(0, i)
    for s in range(nd):
        for y in others:
            arrived(dkv_all.at[s, y], sc_rs.at[s, y])
    for o in range(1, n):
        there = peer_of(o)
        node_block = pl.ds(pl.multiple_of(place_of(there) * nodes, nodes), nodes)
        send(dkv_s.at[:, node_block], ret_kv.at[me], rkv_ss.at[o], rkv_rs.at[me], mp=there)
    for i in range(2):
        for y in others:
            keyval_block(i, y)
    halve(0, n - 1)
    for o in range(1, n):
        there = peer_of(o)
        arrived(ret_kv.at[there], rkv_rs.at[there])
    for m in range(n):
        for k in range(nd):
            dkv_rows[:, column(m, k) : column(m, k) + zc] = ret_kv[m, k]
    dnodes[...] = dot_nt(dkv_rows[...], wkv[...]).astype(BF16)
    for b in range(1, steps):
        for i in range(n):
            halve(b, i)

    for o in range(1, n):
        there = peer_of(o)
        arrived(fin_q.at[there], fq_rs.at[there])
    for m in range(n):
        dwq[:, m * hc : (m + 1) * hc] = fin_q[m].astype(F32)
    for o in range(2):
        for k in range(nd):
            if o or k:
                c, s = lax.rem(core + o, 2), lax.rem(zd + k, nd)
                for y in range(ny):
                    arrived(fin_kv.at[c, s, y], fk_rs.at[c, s, y])
    for c in range(2):
        for k in range(nd):
            for y in range(ny):
                at = column(y * 2 + c, k)
                dwkv[:, at : at + zc] = fin_kv[c, k, y].astype(F32)
    for c, when in sent:
        if when is None:
            c.wait_send()
        else:
            pl.when(when)(c.wait_send)


def copy_kernel(*refs):
    for i in range(len(refs) // 2):
        refs[len(refs) // 2 + i][...] = refs[i][...]


def heads_apart(grid_feat, node_feat, cotangent, w_query, w_keyval, neighbours, send_rows):
    n = lax.axis_size("mp")
    nd = lax.axis_size("dp")
    grid_dev, width = grid_feat.shape[1:]
    nodes = node_feat.shape[1]
    nbrs = neighbours.shape[1]
    cap = send_rows.shape[2]
    rows = n * cap + nodes
    hc = width // n
    zc = 2 * hc // nd
    ny = n // 2
    steps = nd.bit_length() - 1
    out_rows = width // (n * nd)
    wscale = 1.0 / math.sqrt(nd * grid_dev * n)
    idx_rows = -(-nbrs // 8) * 8 + n
    idx_lanes = max(grid_dev, rows)
    vmem = pl.BlockSpec(memory_space=pltpu.VMEM)
    hbm = pl.BlockSpec(memory_space=pltpu.HBM)
    dma = pltpu.SemaphoreType.DMA
    outs = (
        jax.ShapeDtypeStruct((grid_dev, width), BF16),
        jax.ShapeDtypeStruct((nodes, width), BF16),
        jax.ShapeDtypeStruct((out_rows, width), F32),
        jax.ShapeDtypeStruct((out_rows, 2 * width), F32),
    )
    held = pl.pallas_call(
        functools.partial(heads_kernel, n, nd, wscale),
        out_shape=outs,
        in_specs=[hbm] * 7,
        out_specs=(vmem, vmem, vmem, vmem),
        scratch_shapes=[
            pltpu.VMEM((width, width), BF16),
            pltpu.VMEM((width, 2 * width), BF16),
            pltpu.VMEM((grid_dev, width), BF16),
            pltpu.VMEM((n, hc, hc), F32),
            pltpu.VMEM((nbrs, grid_dev), jnp.int32),
            pltpu.VMEM((n, cap), jnp.int32),
            pltpu.VMEM((n, n * nodes, grid_dev), F32),
            pltpu.VMEM((n, -(-idx_rows // 8) * 8, idx_lanes), jnp.int32),
            pltpu.VMEM((n, nodes, width), BF16),
            pltpu.VMEM((nd, n, nodes, width // ny), BF16),
            pltpu.VMEM((n, grid_dev, width), BF16),
            pltpu.VMEM((n, grid_dev, hc), BF16),
            pltpu.VMEM((n, grid_dev, hc), BF16),
            pltpu.VMEM((n, grid_dev, hc), BF16),
            pltpu.VMEM((2, n * nodes, hc), BF16),
            pltpu.VMEM((2, n * nodes, hc), F32),
            pltpu.VMEM((n, grid_dev, hc), BF16),
            pltpu.VMEM((grid_dev, width), BF16),
            pltpu.VMEM((nd, n * nodes, zc), BF16),
            pltpu.VMEM((nd, ny, n * nodes, zc), BF16),
            pltpu.VMEM((n, nd, nodes, zc), BF16),
            pltpu.VMEM((nodes, 2 * width), BF16),
            pltpu.VMEM((n, out_rows, hc), BF16),
            pltpu.VMEM((n, out_rows, hc), BF16),
            pltpu.VMEM((2, ny, nd, out_rows, zc), BF16),
            pltpu.VMEM((2, nd, ny, out_rows, zc), BF16),
        ] + [
            pltpu.VMEM((n, nd >> (b + 1), 2, out_rows, hc), BF16) for b in range(steps)
        ] + [
            pltpu.VMEM((n, nd >> (b + 1), out_rows, hc), BF16) for b in range(steps)
        ] + [
            dma((8,)),
            dma((n,)), dma((n,)),
            dma((ny,)), dma((ny,)), dma((n,)), dma((3, nd, n)), dma((nd, n)),
            dma((n,)), dma((n,)),
            dma((n,)), dma((n,)),
            dma((ny,)), dma((ny,)), dma((n,)),
            dma((2 * nd,)), dma((nd, ny)), dma((nd, ny)),
            dma((n,)), dma((n,)),
            dma((n,)), dma((n,)),
            dma((steps, n)), dma((steps, n)),
            dma((n,)), dma((n,)),
            dma((2, ny, nd)), dma((2, nd, ny)),
        ],
        compiler_params=pltpu.CompilerParams(
            collective_id=0, has_side_effects=True, vmem_limit_bytes=28 * 1024 * 1024
        ),
        name="heads_apart_grads",
    )(*(
        pltpu.with_memory_space_constraint(x, pltpu.HBM)
        for x in (
            grid_feat[0], node_feat[0], cotangent[0], w_query, w_keyval,
            neighbours.T, send_rows[0],
        )
    ))
    d_grid, d_nodes, dw_query, dw_keyval = pl.pallas_call(
        copy_kernel, out_shape=outs, in_specs=[vmem] * 4, out_specs=(vmem,) * 4,
        compiler_params=pltpu.CompilerParams(vmem_limit_bytes=4 * 1024 * 1024),
        name="results",
    )(*held)
    return d_grid[None], d_nodes[None], dw_query, dw_keyval


def per_device(*args):
    n = lax.axis_size("mp")
    nd = lax.axis_size("dp")
    samples_dev, grid_dev, width = args[0].shape
    hc = width // n
    apart = (
        samples_dev == 1
        and n % 2 == 0
        and nd >= 4
        and nd & (nd - 1) == 0
        and hc % LANES == 0
        and 2 * hc % (nd * LANES) == 0
        and grid_dev % LANES == 0
        and width % (HEADS * n) == 0
        and LANES % (width // HEADS) == 0
        and width % (n * nd * 16) == 0
        and args[6].shape[2] * n <= 256
        and args[1].shape[1] * n <= 256
    )
    return heads_apart(*args) if apart else rows_apart(*args)


def solution(mesh):
    in_specs = (
        P(("groups", "dp"), "mp", None),
        P(("groups", "dp"), "mp", None),
        P(("groups", "dp"), "mp", None),
        P(),
        P(),
        P("mp", None),
        P("mp", None, None),
    )
    out_specs = (
        P(("groups", "dp"), "mp", None),
        P(("groups", "dp"), "mp", None),
        P(("groups", "mp", "dp"), None),
        P(("groups", "mp", "dp"), None),
    )
    return jax.shard_map(
        per_device, mesh=mesh, in_specs=in_specs, out_specs=out_specs, check_vma=False
    )
```

```python
import functools
import math

import jax
import jax.numpy as jnp
from jax import lax
from jax.experimental import pallas as pl
from jax.experimental.pallas import tpu as pltpu
from jax.sharding import PartitionSpec as P

HEADS = 16
LANES = 128
MESH = pl.DeviceIdType.MESH
F32 = jnp.float32
BF16 = jnp.bfloat16


def dot_nn(x, y):
    return lax.dot_general(x, y, (((1,), (0,)), ((), ())), preferred_element_type=F32)


def dot_nt(x, y):
    return lax.dot_general(x, y, (((1,), (1,)), ((), ())), preferred_element_type=F32)


def dot_tn(x, y):
    return lax.dot_general(x, y, (((0,), (0,)), ((), ())), preferred_element_type=F32)


def kernel(
    n, nd, wscale,
    gf, nf, cot, wq_h, wkv_h, nbr, sr_col, sr_row,
    dgrid, dnodes, dwq, dwkv,
    wq, wkv, out_feat, tab, q_s, kv_s, count_s, gf_all, nf_all, dq_s, dq_all,
    part_s, ret_s, dkv_s, dkv_all, tq, tkv, rq, rkv, oq, okv, swq, swkv,
    local_sem, feat_ss, feat_rs, half_ss, half_rs, dq_ss, dq_rs, ret_ss, ret_rs,
    dkv_ss, dkv_rs, z_ss, z_rs, sw_ss, sw_rs,
):
    grid_dev, width = gf.shape
    nodes = nf.shape[0]
    slots = sr_col.shape[0]
    rows = slots + nodes
    cap = slots // n
    nbrs = nbr.shape[1]
    a = width // gf_all.shape[2]
    b = n // a
    high = width // a
    wide = width // b
    out_rows = dwq.shape[0]
    head = width // HEADS
    per = LANES // head
    scale = head ** (-0.5)
    me = lax.axis_index("mp")
    zd = lax.axis_index("dp")
    mine_i = me // b
    mine_j = lax.rem(me, b)

    def to_mp(src, dst, ssem, rsem, peer):
        return pltpu.make_async_remote_copy(
            src_ref=src, dst_ref=dst, send_sem=ssem, recv_sem=rsem,
            device_id={"mp": peer}, device_id_type=MESH,
        )

    def to_dp(src, dst, ssem, rsem, peer):
        return pltpu.make_async_remote_copy(
            src_ref=src, dst_ref=dst, send_sem=ssem, recv_sem=rsem,
            device_id={"dp": peer}, device_id_type=MESH,
        )

    def peer_of(o):
        return lax.rem(me + o, n)

    load_q = pltpu.make_async_copy(wq_h, wq, local_sem.at[0])
    load_kv = pltpu.make_async_copy(wkv_h, wkv, local_sem.at[1])
    load_q.start()
    load_kv.start()
    barrier = pltpu.get_barrier_semaphore()
    for o in range(1, n):
        pl.semaphore_signal(barrier, inc=1, device_id={"mp": peer_of(o)}, device_id_type=MESH)
    for o in range(1, nd):
        pl.semaphore_signal(
            barrier, inc=1, device_id={"dp": lax.rem(zd + o, nd)}, device_id_type=MESH
        )
    pick = (sr_col[...] == lax.broadcasted_iota(jnp.int32, (slots, nodes), 1)).astype(BF16)
    out_feat[...] = dot_nn(pick, nf[...]).astype(BF16)
    tab[pl.ds(slots, nodes), :] = nf[...]
    own_slots = pl.ds(pl.multiple_of(me * cap, cap), cap)
    tab[own_slots, :] = jnp.zeros((cap, width), BF16)
    for jb in range(b):
        ret_s[jb, own_slots, :] = jnp.zeros((cap, 2 * wide), BF16)
    pl.semaphore_wait(barrier, n - 1 + nd - 1)

    feat = []
    for o in range(1, n):
        there = pl.ds(pl.multiple_of(peer_of(o) * cap, cap), cap)
        feat.append(
            to_mp(out_feat.at[there], tab.at[own_slots], feat_ss.at[o], feat_rs.at[o], peer_of(o))
        )
        feat[-1].start()

    ids = nbr[...]
    row_id = lax.broadcasted_iota(jnp.int32, (grid_dev, rows), 1)
    count = jnp.zeros((grid_dev, rows), F32)
    for k in range(nbrs):
        count += (ids[:, k : k + 1] == row_id).astype(F32)
    for s in range(per):
        count_s[s * grid_dev : (s + 1) * grid_dev, :] = count
    half_cols = pl.ds(pl.multiple_of(mine_i * high, high), high)
    gf_all[me] = gf[:, half_cols]
    nf_all[me] = nf[:, half_cols]
    load_q.wait()
    q_s[...] = dot_nn(gf[...], wq[...]).astype(BF16)
    for c in feat:
        c.wait_recv()
    half = []
    for o in range(1, n):
        there = pl.ds(pl.multiple_of((peer_of(o) // b) * high, high), high)
        half.append(
            to_mp(nf.at[:, there], nf_all.at[me], half_ss.at[0, o], half_rs.at[0, o], peer_of(o))
        )
        half.append(
            to_mp(gf.at[:, there], gf_all.at[me], half_ss.at[1, o], half_rs.at[1, o], peer_of(o))
        )
    for c in half:
        c.start()
    load_kv.wait()
    kv_s[...] = dot_nn(tab[...], wkv[...]).astype(BF16)

    lane = lax.broadcasted_iota(jnp.int32, (1, LANES), 1)
    keep = [(lane // head) == s for s in range(per)]

    def spread(x):
        return jnp.concatenate([jnp.where(m, x, jnp.zeros_like(x)) for m in keep], axis=0)

    dq_copies = []
    ret_copies = []
    for jb in range(b):

        def one(blk, carry):
            off = pl.multiple_of(jb * wide + blk * LANES, LANES)
            at = pl.ds(off, LANES)
            at_v = pl.ds(pl.multiple_of(width + off, LANES), LANES)
            here = pl.ds(pl.multiple_of(blk * LANES, LANES), LANES)
            here_v = pl.ds(pl.multiple_of(wide + blk * LANES, LANES), LANES)
            qs = spread(q_s[:, at])
            cs = spread(cot[:, at])
            keys = kv_s[:, at]
            values = kv_s[:, at_v]
            times = count_s[...]
            scores = dot_nt(qs, keys) * scale
            d_attn = dot_nt(cs, values)
            top = jnp.max(
                jnp.where(times > 0, scores, -jnp.inf), axis=1, keepdims=True
            )
            e = jnp.where(times > 0, times * jnp.exp(jnp.minimum(scores - top, 0.0)), 0.0)
            attn = e / jnp.sum(e, axis=1, keepdims=True)
            ds = attn * (d_attn - jnp.sum(attn * d_attn, axis=1, keepdims=True)) * scale
            ds = ds.astype(BF16)
            attn = attn.astype(BF16)
            dq = None
            for s in range(per):
                term = dot_nn(
                    ds[s * grid_dev : (s + 1) * grid_dev],
                    jnp.where(keep[s], keys, jnp.zeros_like(keys)),
                )
                dq = term if dq is None else dq + term
            dq_s[jb, :, here] = dq.astype(BF16)
            part_s[jb, :, here] = dot_tn(ds, qs).astype(BF16)
            part_s[jb, :, here_v] = dot_tn(attn, cs).astype(BF16)
            return carry

        lax.fori_loop(0, wide // LANES, one, 0)
        for o in range(1, n):
            peer = peer_of(o)
            c = to_mp(dq_s.at[jb], dq_all.at[me], dq_ss.at[o], dq_rs.at[o], peer)

            @pl.when(lax.rem(peer, b) == jb)
            def _():
                c.start()

        for o in range(1, n):
            there = pl.ds(pl.multiple_of(peer_of(o) * cap, cap), cap)
            c = to_mp(
                part_s.at[jb, there], ret_s.at[jb, own_slots],
                ret_ss.at[jb, o], ret_rs.at[jb, o], peer_of(o),
            )
            c.start()
            ret_copies.append(c)

    dq_all[me] = dq_s[mine_j]
    acc = None
    for jb in range(b):
        term = dot_nt(dq_s[jb], wq[:, jb * wide : (jb + 1) * wide])
        acc = term if acc is None else acc + term
    dgrid[...] = acc.astype(BF16)

    place = (sr_row[...] == lax.broadcasted_iota(jnp.int32, (nodes, slots), 0)).astype(BF16)
    for jb in range(b):
        for o in range(1, n):
            ret_copies[jb * (n - 1) + o - 1].wait_recv()
        dkv = part_s[jb, slots:, :].astype(F32) + dot_nn(place, ret_s[jb])
        dkv_s[jb] = dkv.astype(BF16)
        for o in range(1, n):
            peer = peer_of(o)
            c = to_mp(dkv_s.at[jb], dkv_all.at[me], dkv_ss.at[o], dkv_rs.at[o], peer)

            @pl.when(lax.rem(peer, b) == jb)
            def _():
                c.start()

    dkv_all[me] = dkv_s[mine_j]

    def got(src, dst, ssem, rsem):
        return to_mp(src, dst, ssem, rsem, peer_of(1))

    for c in half:
        c.wait_recv()
    for o in range(1, n):
        got(dq_s.at[0], dq_all.at[me], dq_ss.at[o], dq_rs.at[o]).wait_recv()
    term_q = dot_tn(
        gf_all[...].reshape(n * grid_dev, high), dq_all[...].reshape(n * grid_dev, wide)
    ) * wscale
    term_q = term_q.astype(BF16).reshape(b, nd, out_rows, wide)
    for d in range(nd):
        tq[d] = term_q[:, d]
    z_copies = []
    for o in range(1, nd):
        peer = lax.rem(zd + o, nd)
        z_copies.append(to_dp(tq.at[peer], rq.at[o], z_ss.at[0, o], z_rs.at[0, o], peer))
        z_copies[-1].start()

    acc = None
    for jb in range(b):
        for k in range(2):
            term = dot_nt(
                dkv_s[jb, :, k * wide : (k + 1) * wide],
                wkv[:, k * width + jb * wide : k * width + (jb + 1) * wide],
            )
            acc = term if acc is None else acc + term
    dnodes[...] = acc.astype(BF16)

    for o in range(1, n):
        got(dkv_s.at[0], dkv_all.at[me], dkv_ss.at[o], dkv_rs.at[o]).wait_recv()
    term_kv = dot_tn(
        nf_all[...].reshape(n * nodes, high), dkv_all[...].reshape(n * nodes, 2 * wide)
    ) * wscale
    term_kv = term_kv.astype(BF16).reshape(b, nd, out_rows, 2 * wide)
    for d in range(nd):
        tkv[d] = term_kv[:, d]
    for o in range(1, nd):
        peer = lax.rem(zd + o, nd)
        z_copies.append(to_dp(tkv.at[peer], rkv.at[o], z_ss.at[1, o], z_rs.at[1, o], peer))
        z_copies[-1].start()

    def finish(which, t, r, out, sw, width_out):
        total = t[zd].astype(F32)
        for o in range(1, nd):
            z_copies[which * (nd - 1) + o - 1].wait_recv()
            total += r[o].astype(F32)
        out[...] = total.astype(BF16)
        sent = []
        for o in range(1, b):
            mate = lax.rem(mine_j + o, b)
            c = to_mp(
                out.at[mate], sw.at[o], sw_ss.at[which, o], sw_rs.at[which, o],
                mine_i * b + mate,
            )
            c.start()
            sent.append(c)
        return sent

    sent_q = finish(0, tq, rq, oq, swq, wide)
    sent_kv = finish(1, tkv, rkv, okv, swkv, 2 * wide)

    def columns(j, k):
        return pl.ds(pl.multiple_of(k * width + j * wide, LANES), wide)

    dwq[:, columns(mine_j, 0)] = oq[mine_j].astype(F32)
    for o in range(1, b):
        source = lax.rem(mine_j + b - o, b)
        sent_q[o - 1].wait_recv()
        dwq[:, columns(source, 0)] = swq[o].astype(F32)
    for k in range(2):
        dwkv[:, columns(mine_j, k)] = okv[mine_j][:, k * wide : (k + 1) * wide].astype(F32)
    for o in range(1, b):
        source = lax.rem(mine_j + b - o, b)
        sent_kv[o - 1].wait_recv()
        for k in range(2):
            dwkv[:, columns(source, k)] = swkv[o][:, k * wide : (k + 1) * wide].astype(F32)

    for c in feat + half + ret_copies + z_copies + sent_q + sent_kv:
        c.wait_send()
    for o in range(1, n):
        got(dq_s.at[0], dq_all.at[me], dq_ss.at[o], dq_rs.at[o]).wait_send()
        got(dkv_s.at[0], dkv_all.at[me], dkv_ss.at[o], dkv_rs.at[o]).wait_send()


def rows_apart(grid_feat, node_feat, cotangent, w_query, w_keyval, neighbours, send_rows):
    n = lax.axis_size("mp")
    nd = lax.axis_size("dp")
    samples_dev, grid_dev, width = grid_feat.shape
    nodes = node_feat.shape[1]
    cap = send_rows.shape[2]
    slots = n * cap
    rows = slots + nodes
    a = 2
    b = n // a
    high = width // a
    wide = width // b
    out_rows = width // (n * nd)
    per = LANES * HEADS // width
    wscale = 1.0 / math.sqrt(samples_dev * nd * grid_dev * n)
    vmem = pl.BlockSpec(memory_space=pltpu.VMEM)
    anywhere = pl.BlockSpec(memory_space=pl.ANY)
    dma = pltpu.SemaphoreType.DMA
    d_grid, d_nodes, dw_query, dw_keyval = pl.pallas_call(
        functools.partial(kernel, n, nd, wscale),
        out_shape=(
            jax.ShapeDtypeStruct((grid_dev, width), BF16),
            jax.ShapeDtypeStruct((nodes, width), BF16),
            jax.ShapeDtypeStruct((out_rows, width), F32),
            jax.ShapeDtypeStruct((out_rows, 2 * width), F32),
        ),
        in_specs=[vmem, vmem, vmem, anywhere, anywhere, vmem, vmem, vmem],
        out_specs=(vmem, vmem, vmem, vmem),
        scratch_shapes=[
            pltpu.VMEM((width, width), BF16),
            pltpu.VMEM((width, 2 * width), BF16),
            pltpu.VMEM((slots, width), BF16),
            pltpu.VMEM((rows, width), BF16),
            pltpu.VMEM((grid_dev, width), BF16),
            pltpu.VMEM((rows, 2 * width), BF16),
            pltpu.VMEM((per * grid_dev, rows), F32),
            pltpu.VMEM((n, grid_dev, high), BF16),
            pltpu.VMEM((n, nodes, high), BF16),
            pltpu.VMEM((b, grid_dev, wide), BF16),
            pltpu.VMEM((n, grid_dev, wide), BF16),
            pltpu.VMEM((b, rows, 2 * wide), BF16),
            pltpu.VMEM((b, slots, 2 * wide), BF16),
            pltpu.VMEM((b, nodes, 2 * wide), BF16),
            pltpu.VMEM((n, nodes, 2 * wide), BF16),
            pltpu.VMEM((nd, b, out_rows, wide), BF16),
            pltpu.VMEM((nd, b, out_rows, 2 * wide), BF16),
            pltpu.VMEM((nd, b, out_rows, wide), BF16),
            pltpu.VMEM((nd, b, out_rows, 2 * wide), BF16),
            pltpu.VMEM((b, out_rows, wide), BF16),
            pltpu.VMEM((b, out_rows, 2 * wide), BF16),
            pltpu.VMEM((b, out_rows, wide), BF16),
            pltpu.VMEM((b, out_rows, 2 * wide), BF16),
            dma((2,)),
            dma((n,)), dma((n,)),
            dma((2, n)), dma((2, n)),
            dma((n,)), dma((n,)),
            dma((b, n)), dma((b, n)),
            dma((n,)), dma((n,)),
            dma((2, nd)), dma((2, nd)),
            dma((2, b)), dma((2, b)),
        ],
        compiler_params=pltpu.CompilerParams(
            collective_id=0, has_side_effects=True, vmem_limit_bytes=56 * 1024 * 1024
        ),
        name="graph_attention_grads",
    )(
        grid_feat[0], node_feat[0], cotangent[0], w_query, w_keyval, neighbours,
        send_rows.reshape(slots, 1), send_rows.reshape(1, slots),
    )
    return d_grid[None], d_nodes[None], dw_query, dw_keyval


def heads_kernel(
    n, nd, wscale,
    gf_h, nf_h, cot_h, wq_h, wkv_h, nbr_h, sr_h,
    dgrid, dnodes, dwq, dwkv,
    wq, wkv, cot, own_term, nbr_t, sr, times_all, idx_all, nf_all, nf_part, gf_all, q_s, qc_all, kv_s, dkv_acc, dq_s, dq_rows,
    dkv_s, dkv_all, ret_kv, dkv_rows, fin_s, fin_q, tkv, fin_kv, *rest,
):
    steps = nd.bit_length() - 1
    halves, rest = rest[: steps], rest[steps:]
    gots, rest = rest[: steps], rest[steps:]
    (
        local_sem, idx_ss, idx_rs, nfy_ss, nfm_ss, nf_rs, part_ss, partm_ss, part_rs, partm_rs,
        cot_ss, q_ss, qc_rs, gfy_ss, gfm_ss, gf_rs, sc_ss, scy_ss, sc_rs, rq_ss, rq_rs,
        rkv_ss, rkv_rs, h_ss, h_rs, fq_ss, fq_rs, fk_ss, fk_rs,
    ) = rest
    grid_dev, width = gf_h.shape
    nodes = nf_h.shape[0]
    nbrs = nbr_t.shape[0]
    cap = sr.shape[1]
    slots = n * cap
    rows = slots + nodes
    all_nodes = n * nodes
    hc = width // n
    zc = 2 * hc // nd
    per_half = nd // 2
    out_rows = dwq.shape[0]
    head = width // HEADS
    per = LANES // head
    scale = head ** (-0.5)
    ny = n // 2
    wy = width // ny
    sr_at = idx_all.shape[1] - n
    me = lax.axis_index("mp")
    zd = lax.axis_index("dp")
    core = lax.rem(me, 2)
    chip = lax.div(me, 2)
    mate = me + 1 - 2 * core

    def place_of(m):
        return lax.rem(m, 2) * ny + lax.div(m, 2)

    mine = place_of(me)
    sent = []

    def send(src, dst, ssem, rsem, mp=None, dp=None, when=None):
        device = {}
        if mp is not None:
            device["mp"] = mp
        if dp is not None:
            device["dp"] = dp
        c = pltpu.make_async_remote_copy(
            src_ref=src, dst_ref=dst, send_sem=ssem, recv_sem=rsem,
            device_id=device, device_id_type=MESH,
        )
        if when is None:
            c.start()
        else:
            pl.when(when)(c.start)
        return c

    def left_here(block, ssem):
        pltpu.make_async_remote_copy(
            src_ref=block, dst_ref=block, send_sem=ssem, recv_sem=ssem,
            device_id={"mp": mate}, device_id_type=MESH,
        ).wait_send()

    def arrived(dst, rsem):
        pltpu.make_async_remote_copy(
            src_ref=dst, dst_ref=dst, send_sem=rsem, recv_sem=rsem,
            device_id={"mp": mate}, device_id_type=MESH,
        ).wait_recv()

    def peer_of(o):
        return lax.rem(me + o, n)

    barrier = pltpu.get_barrier_semaphore()
    for o in range(n):
        for k in range(nd):
            if o or k:
                pl.semaphore_signal(
                    barrier, inc=1,
                    device_id={"mp": peer_of(o), "dp": lax.rem(zd + k, nd)}, device_id_type=MESH,
                )
    own_cols = pl.ds(pl.multiple_of(me * hc, hc), hc)
    half_cols = pl.ds(pl.multiple_of(chip * wy, LANES), wy)

    def load(i, src, dst):
        c = pltpu.make_async_copy(src, dst, local_sem.at[i])
        c.start()
        return c

    load_nbr = load(0, nbr_h, nbr_t)
    load_sr = load(1, sr_h, sr)
    load_nf = load(2, nf_h, nf_all.at[mine])
    load_part = load(3, nf_h.at[:, half_cols], nf_part.at[zd, mine])
    load_gf = load(5, gf_h, gf_all.at[mine])
    load_q = load(6, wq_h, wq)
    load_cot = load(4, cot_h, cot)
    load_kv = load(7, wkv_h, wkv)

    load_nbr.wait()
    load_sr.wait()
    lane_slot = lax.broadcasted_iota(jnp.int32, (cap, rows), 1)
    tile = (lax.rem(lane_slot, cap) == lax.broadcasted_iota(jnp.int32, (cap, rows), 0)).astype(BF16)
    spread_rows = dot_nn(sr[...].astype(F32).astype(BF16), tile).astype(jnp.int32) + mine * nodes
    lane_row = lax.broadcasted_iota(jnp.int32, (n, rows), 1)
    own_lane = (lane_row >= me * cap) & (lane_row < me * cap + cap)
    idx_all[me] = jnp.zeros(idx_all.shape[1:], jnp.int32)
    idx_all[me, 0:nbrs, 0:grid_dev] = nbr_t[...]
    idx_all[me, sr_at : sr_at + n, 0:rows] = jnp.where(own_lane, spread_rows, 0)
    load_nf.wait()
    load_part.wait()
    pl.semaphore_wait(barrier, n * nd - 1)

    for o in range(1, n):
        send(idx_all.at[me], idx_all.at[me], idx_ss, idx_rs, mp=peer_of(o))

    has_right = zd + 1 < nd
    has_left = zd > 0

    def pass_on(sample, y, to_right, to_left, when):
        block = nf_part.at[sample, core * ny + y]
        rsem = part_rs.at[sample, y]
        for step, go, at in ((1, to_right, sample), (nd - 1, to_left, sample if when is not None else nd)):
            if go is not None:
                c = send(block, block, part_ss.at[at, y], rsem, dp=lax.rem(zd + step, nd), when=go)
                sent.append((c, go))
        if when is not None:
            send(block, block, partm_ss, partm_rs, mp=mate, when=when)

    for o in range(1, ny):
        there = lax.rem(chip + o, ny) * 2 + core
        send(nf_all.at[mine], nf_all.at[mine], nfy_ss, nf_rs.at[mine], mp=there)
    send(nf_all.at[mine], nf_all.at[mine], nfm_ss, nf_rs.at[mine], mp=mate)
    pass_on(zd, chip, has_right, has_left, None)
    readers = [lax.rem(chip + o, ny) * 2 + lax.rem(core + k, 2) for k in range(2) for o in range(ny)]
    readers = readers[1:ny] + [readers[ny]] + readers[ny + 1 :]

    def send_cot(i):
        there = readers[i]
        cols = pl.ds(pl.multiple_of(there * hc, hc), hc)
        send(cot.at[:, cols], qc_all.at[me, 1], cot_ss, qc_rs.at[me], mp=there)

    load_cot.wait()
    for i in range(ny):
        send_cot(i)
    qc_all[me, 1] = cot[:, own_cols]
    load_gf.wait()
    load_q.wait()
    query = dot_nn(gf_all[mine], wq[...]).astype(BF16)
    for k in range(n):
        q_s[k] = query[:, k * hc : (k + 1) * hc]
    for i in range(n - 1):
        there = readers[i]
        if i >= ny:
            send_cot(i)
        send(q_s.at[there], qc_all.at[me, 0], q_ss, qc_rs.at[me], mp=there)
    qc_all[me, 0] = q_s[me]
    for o in range(1, ny):
        there = lax.rem(chip + o, ny) * 2 + core
        send(gf_all.at[mine], gf_all.at[mine], gfy_ss, gf_rs.at[mine], mp=there)
    send(gf_all.at[mine], gf_all.at[mine], gfm_ss, gf_rs.at[mine], mp=mate)

    arrived(idx_all.at[0 : n - 1], idx_rs)
    plan = None
    for m in range(n):
        part = idx_all[m, sr_at : sr_at + n, 0:rows]
        plan = part if plan is None else plan + part
    own_rows = lax.broadcasted_iota(jnp.int32, (1, rows), 1)
    node_iota = lax.broadcasted_iota(jnp.int32, (all_nodes, rows), 0)
    row_iota = lax.broadcasted_iota(jnp.int32, (rows, grid_dev), 0)
    reader = lax.broadcasted_iota(jnp.int32, (n, rows), 0)

    def count_shard(d, carry):
        ids = idx_all[d, 0:nbrs, 0:grid_dev]
        count = jnp.zeros((rows, grid_dev), F32)
        for k in range(nbrs):
            count += (ids[k : k + 1, :] == row_iota).astype(F32)
        remote = jnp.sum(jnp.where(reader == d, plan, 0), axis=0, keepdims=True)
        target = jnp.where(own_rows < slots, remote, place_of(d) * nodes + own_rows - slots)
        named = (node_iota == target).astype(BF16)
        times_all[d] = dot_nn(named, count.astype(BF16))
        return carry

    lax.fori_loop(0, n, count_shard, 0)
    dkv_acc[...] = jnp.zeros_like(dkv_acc)
    def chain(o, k):
        y = lax.rem(chip + k, ny)
        from_left = zd >= o
        from_right = zd + o < nd
        left_sample = lax.rem(zd + nd - o, nd)
        right_sample = lax.rem(zd + o, nd)

        @pl.when(from_left)
        def _():
            arrived(nf_part.at[left_sample, core * ny + y], part_rs.at[left_sample, y])

        pass_on(left_sample, y, from_left & has_right, None, from_left)

        @pl.when(from_right)
        def _():
            arrived(nf_part.at[right_sample, core * ny + y], part_rs.at[right_sample, y])

        pass_on(right_sample, y, None, from_right & has_left, from_right)

    links = [(o, y) for o in range(1, nd) for y in range(ny)]
    links.sort(key=lambda link: 2 * link[0] + 3 * (link[1] > 0))

    def poll():
        if links:
            chain(*links.pop(0))

    poll()
    for o in range(1, ny):
        y = lax.rem(chip + ny - o, ny)
        p = core * ny + y
        arrived(nf_all.at[p], nf_rs.at[p])
        send(nf_all.at[p], nf_all.at[p], nfm_ss, nf_rs.at[p], mp=mate)
        nf_part[zd, p] = nf_all[p, :, half_cols]
        pass_on(zd, y, has_right, has_left, None)
    for o in range(ny):
        p = (1 - core) * ny + lax.rem(chip + o, ny)
        arrived(nf_all.at[p], nf_rs.at[p])
        nf_part[zd, p] = nf_all[p, :, half_cols]
    load_kv.wait()
    node_rows = nf_all[...].reshape(all_nodes, width)
    for k in range(2):
        cols = pl.ds(pl.multiple_of(k * width + me * hc, LANES), hc)
        kv_s[k] = dot_nn(node_rows, wkv[:, cols]).astype(BF16)
    lane = lax.broadcasted_iota(jnp.int32, (1, LANES), 1)
    keep = [(lane // head) == s for s in range(per)]

    def spread(x):
        return jnp.concatenate([jnp.where(m, x, jnp.zeros_like(x)) for m in keep], axis=0)

    def shard(d):
        times = times_all[d]
        times = jnp.concatenate([times] * per, axis=1)

        def pair(j, carry):
            at = pl.ds(pl.multiple_of(j * LANES, LANES), LANES)
            qs = spread(qc_all[d, 0, :, at])
            cs = spread(qc_all[d, 1, :, at])
            keys = kv_s[0, :, at]
            values = kv_s[1, :, at]
            scores = dot_nt(keys, qs) * scale
            d_attn = dot_nt(values, cs)
            scores = jnp.where(times > 0, scores, -jnp.inf)
            e = times * jnp.exp(scores - jnp.max(scores, axis=0, keepdims=True))
            attn = e * (1.0 / jnp.sum(e, axis=0, keepdims=True))
            ds = attn * (d_attn - jnp.sum(attn * d_attn, axis=0, keepdims=True)) * scale
            ds = ds.astype(BF16)
            attn = attn.astype(BF16)
            both = dot_tn(ds, keys)
            dq = both[:grid_dev]
            for s in range(1, per):
                dq = jnp.where(keep[s], both[s * grid_dev : (s + 1) * grid_dev], dq)
            dq_s[d, :, at] = dq.astype(BF16)
            dkv_acc[0, :, at] += dot_nn(ds, qs).astype(BF16).astype(F32)
            dkv_acc[1, :, at] += dot_nn(attn, cs).astype(BF16).astype(F32)
            return carry

        lax.fori_loop(0, hc // LANES, pair, 0, unroll=True)

    def await_shard(d):
        arrived(qc_all.at[d], qc_rs.at[d])

    shard(me)
    await_shard(mate)
    shard(mate)
    poll()
    poll()
    for o in range(1, ny):
        for k in range(2):
            d = lax.rem(chip + ny - o, ny) * 2 + lax.rem(core + k, 2)
            await_shard(d)
            shard(d)

    for k in range(nd):
        half, off = k // per_half, (k % per_half) * zc
        dkv_s[k] = dkv_acc[half, :, off : off + zc].astype(BF16)
    far_first = []
    for o in range(nd - 1, 0, -1):
        far_first.append((lax.rem(zd + nd - o, nd), zd >= o))
        far_first.append((lax.rem(zd + o, nd), zd + o < nd))
    for there, here in far_first:
        send(
            dkv_s.at[there], dkv_all.at[zd, chip], sc_ss, sc_rs.at[zd, chip],
            dp=there, when=here,
        )
    dkv_all[zd, chip] = dkv_s[zd]

    def across(sample, when):
        block = dkv_all.at[sample, chip]
        for o in range(1, ny):
            there = lax.rem(chip + o, ny) * 2 + core
            send(block, block, scy_ss, sc_rs.at[sample, chip], mp=there, when=when)

    def gather_across(o):
        for sample, here in ((lax.rem(zd + nd - o, nd), zd >= o), (lax.rem(zd + o, nd), zd + o < nd)):

            @pl.when(here)
            def _():
                arrived(dkv_all.at[sample, chip], sc_rs.at[sample, chip])

            across(sample, here)

    across(zd, None)
    for o in range(1, n):
        there = peer_of(o)
        send(dq_s.at[there], dq_rows.at[:, own_cols], rq_ss, rq_rs, mp=there)
    dq_rows[:, own_cols] = dq_s[me]
    ret_kv[me] = dkv_s[:, pl.ds(pl.multiple_of(mine * nodes, nodes), nodes)]

    targets = [peer_of(o + 1) for o in range(n)]
    theirs = (1 - core) * ny + chip
    arrived(gf_all.at[theirs], gf_rs.at[theirs])

    def query_term(t, chips):
        cols = pl.ds(pl.multiple_of(t * hc, LANES), hc)
        left = [gf_all[c * ny + y, :, cols] for y in chips for c in range(2)]
        right = [dq_s[y * 2 + c] for y in chips for c in range(2)]
        return dot_tn(jnp.concatenate(left, axis=0), jnp.concatenate(right, axis=0))

    for t in targets:
        own_term[t] = query_term(t, [chip])
    poll()
    for o in range(1, ny):
        p = core * ny + lax.rem(chip + ny - o, ny)
        arrived(gf_all.at[p], gf_rs.at[p])
        send(gf_all.at[p], gf_all.at[p], gfm_ss, gf_rs.at[p], mp=mate)
    poll()
    for o in range(1, ny):
        p = (1 - core) * ny + lax.rem(chip + o, ny)
        arrived(gf_all.at[p], gf_rs.at[p])

    bits = [lax.rem(lax.div(zd, 1 << b), 2) for b in range(steps)]
    mates = [zd + (1 << b) * (1 - 2 * bits[b]) for b in range(steps)]

    def give(b, t):
        send(
            halves[b].at[t, :, 1 - bits[b]], gots[b].at[t], h_ss.at[b], h_rs.at[b, t],
            dp=mates[b],
        )

    others = [lax.rem(chip + o, ny) for o in range(1, ny)]
    for t in targets:
        term = (own_term[t] + query_term(t, others)) * wscale
        halves[0][t] = term.astype(BF16).reshape(per_half, 2, out_rows, hc)
        give(0, t)

    def column(m, k):
        return (k // per_half) * width + m * hc + (k % per_half) * zc

    def halve(b, i):
        t = targets[i]
        arrived(gots[b].at[t], h_rs.at[b, t])
        total = halves[b][t, :, bits[b]].astype(F32) + gots[b][t].astype(F32)
        total = total.astype(BF16)
        if b + 1 < steps:
            halves[b + 1][t] = total.reshape(halves[b + 1].shape[1:])
            give(b + 1, t)
        elif i < n - 1:
            fin_s[t] = total.reshape(out_rows, hc)
            send(fin_s.at[t], fin_q.at[me], fq_ss, fq_rs, mp=t)
        else:
            fin_q[me] = total.reshape(out_rows, hc)

    for o in range(1, nd):
        gather_across(o)
        poll()
    while links:
        poll()
    def keyval_block(i, y):
        k = lax.rem(core + 1 + i, 2)
        cols = pl.ds(pl.multiple_of(k * hc, LANES), hc)
        term = dot_tn(
            nf_part[:, :, :, cols].reshape(nd * all_nodes, hc),
            dkv_all[:, y].reshape(nd * all_nodes, zc),
        ) * wscale
        tkv[k, y] = term.astype(BF16).reshape(nd, out_rows, zc)

        def block_to(there, when):
            send(
                tkv.at[k, y, there], fin_kv.at[core * nd + zd, y], fk_ss,
                fk_rs, mp=chip * 2 + k, dp=there, when=when,
            )

        for there, here in far_first:
            block_to(there, here)
        if i == 0:
            block_to(zd, None)
        else:
            fin_kv[core * nd + zd, y] = tkv[k, y, zd]

    arrived(nf_part.at[0 : nd - 1, 0:ny], partm_rs)
    keyval_block(0, chip)
    keyval_block(1, chip)
    for o in range(1, n):
        there = peer_of(o)
        node_block = pl.ds(pl.multiple_of(place_of(there) * nodes, nodes), nodes)
        send(dkv_s.at[:, node_block], ret_kv.at[me], rkv_ss, rkv_rs, mp=there)
    for i in range(n // 2):
        halve(0, i)
    arrived(dq_s.at[0 : n - 1], rq_rs)
    dgrid[...] = dot_nt(dq_rows[...], wq[...]).astype(BF16)
    for i in range(n // 2, n - 1):
        halve(0, i)
    for s in range(nd):
        for y in others:
            arrived(dkv_all.at[s, y], sc_rs.at[s, y])
    for i in range(2):
        for y in others:
            keyval_block(i, y)
    halve(0, n - 1)
    for b in range(1, steps - 1):
        for i in range(n):
            halve(b, i)
    for i in range(n // 2):
        halve(steps - 1, i)
    arrived(ret_kv.at[0 : n - 1], rkv_rs)
    for m in range(n):
        for k in range(nd):
            dkv_rows[:, column(m, k) : column(m, k) + zc] = ret_kv[m, k]
    dnodes[...] = dot_nt(dkv_rows[...], wkv[...]).astype(BF16)
    for i in range(n // 2, n):
        halve(steps - 1, i)

    arrived(fin_q.at[0 : n - 1], fq_rs)
    for m in range(n):
        dwq[:, m * hc : (m + 1) * hc] = fin_q[m].astype(F32)
    arrived(fin_kv.at[0 : 2 * nd - 1], fk_rs)
    for c in range(2):
        for k in range(nd):
            for y in range(ny):
                at = column(y * 2 + c, k)
                dwkv[:, at : at + zc] = fin_kv[c * nd + k, y].astype(F32)
    for c, when in sent:
        pl.when(when)(c.wait_send)
    left_here(idx_all.at[0 : n - 1], idx_ss)
    left_here(nf_all.at[0 : ny - 1], nfy_ss)
    left_here(nf_all.at[0:ny], nfm_ss)
    left_here(nf_part.at[0 : nd - 1, 0:ny], partm_ss)
    left_here(q_s.at[0 : n - 1], cot_ss)
    left_here(q_s.at[0 : n - 1], q_ss)
    left_here(gf_all.at[0 : ny - 1], gfy_ss)
    left_here(gf_all.at[0:ny], gfm_ss)
    left_here(dkv_s.at[0 : nd - 1], sc_ss)
    left_here(dkv_all.at[:, 0 : ny - 1], scy_ss)
    left_here(dq_s.at[0 : n - 1], rq_ss)
    left_here(ret_kv.at[0 : n - 1], rkv_ss)
    for b in range(steps):
        left_here(gots[b], h_ss.at[b])
    left_here(fin_s.at[0 : n - 1], fq_ss)
    left_here(fin_kv.at[0 : 2 * nd - 1], fk_ss)


def copy_kernel(*refs):
    for i in range(len(refs) // 2):
        refs[len(refs) // 2 + i][...] = refs[i][...]


def heads_apart(grid_feat, node_feat, cotangent, w_query, w_keyval, neighbours, send_rows):
    n = lax.axis_size("mp")
    nd = lax.axis_size("dp")
    grid_dev, width = grid_feat.shape[1:]
    nodes = node_feat.shape[1]
    nbrs = neighbours.shape[1]
    cap = send_rows.shape[2]
    rows = n * cap + nodes
    hc = width // n
    zc = 2 * hc // nd
    ny = n // 2
    steps = nd.bit_length() - 1
    out_rows = width // (n * nd)
    wscale = 1.0 / math.sqrt(nd * grid_dev * n)
    idx_rows = -(-nbrs // 8) * 8 + n
    idx_lanes = max(grid_dev, rows)
    vmem = pl.BlockSpec(memory_space=pltpu.VMEM)
    hbm = pl.BlockSpec(memory_space=pltpu.HBM)
    dma = pltpu.SemaphoreType.DMA
    one = dma(())
    outs = (
        jax.ShapeDtypeStruct((grid_dev, width), BF16),
        jax.ShapeDtypeStruct((nodes, width), BF16),
        jax.ShapeDtypeStruct((out_rows, width), F32),
        jax.ShapeDtypeStruct((out_rows, 2 * width), F32),
    )
    held = pl.pallas_call(
        functools.partial(heads_kernel, n, nd, wscale),
        out_shape=outs,
        in_specs=[hbm] * 7,
        out_specs=(vmem, vmem, vmem, vmem),
        scratch_shapes=[
            pltpu.VMEM((width, width), BF16),
            pltpu.VMEM((width, 2 * width), BF16),
            pltpu.VMEM((grid_dev, width), BF16),
            pltpu.VMEM((n, hc, hc), F32),
            pltpu.VMEM((nbrs, grid_dev), jnp.int32),
            pltpu.VMEM((n, cap), jnp.int32),
            pltpu.VMEM((n, n * nodes, grid_dev), F32),
            pltpu.VMEM((n, -(-idx_rows // 8) * 8, idx_lanes), jnp.int32),
            pltpu.VMEM((n, nodes, width), BF16),
            pltpu.VMEM((nd, n, nodes, width // ny), BF16),
            pltpu.VMEM((n, grid_dev, width), BF16),
            pltpu.VMEM((n, grid_dev, hc), BF16),
            pltpu.VMEM((n, 2, grid_dev, hc), BF16),
            pltpu.VMEM((2, n * nodes, hc), BF16),
            pltpu.VMEM((2, n * nodes, hc), F32),
            pltpu.VMEM((n, grid_dev, hc), BF16),
            pltpu.VMEM((grid_dev, width), BF16),
            pltpu.VMEM((nd, n * nodes, zc), BF16),
            pltpu.VMEM((nd, ny, n * nodes, zc), BF16),
            pltpu.VMEM((n, nd, nodes, zc), BF16),
            pltpu.VMEM((nodes, 2 * width), BF16),
            pltpu.VMEM((n, out_rows, hc), BF16),
            pltpu.VMEM((n, out_rows, hc), BF16),
            pltpu.VMEM((2, ny, nd, out_rows, zc), BF16),
            pltpu.VMEM((2 * nd, ny, out_rows, zc), BF16),
        ] + [
            pltpu.VMEM((n, nd >> (b + 1), 2, out_rows, hc), BF16) for b in range(steps)
        ] + [
            pltpu.VMEM((n, nd >> (b + 1), out_rows, hc), BF16) for b in range(steps)
        ] + [
            dma((8,)), one, one,
            one, one, dma((n,)),
            dma((nd + 1, ny)), one, dma((nd, ny)), one,
            one, one, dma((n,)),
            one, one, dma((n,)),
            one, one, dma((nd, ny)),
            one, one, one, one,
            dma((steps,)), dma((steps, n)),
            one, one, one, one,
        ],
        compiler_params=pltpu.CompilerParams(
            collective_id=0, has_side_effects=True, vmem_limit_bytes=28 * 1024 * 1024
        ),
        name="heads_apart_grads",
    )(*(
        pltpu.with_memory_space_constraint(x, pltpu.HBM)
        for x in (
            grid_feat[0], node_feat[0], cotangent[0], w_query, w_keyval,
            neighbours.T, send_rows[0],
        )
    ))
    d_grid, d_nodes, dw_query, dw_keyval = pl.pallas_call(
        copy_kernel, out_shape=outs, in_specs=[vmem] * 4, out_specs=(vmem,) * 4,
        compiler_params=pltpu.CompilerParams(vmem_limit_bytes=4 * 1024 * 1024),
        name="results",
    )(*held)
    return d_grid[None], d_nodes[None], dw_query, dw_keyval


def per_device(*args):
    n = lax.axis_size("mp")
    nd = lax.axis_size("dp")
    samples_dev, grid_dev, width = args[0].shape
    hc = width // n
    apart = (
        samples_dev == 1
        and n % 2 == 0
        and nd >= 4
        and nd & (nd - 1) == 0
        and hc % LANES == 0
        and 2 * hc % (nd * LANES) == 0
        and grid_dev % LANES == 0
        and width % (HEADS * n) == 0
        and LANES % (width // HEADS) == 0
        and width % (n * nd * 16) == 0
        and args[6].shape[2] * n <= 256
        and args[1].shape[1] * n <= 256
    )
    return heads_apart(*args) if apart else rows_apart(*args)


def solution(mesh):
    in_specs = (
        P(("groups", "dp"), "mp", None),
        P(("groups", "dp"), "mp", None),
        P(("groups", "dp"), "mp", None),
        P(),
        P(),
        P("mp", None),
        P("mp", None, None),
    )
    out_specs = (
        P(("groups", "dp"), "mp", None),
        P(("groups", "dp"), "mp", None),
        P(("groups", "mp", "dp"), None),
        P(("groups", "mp", "dp"), None),
    )
    return jax.shard_map(
        per_device, mesh=mesh, in_specs=in_specs, out_specs=out_specs, check_vma=False
    )
```

```python
import functools
import math

import jax
import jax.numpy as jnp
from jax import lax
from jax.experimental import pallas as pl
from jax.experimental.pallas import tpu as pltpu
from jax.sharding import PartitionSpec as P

HEADS = 16
LANES = 128
MESH = pl.DeviceIdType.MESH
F32 = jnp.float32
BF16 = jnp.bfloat16


def dot_nn(x, y):
    return lax.dot_general(x, y, (((1,), (0,)), ((), ())), preferred_element_type=F32)


def dot_nt(x, y):
    return lax.dot_general(x, y, (((1,), (1,)), ((), ())), preferred_element_type=F32)


def dot_tn(x, y):
    return lax.dot_general(x, y, (((0,), (0,)), ((), ())), preferred_element_type=F32)


def kernel(
    n, nd, wscale,
    gf, nf, cot, wq_h, wkv_h, nbr, sr_col, sr_row,
    dgrid, dnodes, dwq, dwkv,
    wq, wkv, out_feat, tab, q_s, kv_s, count_s, gf_all, nf_all, dq_s, dq_all,
    part_s, ret_s, dkv_s, dkv_all, tq, tkv, rq, rkv, oq, okv, swq, swkv,
    local_sem, feat_ss, feat_rs, half_ss, half_rs, dq_ss, dq_rs, ret_ss, ret_rs,
    dkv_ss, dkv_rs, z_ss, z_rs, sw_ss, sw_rs,
):
    grid_dev, width = gf.shape
    nodes = nf.shape[0]
    slots = sr_col.shape[0]
    rows = slots + nodes
    cap = slots // n
    nbrs = nbr.shape[1]
    a = width // gf_all.shape[2]
    b = n // a
    high = width // a
    wide = width // b
    out_rows = dwq.shape[0]
    head = width // HEADS
    per = LANES // head
    scale = head ** (-0.5)
    me = lax.axis_index("mp")
    zd = lax.axis_index("dp")
    mine_i = me // b
    mine_j = lax.rem(me, b)

    def to_mp(src, dst, ssem, rsem, peer):
        return pltpu.make_async_remote_copy(
            src_ref=src, dst_ref=dst, send_sem=ssem, recv_sem=rsem,
            device_id={"mp": peer}, device_id_type=MESH,
        )

    def to_dp(src, dst, ssem, rsem, peer):
        return pltpu.make_async_remote_copy(
            src_ref=src, dst_ref=dst, send_sem=ssem, recv_sem=rsem,
            device_id={"dp": peer}, device_id_type=MESH,
        )

    def peer_of(o):
        return lax.rem(me + o, n)

    load_q = pltpu.make_async_copy(wq_h, wq, local_sem.at[0])
    load_kv = pltpu.make_async_copy(wkv_h, wkv, local_sem.at[1])
    load_q.start()
    load_kv.start()
    barrier = pltpu.get_barrier_semaphore()
    for o in range(1, n):
        pl.semaphore_signal(barrier, inc=1, device_id={"mp": peer_of(o)}, device_id_type=MESH)
    for o in range(1, nd):
        pl.semaphore_signal(
            barrier, inc=1, device_id={"dp": lax.rem(zd + o, nd)}, device_id_type=MESH
        )
    pick = (sr_col[...] == lax.broadcasted_iota(jnp.int32, (slots, nodes), 1)).astype(BF16)
    out_feat[...] = dot_nn(pick, nf[...]).astype(BF16)
    tab[pl.ds(slots, nodes), :] = nf[...]
    own_slots = pl.ds(pl.multiple_of(me * cap, cap), cap)
    tab[own_slots, :] = jnp.zeros((cap, width), BF16)
    for jb in range(b):
        ret_s[jb, own_slots, :] = jnp.zeros((cap, 2 * wide), BF16)
    pl.semaphore_wait(barrier, n - 1 + nd - 1)

    feat = []
    for o in range(1, n):
        there = pl.ds(pl.multiple_of(peer_of(o) * cap, cap), cap)
        feat.append(
            to_mp(out_feat.at[there], tab.at[own_slots], feat_ss.at[o], feat_rs.at[o], peer_of(o))
        )
        feat[-1].start()

    ids = nbr[...]
    row_id = lax.broadcasted_iota(jnp.int32, (grid_dev, rows), 1)
    count = jnp.zeros((grid_dev, rows), F32)
    for k in range(nbrs):
        count += (ids[:, k : k + 1] == row_id).astype(F32)
    for s in range(per):
        count_s[s * grid_dev : (s + 1) * grid_dev, :] = count
    half_cols = pl.ds(pl.multiple_of(mine_i * high, high), high)
    gf_all[me] = gf[:, half_cols]
    nf_all[me] = nf[:, half_cols]
    load_q.wait()
    q_s[...] = dot_nn(gf[...], wq[...]).astype(BF16)
    for c in feat:
        c.wait_recv()
    half = []
    for o in range(1, n):
        there = pl.ds(pl.multiple_of((peer_of(o) // b) * high, high), high)
        half.append(
            to_mp(nf.at[:, there], nf_all.at[me], half_ss.at[0, o], half_rs.at[0, o], peer_of(o))
        )
        half.append(
            to_mp(gf.at[:, there], gf_all.at[me], half_ss.at[1, o], half_rs.at[1, o], peer_of(o))
        )
    for c in half:
        c.start()
    load_kv.wait()
    kv_s[...] = dot_nn(tab[...], wkv[...]).astype(BF16)

    lane = lax.broadcasted_iota(jnp.int32, (1, LANES), 1)
    keep = [(lane // head) == s for s in range(per)]

    def spread(x):
        return jnp.concatenate([jnp.where(m, x, jnp.zeros_like(x)) for m in keep], axis=0)

    dq_copies = []
    ret_copies = []
    for jb in range(b):

        def one(blk, carry):
            off = pl.multiple_of(jb * wide + blk * LANES, LANES)
            at = pl.ds(off, LANES)
            at_v = pl.ds(pl.multiple_of(width + off, LANES), LANES)
            here = pl.ds(pl.multiple_of(blk * LANES, LANES), LANES)
            here_v = pl.ds(pl.multiple_of(wide + blk * LANES, LANES), LANES)
            qs = spread(q_s[:, at])
            cs = spread(cot[:, at])
            keys = kv_s[:, at]
            values = kv_s[:, at_v]
            times = count_s[...]
            scores = dot_nt(qs, keys) * scale
            d_attn = dot_nt(cs, values)
            top = jnp.max(
                jnp.where(times > 0, scores, -jnp.inf), axis=1, keepdims=True
            )
            e = jnp.where(times > 0, times * jnp.exp(jnp.minimum(scores - top, 0.0)), 0.0)
            attn = e / jnp.sum(e, axis=1, keepdims=True)
            ds = attn * (d_attn - jnp.sum(attn * d_attn, axis=1, keepdims=True)) * scale
            ds = ds.astype(BF16)
            attn = attn.astype(BF16)
            dq = None
            for s in range(per):
                term = dot_nn(
                    ds[s * grid_dev : (s + 1) * grid_dev],
                    jnp.where(keep[s], keys, jnp.zeros_like(keys)),
                )
                dq = term if dq is None else dq + term
            dq_s[jb, :, here] = dq.astype(BF16)
            part_s[jb, :, here] = dot_tn(ds, qs).astype(BF16)
            part_s[jb, :, here_v] = dot_tn(attn, cs).astype(BF16)
            return carry

        lax.fori_loop(0, wide // LANES, one, 0)
        for o in range(1, n):
            peer = peer_of(o)
            c = to_mp(dq_s.at[jb], dq_all.at[me], dq_ss.at[o], dq_rs.at[o], peer)

            @pl.when(lax.rem(peer, b) == jb)
            def _():
                c.start()

        for o in range(1, n):
            there = pl.ds(pl.multiple_of(peer_of(o) * cap, cap), cap)
            c = to_mp(
                part_s.at[jb, there], ret_s.at[jb, own_slots],
                ret_ss.at[jb, o], ret_rs.at[jb, o], peer_of(o),
            )
            c.start()
            ret_copies.append(c)

    dq_all[me] = dq_s[mine_j]
    acc = None
    for jb in range(b):
        term = dot_nt(dq_s[jb], wq[:, jb * wide : (jb + 1) * wide])
        acc = term if acc is None else acc + term
    dgrid[...] = acc.astype(BF16)

    place = (sr_row[...] == lax.broadcasted_iota(jnp.int32, (nodes, slots), 0)).astype(BF16)
    for jb in range(b):
        for o in range(1, n):
            ret_copies[jb * (n - 1) + o - 1].wait_recv()
        dkv = part_s[jb, slots:, :].astype(F32) + dot_nn(place, ret_s[jb])
        dkv_s[jb] = dkv.astype(BF16)
        for o in range(1, n):
            peer = peer_of(o)
            c = to_mp(dkv_s.at[jb], dkv_all.at[me], dkv_ss.at[o], dkv_rs.at[o], peer)

            @pl.when(lax.rem(peer, b) == jb)
            def _():
                c.start()

    dkv_all[me] = dkv_s[mine_j]

    def got(src, dst, ssem, rsem):
        return to_mp(src, dst, ssem, rsem, peer_of(1))

    for c in half:
        c.wait_recv()
    for o in range(1, n):
        got(dq_s.at[0], dq_all.at[me], dq_ss.at[o], dq_rs.at[o]).wait_recv()
    term_q = dot_tn(
        gf_all[...].reshape(n * grid_dev, high), dq_all[...].reshape(n * grid_dev, wide)
    ) * wscale
    term_q = term_q.astype(BF16).reshape(b, nd, out_rows, wide)
    for d in range(nd):
        tq[d] = term_q[:, d]
    z_copies = []
    for o in range(1, nd):
        peer = lax.rem(zd + o, nd)
        z_copies.append(to_dp(tq.at[peer], rq.at[o], z_ss.at[0, o], z_rs.at[0, o], peer))
        z_copies[-1].start()

    acc = None
    for jb in range(b):
        for k in range(2):
            term = dot_nt(
                dkv_s[jb, :, k * wide : (k + 1) * wide],
                wkv[:, k * width + jb * wide : k * width + (jb + 1) * wide],
            )
            acc = term if acc is None else acc + term
    dnodes[...] = acc.astype(BF16)

    for o in range(1, n):
        got(dkv_s.at[0], dkv_all.at[me], dkv_ss.at[o], dkv_rs.at[o]).wait_recv()
    term_kv = dot_tn(
        nf_all[...].reshape(n * nodes, high), dkv_all[...].reshape(n * nodes, 2 * wide)
    ) * wscale
    term_kv = term_kv.astype(BF16).reshape(b, nd, out_rows, 2 * wide)
    for d in range(nd):
        tkv[d] = term_kv[:, d]
    for o in range(1, nd):
        peer = lax.rem(zd + o, nd)
        z_copies.append(to_dp(tkv.at[peer], rkv.at[o], z_ss.at[1, o], z_rs.at[1, o], peer))
        z_copies[-1].start()

    def finish(which, t, r, out, sw, width_out):
        total = t[zd].astype(F32)
        for o in range(1, nd):
            z_copies[which * (nd - 1) + o - 1].wait_recv()
            total += r[o].astype(F32)
        out[...] = total.astype(BF16)
        sent = []
        for o in range(1, b):
            mate = lax.rem(mine_j + o, b)
            c = to_mp(
                out.at[mate], sw.at[o], sw_ss.at[which, o], sw_rs.at[which, o],
                mine_i * b + mate,
            )
            c.start()
            sent.append(c)
        return sent

    sent_q = finish(0, tq, rq, oq, swq, wide)
    sent_kv = finish(1, tkv, rkv, okv, swkv, 2 * wide)

    def columns(j, k):
        return pl.ds(pl.multiple_of(k * width + j * wide, LANES), wide)

    dwq[:, columns(mine_j, 0)] = oq[mine_j].astype(F32)
    for o in range(1, b):
        source = lax.rem(mine_j + b - o, b)
        sent_q[o - 1].wait_recv()
        dwq[:, columns(source, 0)] = swq[o].astype(F32)
    for k in range(2):
        dwkv[:, columns(mine_j, k)] = okv[mine_j][:, k * wide : (k + 1) * wide].astype(F32)
    for o in range(1, b):
        source = lax.rem(mine_j + b - o, b)
        sent_kv[o - 1].wait_recv()
        for k in range(2):
            dwkv[:, columns(source, k)] = swkv[o][:, k * wide : (k + 1) * wide].astype(F32)

    for c in feat + half + ret_copies + z_copies + sent_q + sent_kv:
        c.wait_send()
    for o in range(1, n):
        got(dq_s.at[0], dq_all.at[me], dq_ss.at[o], dq_rs.at[o]).wait_send()
        got(dkv_s.at[0], dkv_all.at[me], dkv_ss.at[o], dkv_rs.at[o]).wait_send()


def rows_apart(grid_feat, node_feat, cotangent, w_query, w_keyval, neighbours, send_rows):
    n = lax.axis_size("mp")
    nd = lax.axis_size("dp")
    samples_dev, grid_dev, width = grid_feat.shape
    nodes = node_feat.shape[1]
    cap = send_rows.shape[2]
    slots = n * cap
    rows = slots + nodes
    a = 2
    b = n // a
    high = width // a
    wide = width // b
    out_rows = width // (n * nd)
    per = LANES * HEADS // width
    wscale = 1.0 / math.sqrt(samples_dev * nd * grid_dev * n)
    vmem = pl.BlockSpec(memory_space=pltpu.VMEM)
    anywhere = pl.BlockSpec(memory_space=pl.ANY)
    dma = pltpu.SemaphoreType.DMA
    d_grid, d_nodes, dw_query, dw_keyval = pl.pallas_call(
        functools.partial(kernel, n, nd, wscale),
        out_shape=(
            jax.ShapeDtypeStruct((grid_dev, width), BF16),
            jax.ShapeDtypeStruct((nodes, width), BF16),
            jax.ShapeDtypeStruct((out_rows, width), F32),
            jax.ShapeDtypeStruct((out_rows, 2 * width), F32),
        ),
        in_specs=[vmem, vmem, vmem, anywhere, anywhere, vmem, vmem, vmem],
        out_specs=(vmem, vmem, vmem, vmem),
        scratch_shapes=[
            pltpu.VMEM((width, width), BF16),
            pltpu.VMEM((width, 2 * width), BF16),
            pltpu.VMEM((slots, width), BF16),
            pltpu.VMEM((rows, width), BF16),
            pltpu.VMEM((grid_dev, width), BF16),
            pltpu.VMEM((rows, 2 * width), BF16),
            pltpu.VMEM((per * grid_dev, rows), F32),
            pltpu.VMEM((n, grid_dev, high), BF16),
            pltpu.VMEM((n, nodes, high), BF16),
            pltpu.VMEM((b, grid_dev, wide), BF16),
            pltpu.VMEM((n, grid_dev, wide), BF16),
            pltpu.VMEM((b, rows, 2 * wide), BF16),
            pltpu.VMEM((b, slots, 2 * wide), BF16),
            pltpu.VMEM((b, nodes, 2 * wide), BF16),
            pltpu.VMEM((n, nodes, 2 * wide), BF16),
            pltpu.VMEM((nd, b, out_rows, wide), BF16),
            pltpu.VMEM((nd, b, out_rows, 2 * wide), BF16),
            pltpu.VMEM((nd, b, out_rows, wide), BF16),
            pltpu.VMEM((nd, b, out_rows, 2 * wide), BF16),
            pltpu.VMEM((b, out_rows, wide), BF16),
            pltpu.VMEM((b, out_rows, 2 * wide), BF16),
            pltpu.VMEM((b, out_rows, wide), BF16),
            pltpu.VMEM((b, out_rows, 2 * wide), BF16),
            dma((2,)),
            dma((n,)), dma((n,)),
            dma((2, n)), dma((2, n)),
            dma((n,)), dma((n,)),
            dma((b, n)), dma((b, n)),
            dma((n,)), dma((n,)),
            dma((2, nd)), dma((2, nd)),
            dma((2, b)), dma((2, b)),
        ],
        compiler_params=pltpu.CompilerParams(
            collective_id=0, has_side_effects=True, vmem_limit_bytes=56 * 1024 * 1024
        ),
        name="graph_attention_grads",
    )(
        grid_feat[0], node_feat[0], cotangent[0], w_query, w_keyval, neighbours,
        send_rows.reshape(slots, 1), send_rows.reshape(1, slots),
    )
    return d_grid[None], d_nodes[None], dw_query, dw_keyval


def heads_kernel(
    n, nd, wscale,
    gf_h, nf_h, cot_h, wq_h, wkv_h, nbr_h, sr_h,
    dgrid, dnodes, dwq, dwkv,
    wq, wkv, cot, own_term, nbr_t, sr, times_all, idx_all, nf_all, nf_sel, nf_part, gf_all, q_s, qc_all, kv_s, keys_t, dkv_acc, dq_s, dq_rows,
    dkv_s, dkv_all, ret_kv, dkv_rows, fin_s, fin_q, tkv, fin_kv, *rest,
):
    steps = nd.bit_length() - 1
    halves, rest = rest[: steps], rest[steps:]
    gots, rest = rest[: steps], rest[steps:]
    (
        local_sem, idx_ss, idx_rs, nfy_ss, nfm_ss, nf_rs, part_ss, partm_ss, part_rs, partm_rs,
        cot_ss, q_ss, qc_rs, gfy_ss, gfm_ss, gf_rs, sc_ss, sc_rs, rq_ss, rq_rs,
        rkv_ss, rkv_rs, h_ss, h_rs, fq_ss, fq_rs, fk_ss, fk_rs,
    ) = rest
    grid_dev, width = gf_h.shape
    nodes = nf_h.shape[0]
    nbrs = nbr_t.shape[0]
    cap = sr.shape[1]
    slots = n * cap
    rows = slots + nodes
    all_nodes = n * nodes
    hc = width // n
    side_len = nd // 2
    zc = 2 * hc // side_len
    per_half = side_len // 2
    side_rows = hc // 2
    out_rows = dwq.shape[0]
    head = width // HEADS
    per = LANES // head
    scale = head ** (-0.5)
    ny = n // 2
    sr_at = idx_all.shape[1] - n
    me = lax.axis_index("mp")
    zd = lax.axis_index("dp")
    core = lax.rem(me, 2)
    chip = lax.div(me, 2)
    mate = me + 1 - 2 * core

    def place_of(m):
        return lax.rem(m, 2) * ny + lax.div(m, 2)

    mine = place_of(me)
    side = lax.div(zd, side_len)
    in_side = lax.rem(zd, side_len)
    def send(src, dst, ssem, rsem, mp=None, dp=None, when=None):
        device = {}
        if mp is not None:
            device["mp"] = mp
        if dp is not None:
            device["dp"] = dp
        c = pltpu.make_async_remote_copy(
            src_ref=src, dst_ref=dst, send_sem=ssem, recv_sem=rsem,
            device_id=device, device_id_type=MESH,
        )
        if when is None:
            c.start()
        else:
            pl.when(when)(c.start)
        return c

    def left_here(block, ssem):
        pltpu.make_async_remote_copy(
            src_ref=block, dst_ref=block, send_sem=ssem, recv_sem=ssem,
            device_id={"mp": mate}, device_id_type=MESH,
        ).wait_send()

    def arrived(dst, rsem):
        pltpu.make_async_remote_copy(
            src_ref=dst, dst_ref=dst, send_sem=rsem, recv_sem=rsem,
            device_id={"mp": mate}, device_id_type=MESH,
        ).wait_recv()

    def peer_of(o):
        return lax.rem(me + o, n)

    barrier = pltpu.get_barrier_semaphore()
    for o in range(n):
        for k in range(nd):
            if o or k:
                pl.semaphore_signal(
                    barrier, inc=1,
                    device_id={"mp": peer_of(o), "dp": lax.rem(zd + k, nd)}, device_id_type=MESH,
                )
    own_cols = pl.ds(pl.multiple_of(me * hc, hc), hc)

    def load(i, src, dst):
        c = pltpu.make_async_copy(src, dst, local_sem.at[i])
        c.start()
        return c

    load_nbr = load(0, nbr_h, nbr_t)
    load_sr = load(1, sr_h, sr)
    load_nf = load(2, nf_h, nf_all.at[mine])
    load_gf = load(5, gf_h, gf_all.at[mine])
    load_q = load(6, wq_h, wq)
    load_cot = load(4, cot_h, cot)
    load_kv = load(7, wkv_h, wkv)

    load_nbr.wait()
    load_sr.wait()
    lane_slot = lax.broadcasted_iota(jnp.int32, (cap, rows), 1)
    tile = (lax.rem(lane_slot, cap) == lax.broadcasted_iota(jnp.int32, (cap, rows), 0)).astype(BF16)
    spread_rows = dot_nn(sr[...].astype(F32).astype(BF16), tile).astype(jnp.int32) + mine * nodes
    lane_row = lax.broadcasted_iota(jnp.int32, (n, rows), 1)
    own_lane = (lane_row >= me * cap) & (lane_row < me * cap + cap)
    idx_all[me] = jnp.zeros(idx_all.shape[1:], jnp.int32)
    idx_all[me, 0:nbrs, 0:grid_dev] = nbr_t[...]
    idx_all[me, sr_at : sr_at + n, 0:rows] = jnp.where(own_lane, spread_rows, 0)
    load_nf.wait()

    def own_sample(y):
        p = core * ny + y
        for h in range(2):
            for m in range(n):
                at = m * hc + h * side_rows
                nf_sel[h, y, :, m * side_rows : (m + 1) * side_rows] = nf_all[p, :, at : at + side_rows]
        nf_part[zd, p] = nf_sel[side, y]

    own_sample(chip)
    pl.semaphore_wait(barrier, n * nd - 1)

    for o in range(1, n):
        send(idx_all.at[me], idx_all.at[me], idx_ss, idx_rs, mp=peer_of(o))

    def send_sample(y):
        for o in range(1, nd):
            there = lax.rem(zd + o, nd)
            send(
                nf_sel.at[lax.div(there, side_len), y], nf_part.at[zd, core * ny + y], part_ss,
                part_rs.at[zd, y], dp=there,
            )

    for o in range(1, ny):
        there = lax.rem(chip + o, ny) * 2 + core
        send(nf_all.at[mine], nf_all.at[mine], nfy_ss, nf_rs.at[mine], mp=there)
    send(nf_all.at[mine], nf_all.at[mine], nfm_ss, nf_rs.at[mine], mp=mate)
    send_sample(chip)
    readers = [lax.rem(chip + o, ny) * 2 + lax.rem(core + k, 2) for k in range(2) for o in range(ny)]
    readers = readers[1:ny] + [readers[ny]] + readers[ny + 1 :]

    def send_cot(i):
        there = readers[i]
        cols = pl.ds(pl.multiple_of(there * hc, hc), hc)
        send(cot.at[:, cols], qc_all.at[me, 1], cot_ss, qc_rs.at[me], mp=there)

    load_cot.wait()
    for i in range(ny):
        send_cot(i)
    qc_all[me, 1] = cot[:, own_cols]
    load_gf.wait()
    load_q.wait()
    query = dot_nn(gf_all[mine], wq[...]).astype(BF16)
    for k in range(n):
        q_s[k] = query[:, k * hc : (k + 1) * hc]
    for i in range(n - 1):
        there = readers[i]
        if i >= ny:
            send_cot(i)
        send(q_s.at[there], qc_all.at[me, 0], q_ss, qc_rs.at[me], mp=there)
    qc_all[me, 0] = q_s[me]
    for o in range(1, ny):
        there = lax.rem(chip + o, ny) * 2 + core
        send(gf_all.at[mine], gf_all.at[mine], gfy_ss, gf_rs.at[mine], mp=there)
    send(gf_all.at[mine], gf_all.at[mine], gfm_ss, gf_rs.at[mine], mp=mate)

    arrived(idx_all.at[0 : n - 1], idx_rs)
    plan = None
    for m in range(n):
        part = idx_all[m, sr_at : sr_at + n, 0:rows]
        plan = part if plan is None else plan + part
    own_rows = lax.broadcasted_iota(jnp.int32, (1, rows), 1)
    node_iota = lax.broadcasted_iota(jnp.int32, (all_nodes, rows), 0)
    row_iota = lax.broadcasted_iota(jnp.int32, (rows, grid_dev), 0)
    reader = lax.broadcasted_iota(jnp.int32, (n, rows), 0)

    def count_shard(d, carry):
        ids = idx_all[d, 0:nbrs, 0:grid_dev]
        count = jnp.zeros((rows, grid_dev), F32)
        for k in range(nbrs):
            count += (ids[k : k + 1, :] == row_iota).astype(F32)
        remote = jnp.sum(jnp.where(reader == d, plan, 0), axis=0, keepdims=True)
        target = jnp.where(own_rows < slots, remote, place_of(d) * nodes + own_rows - slots)
        named = (node_iota == target).astype(BF16)
        times_all[d] = jnp.log2(dot_nn(named, count.astype(BF16)))
        return carry

    lax.fori_loop(0, n, count_shard, 0)
    dkv_acc[...] = jnp.zeros_like(dkv_acc)
    for o in range(1, ny):
        y = lax.rem(chip + ny - o, ny)
        p = core * ny + y
        arrived(nf_all.at[p], nf_rs.at[p])
        send(nf_all.at[p], nf_all.at[p], nfm_ss, nf_rs.at[p], mp=mate)
        own_sample(y)
        send_sample(y)
    for o in range(ny):
        p = (1 - core) * ny + lax.rem(chip + o, ny)
        arrived(nf_all.at[p], nf_rs.at[p])
        for m in range(n):
            at = pl.ds(pl.multiple_of(m * hc + side * side_rows, LANES), side_rows)
            nf_part[zd, p, :, m * side_rows : (m + 1) * side_rows] = nf_all[p, :, at]
    load_kv.wait()
    node_rows = nf_all[...].reshape(all_nodes, width)
    for k in range(2):
        cols = pl.ds(pl.multiple_of(k * width + me * hc, LANES), hc)
        kv_s[k] = dot_nn(node_rows, wkv[:, cols]).astype(BF16)
    for j in range(hc // LANES):
        keys_t[j] = kv_s[0, :, j * LANES : (j + 1) * LANES].T
    lane = lax.broadcasted_iota(jnp.int32, (1, LANES), 1)
    keep = [(lane // head) == s for s in range(per)]

    def spread(x):
        return jnp.concatenate([jnp.where(m, x, jnp.zeros_like(x)) for m in keep], axis=0)

    def shard(d):
        times = times_all[d]
        times = jnp.concatenate([times] * per, axis=1)

        def pair(j, carry):
            at = pl.ds(pl.multiple_of(j * LANES, LANES), LANES)
            qs = spread(qc_all[d, 0, :, at])
            cs = spread(qc_all[d, 1, :, at])
            keys = kv_s[0, :, at]
            values = kv_s[1, :, at]
            scores = dot_nt(keys, qs) * (scale * math.log2(math.e)) + times
            d_attn = dot_nt(values, cs)
            e = jnp.exp2(scores - jnp.max(scores, axis=0, keepdims=True))
            attn = e * (1.0 / jnp.sum(e, axis=0, keepdims=True))
            ds = attn * (d_attn - jnp.sum(attn * d_attn, axis=0, keepdims=True)) * scale
            ds = ds.astype(BF16)
            attn = attn.astype(BF16)
            both = dot_nn(keys_t[j], ds).astype(BF16)
            dq = jnp.concatenate(
                [
                    both[s * head : (s + 1) * head, s * grid_dev : (s + 1) * grid_dev]
                    for s in range(per)
                ],
                axis=0,
            )
            dq_s[d, :, at] = dq.T
            dkv_acc[0, :, at] += dot_nn(ds, qs).astype(BF16).astype(F32)
            dkv_acc[1, :, at] += dot_nn(attn, cs).astype(BF16).astype(F32)
            return carry

        lax.fori_loop(0, hc // LANES, pair, 0, unroll=True)

    def await_shard(d):
        arrived(qc_all.at[d], qc_rs.at[d])

    shard(me)
    await_shard(mate)
    shard(mate)
    for o in range(1, ny):
        for k in range(2):
            d = lax.rem(chip + ny - o, ny) * 2 + lax.rem(core + k, 2)
            await_shard(d)
            shard(d)

    for k in range(side_len):
        half, off = k // per_half, (k % per_half) * zc
        dkv_s[k] = dkv_acc[half, :, off : off + zc].astype(BF16)
    inward = 1 - 2 * lax.div(zd, nd // 2)
    far_first = []
    for o in range(nd - 1, 0, -1):
        for there in (zd + inward * o, zd - inward * o):
            far_first.append((lax.rem(there + nd, nd), (there >= 0) & (there < nd)))
    for there, here in far_first:
        send(
            dkv_s.at[lax.rem(there, side_len)], dkv_all.at[zd], sc_ss, sc_rs.at[zd],
            dp=there, when=here,
        )
    dkv_all[zd] = dkv_s[in_side]

    for o in range(1, n):
        there = peer_of(o)
        send(dq_s.at[there], dq_rows.at[:, own_cols], rq_ss, rq_rs, mp=there)
    dq_rows[:, own_cols] = dq_s[me]
    ret_kv[me] = dkv_s[:, pl.ds(pl.multiple_of(mine * nodes, nodes), nodes)]

    for o in range(1, nd):
        sample = lax.rem(zd + o, nd)
        for y in range(ny):
            block = nf_part.at[sample, core * ny + y]
            arrived(block, part_rs.at[sample, y])
            send(block, block, partm_ss, partm_rs, mp=mate)

    targets = [peer_of(o + 1) for o in range(n)]
    theirs = (1 - core) * ny + chip
    arrived(gf_all.at[theirs], gf_rs.at[theirs])

    def query_term(t, chips):
        cols = pl.ds(pl.multiple_of(t * hc, LANES), hc)
        left = [gf_all[c * ny + y, :, cols] for y in chips for c in range(2)]
        right = [dq_s[y * 2 + c] for y in chips for c in range(2)]
        return dot_tn(jnp.concatenate(left, axis=0), jnp.concatenate(right, axis=0))

    for t in targets:
        own_term[t] = query_term(t, [chip])
    for o in range(1, ny):
        p = core * ny + lax.rem(chip + ny - o, ny)
        arrived(gf_all.at[p], gf_rs.at[p])
        send(gf_all.at[p], gf_all.at[p], gfm_ss, gf_rs.at[p], mp=mate)
    for o in range(1, ny):
        p = (1 - core) * ny + lax.rem(chip + o, ny)
        arrived(gf_all.at[p], gf_rs.at[p])

    bits = [lax.rem(lax.div(zd, 1 << b), 2) for b in range(steps)]
    mates = [zd + (1 << b) * (1 - 2 * bits[b]) for b in range(steps)]

    def give(b, t):
        send(
            halves[b].at[t, :, 1 - bits[b]], gots[b].at[t], h_ss.at[b], h_rs.at[b, t],
            dp=mates[b],
        )

    others = [lax.rem(chip + o, ny) for o in range(1, ny)]
    for t in targets:
        term = (own_term[t] + query_term(t, others)) * wscale
        halves[0][t] = term.astype(BF16).reshape(side_len, 2, out_rows, hc)
        give(0, t)

    def column(m, k):
        return (k // per_half) * width + m * hc + (k % per_half) * zc

    def halve(b, i):
        t = targets[i]
        arrived(gots[b].at[t], h_rs.at[b, t])
        total = halves[b][t, :, bits[b]].astype(F32) + gots[b][t].astype(F32)
        total = total.astype(BF16)
        if b + 1 < steps:
            halves[b + 1][t] = total.reshape(halves[b + 1].shape[1:])
            give(b + 1, t)
        elif i < n - 1:
            fin_s[t] = total.reshape(out_rows, hc)
            send(fin_s.at[t], fin_q.at[me], fq_ss, fq_rs, mp=t)
        else:
            fin_q[me] = total.reshape(out_rows, hc)

    for o in range(1, n):
        there = peer_of(o)
        node_block = pl.ds(pl.multiple_of(place_of(there) * nodes, nodes), nodes)
        send(dkv_s.at[:, node_block], ret_kv.at[me], rkv_ss, rkv_rs, mp=there)
    arrived(dq_s.at[0 : n - 1], rq_rs)
    dgrid[...] = dot_nt(dq_rows[...], wq[...]).astype(BF16)
    for i in range(n - 1):
        halve(0, i)
    arrived(nf_part.at[0 : nd - 1, 0:ny], partm_rs)
    for o in range(1, nd):
        sample = lax.rem(zd + o, nd)
        arrived(dkv_all.at[sample], sc_rs.at[sample])
    term = dot_tn(
        nf_part[...].reshape(nd * all_nodes, n * side_rows), dkv_all[...].reshape(nd * all_nodes, zc)
    ) * wscale
    tkv[...] = term.astype(BF16).reshape(n, side_len, out_rows, zc)
    own_slot = me * side_len + in_side

    def send_rows_of(o, k):
        to_m, to = peer_of(o), lax.rem(in_side + k, side_len)
        send(
            tkv.at[to_m, to], fin_kv.at[own_slot], fk_ss, fk_rs, mp=to_m, dp=side * side_len + to
        )

    for o in range(1, n):
        send_rows_of(o, 0)
    halve(0, n - 1)
    for k in range(1, side_len):
        for o in range(n):
            send_rows_of(o, k)
    fin_kv[own_slot] = tkv[me, in_side]
    arrived(ret_kv.at[0 : n - 1], rkv_rs)
    for m in range(n):
        for k in range(side_len):
            dkv_rows[:, column(m, k) : column(m, k) + zc] = ret_kv[m, k]
    dnodes[...] = dot_nt(dkv_rows[...], wkv[...]).astype(BF16)
    for b in range(1, steps):
        for i in range(n):
            halve(b, i)

    arrived(fin_q.at[0 : n - 1], fq_rs)
    for m in range(n):
        dwq[:, m * hc : (m + 1) * hc] = fin_q[m].astype(F32)
    arrived(fin_kv.at[0 : n * side_len - 1], fk_rs)
    for m in range(n):
        for k in range(side_len):
            dwkv[:, column(m, k) : column(m, k) + zc] = fin_kv[m * side_len + k].astype(F32)
    left_here(nf_part.at[0 : nd - 1, 0:ny], part_ss)
    left_here(idx_all.at[0 : n - 1], idx_ss)
    left_here(nf_all.at[0 : ny - 1], nfy_ss)
    left_here(nf_all.at[0:ny], nfm_ss)
    left_here(nf_part.at[0 : nd - 1, 0:ny], partm_ss)
    left_here(q_s.at[0 : n - 1], cot_ss)
    left_here(q_s.at[0 : n - 1], q_ss)
    left_here(gf_all.at[0 : ny - 1], gfy_ss)
    left_here(gf_all.at[0:ny], gfm_ss)
    left_here(dkv_all.at[0 : nd - 1], sc_ss)
    left_here(dq_s.at[0 : n - 1], rq_ss)
    left_here(ret_kv.at[0 : n - 1], rkv_ss)
    for b in range(steps):
        left_here(gots[b], h_ss.at[b])
    left_here(fin_s.at[0 : n - 1], fq_ss)
    left_here(fin_kv.at[0 : n * side_len - 1], fk_ss)


def copy_kernel(*refs):
    for i in range(len(refs) // 2):
        refs[len(refs) // 2 + i][...] = refs[i][...]


def heads_apart(grid_feat, node_feat, cotangent, w_query, w_keyval, neighbours, send_rows):
    n = lax.axis_size("mp")
    nd = lax.axis_size("dp")
    grid_dev, width = grid_feat.shape[1:]
    nodes = node_feat.shape[1]
    nbrs = neighbours.shape[1]
    cap = send_rows.shape[2]
    rows = n * cap + nodes
    hc = width // n
    side_len = nd // 2
    zc = 2 * hc // side_len
    ny = n // 2
    steps = nd.bit_length() - 1
    out_rows = width // (n * nd)
    wscale = 1.0 / math.sqrt(nd * grid_dev * n)
    idx_rows = nbrs + n
    idx_lanes = max(grid_dev, rows)
    vmem = pl.BlockSpec(memory_space=pltpu.VMEM)
    hbm = pl.BlockSpec(memory_space=pltpu.HBM)
    dma = pltpu.SemaphoreType.DMA
    one = dma(())
    outs = (
        jax.ShapeDtypeStruct((grid_dev, width), BF16),
        jax.ShapeDtypeStruct((nodes, width), BF16),
        jax.ShapeDtypeStruct((out_rows, width), F32),
        jax.ShapeDtypeStruct((out_rows, 2 * width), F32),
    )
    held = pl.pallas_call(
        functools.partial(heads_kernel, n, nd, wscale),
        out_shape=outs,
        in_specs=[hbm] * 7,
        out_specs=(vmem, vmem, vmem, vmem),
        scratch_shapes=[
            pltpu.VMEM((width, width), BF16),
            pltpu.VMEM((width, 2 * width), BF16),
            pltpu.VMEM((grid_dev, width), BF16),
            pltpu.VMEM((n, hc, hc), F32),
            pltpu.VMEM((nbrs, grid_dev), jnp.int32),
            pltpu.VMEM((n, cap), jnp.int32),
            pltpu.VMEM((n, n * nodes, grid_dev), F32),
            pltpu.VMEM((n, -(-idx_rows // 8) * 8, idx_lanes), jnp.int32),
            pltpu.VMEM((n, nodes, width), BF16),
            pltpu.VMEM((2, ny, nodes, width // 2), BF16),
            pltpu.VMEM((nd, n, nodes, width // 2), BF16),
            pltpu.VMEM((n, grid_dev, width), BF16),
            pltpu.VMEM((n, grid_dev, hc), BF16),
            pltpu.VMEM((n, 2, grid_dev, hc), BF16),
            pltpu.VMEM((2, n * nodes, hc), BF16),
            pltpu.VMEM((hc // LANES, LANES, n * nodes), BF16),
            pltpu.VMEM((2, n * nodes, hc), F32),
            pltpu.VMEM((n, grid_dev, hc), BF16),
            pltpu.VMEM((grid_dev, width), BF16),
            pltpu.VMEM((side_len, n * nodes, zc), BF16),
            pltpu.VMEM((nd, n * nodes, zc), BF16),
            pltpu.VMEM((n, side_len, nodes, zc), BF16),
            pltpu.VMEM((nodes, 2 * width), BF16),
            pltpu.VMEM((n, out_rows, hc), BF16),
            pltpu.VMEM((n, out_rows, hc), BF16),
            pltpu.VMEM((n, side_len, out_rows, zc), BF16),
            pltpu.VMEM((n * side_len, out_rows, zc), BF16),
        ] + [
            pltpu.VMEM((n, nd >> (b + 1), 2, out_rows, hc), BF16) for b in range(steps)
        ] + [
            pltpu.VMEM((n, nd >> (b + 1), out_rows, hc), BF16) for b in range(steps)
        ] + [
            dma((8,)), one, one,
            one, one, dma((n,)),
            one, one, dma((nd, ny)), one,
            one, one, dma((n,)),
            one, one, dma((n,)),
            one, dma((nd,)),
            one, one, one, one,
            dma((steps,)), dma((steps, n)),
            one, one, one, one,
        ],
        compiler_params=pltpu.CompilerParams(
            collective_id=0, has_side_effects=True, vmem_limit_bytes=28 * 1024 * 1024
        ),
        name="heads_apart_grads",
    )(*(
        pltpu.with_memory_space_constraint(x, pltpu.HBM)
        for x in (
            grid_feat[0], node_feat[0], cotangent[0], w_query, w_keyval,
            neighbours.T, send_rows[0],
        )
    ))
    d_grid, d_nodes, dw_query, dw_keyval = pl.pallas_call(
        copy_kernel, out_shape=outs, in_specs=[vmem] * 4, out_specs=(vmem,) * 4,
        compiler_params=pltpu.CompilerParams(vmem_limit_bytes=4 * 1024 * 1024),
        name="results",
    )(*held)
    return d_grid[None], d_nodes[None], dw_query, dw_keyval


def per_device(*args):
    n = lax.axis_size("mp")
    nd = lax.axis_size("dp")
    samples_dev, grid_dev, width = args[0].shape
    hc = width // n
    apart = (
        samples_dev == 1
        and n % 2 == 0
        and nd >= 4
        and nd & (nd - 1) == 0
        and hc % LANES == 0
        and 4 * hc % (nd * LANES) == 0
        and hc % (2 * LANES) == 0
        and grid_dev % LANES == 0
        and width % (HEADS * n) == 0
        and LANES % (width // HEADS) == 0
        and width % (n * nd * 16) == 0
        and args[6].shape[2] * n <= 256
        and args[1].shape[1] * n <= 256
    )
    return heads_apart(*args) if apart else rows_apart(*args)


def solution(mesh):
    in_specs = (
        P(("groups", "dp"), "mp", None),
        P(("groups", "dp"), "mp", None),
        P(("groups", "dp"), "mp", None),
        P(),
        P(),
        P("mp", None),
        P("mp", None, None),
    )
    out_specs = (
        P(("groups", "dp"), "mp", None),
        P(("groups", "dp"), "mp", None),
        P(("groups", "mp", "dp"), None),
        P(("groups", "mp", "dp"), None),
    )
    return jax.shard_map(
        per_device, mesh=mesh, in_specs=in_specs, out_specs=out_specs, check_vma=False
    )
```

```python
import functools
import math

import jax
import jax.numpy as jnp
from jax import lax
from jax.experimental import pallas as pl
from jax.experimental.pallas import tpu as pltpu
from jax.sharding import PartitionSpec as P

HEADS = 16
LANES = 128
MESH = pl.DeviceIdType.MESH
F32 = jnp.float32
BF16 = jnp.bfloat16


def dot_nn(x, y):
    return lax.dot_general(x, y, (((1,), (0,)), ((), ())), preferred_element_type=F32)


def dot_nt(x, y):
    return lax.dot_general(x, y, (((1,), (1,)), ((), ())), preferred_element_type=F32)


def dot_tn(x, y):
    return lax.dot_general(x, y, (((0,), (0,)), ((), ())), preferred_element_type=F32)


def kernel(
    n, nd, wscale,
    gf, nf, cot, wq_h, wkv_h, nbr, sr_col, sr_row,
    dgrid, dnodes, dwq, dwkv,
    wq, wkv, out_feat, tab, q_s, kv_s, count_s, gf_all, nf_all, dq_s, dq_all,
    part_s, ret_s, dkv_s, dkv_all, tq, tkv, rq, rkv, oq, okv, swq, swkv,
    local_sem, feat_ss, feat_rs, half_ss, half_rs, dq_ss, dq_rs, ret_ss, ret_rs,
    dkv_ss, dkv_rs, z_ss, z_rs, sw_ss, sw_rs,
):
    grid_dev, width = gf.shape
    nodes = nf.shape[0]
    slots = sr_col.shape[0]
    rows = slots + nodes
    cap = slots // n
    nbrs = nbr.shape[1]
    a = width // gf_all.shape[2]
    b = n // a
    high = width // a
    wide = width // b
    out_rows = dwq.shape[0]
    head = width // HEADS
    per = LANES // head
    scale = head ** (-0.5)
    me = lax.axis_index("mp")
    zd = lax.axis_index("dp")
    mine_i = me // b
    mine_j = lax.rem(me, b)

    def to_mp(src, dst, ssem, rsem, peer):
        return pltpu.make_async_remote_copy(
            src_ref=src, dst_ref=dst, send_sem=ssem, recv_sem=rsem,
            device_id={"mp": peer}, device_id_type=MESH,
        )

    def to_dp(src, dst, ssem, rsem, peer):
        return pltpu.make_async_remote_copy(
            src_ref=src, dst_ref=dst, send_sem=ssem, recv_sem=rsem,
            device_id={"dp": peer}, device_id_type=MESH,
        )

    def peer_of(o):
        return lax.rem(me + o, n)

    load_q = pltpu.make_async_copy(wq_h, wq, local_sem.at[0])
    load_kv = pltpu.make_async_copy(wkv_h, wkv, local_sem.at[1])
    load_q.start()
    load_kv.start()
    barrier = pltpu.get_barrier_semaphore()
    for o in range(1, n):
        pl.semaphore_signal(barrier, inc=1, device_id={"mp": peer_of(o)}, device_id_type=MESH)
    for o in range(1, nd):
        pl.semaphore_signal(
            barrier, inc=1, device_id={"dp": lax.rem(zd + o, nd)}, device_id_type=MESH
        )
    pick = (sr_col[...] == lax.broadcasted_iota(jnp.int32, (slots, nodes), 1)).astype(BF16)
    out_feat[...] = dot_nn(pick, nf[...]).astype(BF16)
    tab[pl.ds(slots, nodes), :] = nf[...]
    own_slots = pl.ds(pl.multiple_of(me * cap, cap), cap)
    tab[own_slots, :] = jnp.zeros((cap, width), BF16)
    for jb in range(b):
        ret_s[jb, own_slots, :] = jnp.zeros((cap, 2 * wide), BF16)
    pl.semaphore_wait(barrier, n - 1 + nd - 1)

    feat = []
    for o in range(1, n):
        there = pl.ds(pl.multiple_of(peer_of(o) * cap, cap), cap)
        feat.append(
            to_mp(out_feat.at[there], tab.at[own_slots], feat_ss.at[o], feat_rs.at[o], peer_of(o))
        )
        feat[-1].start()

    ids = nbr[...]
    row_id = lax.broadcasted_iota(jnp.int32, (grid_dev, rows), 1)
    count = jnp.zeros((grid_dev, rows), F32)
    for k in range(nbrs):
        count += (ids[:, k : k + 1] == row_id).astype(F32)
    for s in range(per):
        count_s[s * grid_dev : (s + 1) * grid_dev, :] = count
    half_cols = pl.ds(pl.multiple_of(mine_i * high, high), high)
    gf_all[me] = gf[:, half_cols]
    nf_all[me] = nf[:, half_cols]
    load_q.wait()
    q_s[...] = dot_nn(gf[...], wq[...]).astype(BF16)
    for c in feat:
        c.wait_recv()
    half = []
    for o in range(1, n):
        there = pl.ds(pl.multiple_of((peer_of(o) // b) * high, high), high)
        half.append(
            to_mp(nf.at[:, there], nf_all.at[me], half_ss.at[0, o], half_rs.at[0, o], peer_of(o))
        )
        half.append(
            to_mp(gf.at[:, there], gf_all.at[me], half_ss.at[1, o], half_rs.at[1, o], peer_of(o))
        )
    for c in half:
        c.start()
    load_kv.wait()
    kv_s[...] = dot_nn(tab[...], wkv[...]).astype(BF16)

    lane = lax.broadcasted_iota(jnp.int32, (1, LANES), 1)
    keep = [(lane // head) == s for s in range(per)]

    def spread(x):
        return jnp.concatenate([jnp.where(m, x, jnp.zeros_like(x)) for m in keep], axis=0)

    dq_copies = []
    ret_copies = []
    for jb in range(b):

        def one(blk, carry):
            off = pl.multiple_of(jb * wide + blk * LANES, LANES)
            at = pl.ds(off, LANES)
            at_v = pl.ds(pl.multiple_of(width + off, LANES), LANES)
            here = pl.ds(pl.multiple_of(blk * LANES, LANES), LANES)
            here_v = pl.ds(pl.multiple_of(wide + blk * LANES, LANES), LANES)
            qs = spread(q_s[:, at])
            cs = spread(cot[:, at])
            keys = kv_s[:, at]
            values = kv_s[:, at_v]
            times = count_s[...]
            scores = dot_nt(qs, keys) * scale
            d_attn = dot_nt(cs, values)
            top = jnp.max(
                jnp.where(times > 0, scores, -jnp.inf), axis=1, keepdims=True
            )
            e = jnp.where(times > 0, times * jnp.exp(jnp.minimum(scores - top, 0.0)), 0.0)
            attn = e / jnp.sum(e, axis=1, keepdims=True)
            ds = attn * (d_attn - jnp.sum(attn * d_attn, axis=1, keepdims=True)) * scale
            ds = ds.astype(BF16)
            attn = attn.astype(BF16)
            dq = None
            for s in range(per):
                term = dot_nn(
                    ds[s * grid_dev : (s + 1) * grid_dev],
                    jnp.where(keep[s], keys, jnp.zeros_like(keys)),
                )
                dq = term if dq is None else dq + term
            dq_s[jb, :, here] = dq.astype(BF16)
            part_s[jb, :, here] = dot_tn(ds, qs).astype(BF16)
            part_s[jb, :, here_v] = dot_tn(attn, cs).astype(BF16)
            return carry

        lax.fori_loop(0, wide // LANES, one, 0)
        for o in range(1, n):
            peer = peer_of(o)
            c = to_mp(dq_s.at[jb], dq_all.at[me], dq_ss.at[o], dq_rs.at[o], peer)

            @pl.when(lax.rem(peer, b) == jb)
            def _():
                c.start()

        for o in range(1, n):
            there = pl.ds(pl.multiple_of(peer_of(o) * cap, cap), cap)
            c = to_mp(
                part_s.at[jb, there], ret_s.at[jb, own_slots],
                ret_ss.at[jb, o], ret_rs.at[jb, o], peer_of(o),
            )
            c.start()
            ret_copies.append(c)

    dq_all[me] = dq_s[mine_j]
    acc = None
    for jb in range(b):
        term = dot_nt(dq_s[jb], wq[:, jb * wide : (jb + 1) * wide])
        acc = term if acc is None else acc + term
    dgrid[...] = acc.astype(BF16)

    place = (sr_row[...] == lax.broadcasted_iota(jnp.int32, (nodes, slots), 0)).astype(BF16)
    for jb in range(b):
        for o in range(1, n):
            ret_copies[jb * (n - 1) + o - 1].wait_recv()
        dkv = part_s[jb, slots:, :].astype(F32) + dot_nn(place, ret_s[jb])
        dkv_s[jb] = dkv.astype(BF16)
        for o in range(1, n):
            peer = peer_of(o)
            c = to_mp(dkv_s.at[jb], dkv_all.at[me], dkv_ss.at[o], dkv_rs.at[o], peer)

            @pl.when(lax.rem(peer, b) == jb)
            def _():
                c.start()

    dkv_all[me] = dkv_s[mine_j]

    def got(src, dst, ssem, rsem):
        return to_mp(src, dst, ssem, rsem, peer_of(1))

    for c in half:
        c.wait_recv()
    for o in range(1, n):
        got(dq_s.at[0], dq_all.at[me], dq_ss.at[o], dq_rs.at[o]).wait_recv()
    term_q = dot_tn(
        gf_all[...].reshape(n * grid_dev, high), dq_all[...].reshape(n * grid_dev, wide)
    ) * wscale
    term_q = term_q.astype(BF16).reshape(b, nd, out_rows, wide)
    for d in range(nd):
        tq[d] = term_q[:, d]
    z_copies = []
    for o in range(1, nd):
        peer = lax.rem(zd + o, nd)
        z_copies.append(to_dp(tq.at[peer], rq.at[o], z_ss.at[0, o], z_rs.at[0, o], peer))
        z_copies[-1].start()

    acc = None
    for jb in range(b):
        for k in range(2):
            term = dot_nt(
                dkv_s[jb, :, k * wide : (k + 1) * wide],
                wkv[:, k * width + jb * wide : k * width + (jb + 1) * wide],
            )
            acc = term if acc is None else acc + term
    dnodes[...] = acc.astype(BF16)

    for o in range(1, n):
        got(dkv_s.at[0], dkv_all.at[me], dkv_ss.at[o], dkv_rs.at[o]).wait_recv()
    term_kv = dot_tn(
        nf_all[...].reshape(n * nodes, high), dkv_all[...].reshape(n * nodes, 2 * wide)
    ) * wscale
    term_kv = term_kv.astype(BF16).reshape(b, nd, out_rows, 2 * wide)
    for d in range(nd):
        tkv[d] = term_kv[:, d]
    for o in range(1, nd):
        peer = lax.rem(zd + o, nd)
        z_copies.append(to_dp(tkv.at[peer], rkv.at[o], z_ss.at[1, o], z_rs.at[1, o], peer))
        z_copies[-1].start()

    def finish(which, t, r, out, sw, width_out):
        total = t[zd].astype(F32)
        for o in range(1, nd):
            z_copies[which * (nd - 1) + o - 1].wait_recv()
            total += r[o].astype(F32)
        out[...] = total.astype(BF16)
        sent = []
        for o in range(1, b):
            mate = lax.rem(mine_j + o, b)
            c = to_mp(
                out.at[mate], sw.at[o], sw_ss.at[which, o], sw_rs.at[which, o],
                mine_i * b + mate,
            )
            c.start()
            sent.append(c)
        return sent

    sent_q = finish(0, tq, rq, oq, swq, wide)
    sent_kv = finish(1, tkv, rkv, okv, swkv, 2 * wide)

    def columns(j, k):
        return pl.ds(pl.multiple_of(k * width + j * wide, LANES), wide)

    dwq[:, columns(mine_j, 0)] = oq[mine_j].astype(F32)
    for o in range(1, b):
        source = lax.rem(mine_j + b - o, b)
        sent_q[o - 1].wait_recv()
        dwq[:, columns(source, 0)] = swq[o].astype(F32)
    for k in range(2):
        dwkv[:, columns(mine_j, k)] = okv[mine_j][:, k * wide : (k + 1) * wide].astype(F32)
    for o in range(1, b):
        source = lax.rem(mine_j + b - o, b)
        sent_kv[o - 1].wait_recv()
        for k in range(2):
            dwkv[:, columns(source, k)] = swkv[o][:, k * wide : (k + 1) * wide].astype(F32)

    for c in feat + half + ret_copies + z_copies + sent_q + sent_kv:
        c.wait_send()
    for o in range(1, n):
        got(dq_s.at[0], dq_all.at[me], dq_ss.at[o], dq_rs.at[o]).wait_send()
        got(dkv_s.at[0], dkv_all.at[me], dkv_ss.at[o], dkv_rs.at[o]).wait_send()


def rows_apart(grid_feat, node_feat, cotangent, w_query, w_keyval, neighbours, send_rows):
    n = lax.axis_size("mp")
    nd = lax.axis_size("dp")
    samples_dev, grid_dev, width = grid_feat.shape
    nodes = node_feat.shape[1]
    cap = send_rows.shape[2]
    slots = n * cap
    rows = slots + nodes
    a = 2
    b = n // a
    high = width // a
    wide = width // b
    out_rows = width // (n * nd)
    per = LANES * HEADS // width
    wscale = 1.0 / math.sqrt(samples_dev * nd * grid_dev * n)
    vmem = pl.BlockSpec(memory_space=pltpu.VMEM)
    anywhere = pl.BlockSpec(memory_space=pl.ANY)
    dma = pltpu.SemaphoreType.DMA
    d_grid, d_nodes, dw_query, dw_keyval = pl.pallas_call(
        functools.partial(kernel, n, nd, wscale),
        out_shape=(
            jax.ShapeDtypeStruct((grid_dev, width), BF16),
            jax.ShapeDtypeStruct((nodes, width), BF16),
            jax.ShapeDtypeStruct((out_rows, width), F32),
            jax.ShapeDtypeStruct((out_rows, 2 * width), F32),
        ),
        in_specs=[vmem, vmem, vmem, anywhere, anywhere, vmem, vmem, vmem],
        out_specs=(vmem, vmem, vmem, vmem),
        scratch_shapes=[
            pltpu.VMEM((width, width), BF16),
            pltpu.VMEM((width, 2 * width), BF16),
            pltpu.VMEM((slots, width), BF16),
            pltpu.VMEM((rows, width), BF16),
            pltpu.VMEM((grid_dev, width), BF16),
            pltpu.VMEM((rows, 2 * width), BF16),
            pltpu.VMEM((per * grid_dev, rows), F32),
            pltpu.VMEM((n, grid_dev, high), BF16),
            pltpu.VMEM((n, nodes, high), BF16),
            pltpu.VMEM((b, grid_dev, wide), BF16),
            pltpu.VMEM((n, grid_dev, wide), BF16),
            pltpu.VMEM((b, rows, 2 * wide), BF16),
            pltpu.VMEM((b, slots, 2 * wide), BF16),
            pltpu.VMEM((b, nodes, 2 * wide), BF16),
            pltpu.VMEM((n, nodes, 2 * wide), BF16),
            pltpu.VMEM((nd, b, out_rows, wide), BF16),
            pltpu.VMEM((nd, b, out_rows, 2 * wide), BF16),
            pltpu.VMEM((nd, b, out_rows, wide), BF16),
            pltpu.VMEM((nd, b, out_rows, 2 * wide), BF16),
            pltpu.VMEM((b, out_rows, wide), BF16),
            pltpu.VMEM((b, out_rows, 2 * wide), BF16),
            pltpu.VMEM((b, out_rows, wide), BF16),
            pltpu.VMEM((b, out_rows, 2 * wide), BF16),
            dma((2,)),
            dma((n,)), dma((n,)),
            dma((2, n)), dma((2, n)),
            dma((n,)), dma((n,)),
            dma((b, n)), dma((b, n)),
            dma((n,)), dma((n,)),
            dma((2, nd)), dma((2, nd)),
            dma((2, b)), dma((2, b)),
        ],
        compiler_params=pltpu.CompilerParams(
            collective_id=0, has_side_effects=True, vmem_limit_bytes=56 * 1024 * 1024
        ),
        name="graph_attention_grads",
    )(
        grid_feat[0], node_feat[0], cotangent[0], w_query, w_keyval, neighbours,
        send_rows.reshape(slots, 1), send_rows.reshape(1, slots),
    )
    return d_grid[None], d_nodes[None], dw_query, dw_keyval


def heads_kernel(
    n, nd, wscale,
    gf_h, nf_h, cot_h, wq_h, wkv_h, nbr_h, sr_h,
    dgrid, dnodes, dwq, dwkv,
    wq, wkv, cot, own_term, nbr_t, sr, times_all, idx_all, nf_all, nf_part, gf_all, q_s, qc_all, kv_s, keys_t, dkv_acc, dq_s, dq_rows,
    dkv_s, dkv_all, ret_kv, dkv_rows, fin_s, fin_q, tkv, fin_kv, *rest,
):
    steps = nd.bit_length() - 1
    halves, rest = rest[: steps], rest[steps:]
    gots, rest = rest[: steps], rest[steps:]
    (
        local_sem, idx_ss, idx_rs, nfy_ss, nfm_ss, nf_rs, part_ss, partm_ss, part_rs, partm_rs,
        cot_ss, q_ss, qc_rs, gfy_ss, gfm_ss, gf_rs, sc_ss, scy_ss, sc_rs, rq_ss, rq_rs,
        rkv_ss, rkv_rs, h_ss, h_rs, fq_ss, fq_rs, fk_ss, fk_rs,
    ) = rest
    grid_dev, width = gf_h.shape
    nodes = nf_h.shape[0]
    nbrs = nbr_t.shape[0]
    cap = sr.shape[1]
    slots = n * cap
    rows = slots + nodes
    all_nodes = n * nodes
    hc = width // n
    zc = 2 * hc // nd
    per_half = nd // 2
    out_rows = dwq.shape[0]
    head = width // HEADS
    per = LANES // head
    scale = head ** (-0.5)
    ny = n // 2
    wy = width // ny
    sr_at = idx_all.shape[1] - n
    me = lax.axis_index("mp")
    zd = lax.axis_index("dp")
    core = lax.rem(me, 2)
    chip = lax.div(me, 2)
    mate = me + 1 - 2 * core

    def place_of(m):
        return lax.rem(m, 2) * ny + lax.div(m, 2)

    mine = place_of(me)
    sent = []

    def send(src, dst, ssem, rsem, mp=None, dp=None, when=None):
        device = {}
        if mp is not None:
            device["mp"] = mp
        if dp is not None:
            device["dp"] = dp
        c = pltpu.make_async_remote_copy(
            src_ref=src, dst_ref=dst, send_sem=ssem, recv_sem=rsem,
            device_id=device, device_id_type=MESH,
        )
        if when is None:
            c.start()
        else:
            pl.when(when)(c.start)
        return c

    def left_here(block, ssem):
        pltpu.make_async_remote_copy(
            src_ref=block, dst_ref=block, send_sem=ssem, recv_sem=ssem,
            device_id={"mp": mate}, device_id_type=MESH,
        ).wait_send()

    def arrived(dst, rsem):
        pltpu.make_async_remote_copy(
            src_ref=dst, dst_ref=dst, send_sem=rsem, recv_sem=rsem,
            device_id={"mp": mate}, device_id_type=MESH,
        ).wait_recv()

    def peer_of(o):
        return lax.rem(me + o, n)

    barrier = pltpu.get_barrier_semaphore()
    for o in range(n):
        for k in range(nd):
            if o or k:
                pl.semaphore_signal(
                    barrier, inc=1,
                    device_id={"mp": peer_of(o), "dp": lax.rem(zd + k, nd)}, device_id_type=MESH,
                )
    own_cols = pl.ds(pl.multiple_of(me * hc, hc), hc)
    half_cols = pl.ds(pl.multiple_of(chip * wy, LANES), wy)

    def load(i, src, dst):
        c = pltpu.make_async_copy(src, dst, local_sem.at[i])
        c.start()
        return c

    load_nbr = load(0, nbr_h, nbr_t)
    load_sr = load(1, sr_h, sr)
    load_nf = load(2, nf_h, nf_all.at[mine])
    load_part = load(3, nf_h.at[:, half_cols], nf_part.at[zd, mine])
    load_gf = load(5, gf_h, gf_all.at[mine])
    load_q = load(6, wq_h, wq)
    load_cot = load(4, cot_h, cot)
    load_kv = load(7, wkv_h, wkv)

    load_nbr.wait()
    load_sr.wait()
    lane_slot = lax.broadcasted_iota(jnp.int32, (cap, rows), 1)
    tile = (lax.rem(lane_slot, cap) == lax.broadcasted_iota(jnp.int32, (cap, rows), 0)).astype(BF16)
    spread_rows = dot_nn(sr[...].astype(F32).astype(BF16), tile).astype(jnp.int32) + mine * nodes
    lane_row = lax.broadcasted_iota(jnp.int32, (n, rows), 1)
    own_lane = (lane_row >= me * cap) & (lane_row < me * cap + cap)
    idx_all[me] = jnp.zeros(idx_all.shape[1:], jnp.int32)
    idx_all[me, 0:nbrs, 0:grid_dev] = nbr_t[...]
    idx_all[me, sr_at : sr_at + n, 0:rows] = jnp.where(own_lane, spread_rows, 0)
    load_nf.wait()
    load_part.wait()
    pl.semaphore_wait(barrier, n * nd - 1)

    for o in range(1, n):
        send(idx_all.at[me], idx_all.at[me], idx_ss, idx_rs, mp=peer_of(o))

    has_right = zd + 1 < nd
    has_left = zd > 0

    def pass_on(sample, y, to_right, to_left, when):
        block = nf_part.at[sample, core * ny + y]
        rsem = part_rs.at[sample, y]
        for step, go, at in ((1, to_right, sample), (nd - 1, to_left, sample if when is not None else nd)):
            if go is not None:
                c = send(block, block, part_ss.at[at, y], rsem, dp=lax.rem(zd + step, nd), when=go)
                sent.append((c, go))
        if when is not None:
            send(block, block, partm_ss, partm_rs, mp=mate, when=when)

    for o in range(1, ny):
        there = lax.rem(chip + o, ny) * 2 + core
        send(nf_all.at[mine], nf_all.at[mine], nfy_ss, nf_rs.at[mine], mp=there)
    send(nf_all.at[mine], nf_all.at[mine], nfm_ss, nf_rs.at[mine], mp=mate)
    pass_on(zd, chip, has_right, has_left, None)
    readers = [lax.rem(chip + o, ny) * 2 + lax.rem(core + k, 2) for k in range(2) for o in range(ny)]
    readers = readers[1:ny] + [readers[ny]] + readers[ny + 1 :]

    def send_cot(i):
        there = readers[i]
        cols = pl.ds(pl.multiple_of(there * hc, hc), hc)
        send(cot.at[:, cols], qc_all.at[me, 1], cot_ss, qc_rs.at[me], mp=there)

    load_cot.wait()
    for i in range(ny):
        send_cot(i)
    qc_all[me, 1] = cot[:, own_cols]
    load_gf.wait()
    load_q.wait()
    query = dot_nn(gf_all[mine], wq[...]).astype(BF16)
    for k in range(n):
        q_s[k] = query[:, k * hc : (k + 1) * hc]
    for i in range(n - 1):
        there = readers[i]
        if i >= ny:
            send_cot(i)
        send(q_s.at[there], qc_all.at[me, 0], q_ss, qc_rs.at[me], mp=there)
    qc_all[me, 0] = q_s[me]
    for o in range(1, ny):
        there = lax.rem(chip + o, ny) * 2 + core
        send(gf_all.at[mine], gf_all.at[mine], gfy_ss, gf_rs.at[mine], mp=there)
    send(gf_all.at[mine], gf_all.at[mine], gfm_ss, gf_rs.at[mine], mp=mate)

    arrived(idx_all.at[0 : n - 1], idx_rs)
    plan = None
    for m in range(n):
        part = idx_all[m, sr_at : sr_at + n, 0:rows]
        plan = part if plan is None else plan + part
    own_rows = lax.broadcasted_iota(jnp.int32, (1, rows), 1)
    node_iota = lax.broadcasted_iota(jnp.int32, (all_nodes, rows), 0)
    row_iota = lax.broadcasted_iota(jnp.int32, (rows, grid_dev), 0)
    reader = lax.broadcasted_iota(jnp.int32, (n, rows), 0)

    def count_shard(d, carry):
        ids = idx_all[d, 0:nbrs, 0:grid_dev]
        count = jnp.zeros((rows, grid_dev), F32)
        for k in range(nbrs):
            count += (ids[k : k + 1, :] == row_iota).astype(F32)
        remote = jnp.sum(jnp.where(reader == d, plan, 0), axis=0, keepdims=True)
        target = jnp.where(own_rows < slots, remote, place_of(d) * nodes + own_rows - slots)
        named = (node_iota == target).astype(BF16)
        times_all[d] = jnp.log2(dot_nn(named, count.astype(BF16)))
        return carry

    lax.fori_loop(0, n, count_shard, 0)
    dkv_acc[...] = jnp.zeros_like(dkv_acc)
    def chain(o, k):
        y = lax.rem(chip + k, ny)
        from_left = zd >= o
        from_right = zd + o < nd
        left_sample = lax.rem(zd + nd - o, nd)
        right_sample = lax.rem(zd + o, nd)

        @pl.when(from_left)
        def _():
            arrived(nf_part.at[left_sample, core * ny + y], part_rs.at[left_sample, y])

        pass_on(left_sample, y, from_left & has_right, None, from_left)

        @pl.when(from_right)
        def _():
            arrived(nf_part.at[right_sample, core * ny + y], part_rs.at[right_sample, y])

        pass_on(right_sample, y, None, from_right & has_left, from_right)

    links = [(o, y) for o in range(1, nd) for y in range(ny)]
    links.sort(key=lambda link: 2 * link[0] + 3 * (link[1] > 0))

    def poll():
        if links:
            chain(*links.pop(0))

    poll()
    for o in range(1, ny):
        y = lax.rem(chip + ny - o, ny)
        p = core * ny + y
        arrived(nf_all.at[p], nf_rs.at[p])
        send(nf_all.at[p], nf_all.at[p], nfm_ss, nf_rs.at[p], mp=mate)
        nf_part[zd, p] = nf_all[p, :, half_cols]
        pass_on(zd, y, has_right, has_left, None)
    for o in range(ny):
        p = (1 - core) * ny + lax.rem(chip + o, ny)
        arrived(nf_all.at[p], nf_rs.at[p])
        nf_part[zd, p] = nf_all[p, :, half_cols]
    load_kv.wait()
    node_rows = nf_all[...].reshape(all_nodes, width)
    for k in range(2):
        cols = pl.ds(pl.multiple_of(k * width + me * hc, LANES), hc)
        kv_s[k] = dot_nn(node_rows, wkv[:, cols]).astype(BF16)
    for j in range(hc // LANES):
        keys_t[j] = kv_s[0, :, j * LANES : (j + 1) * LANES].T
    lane = lax.broadcasted_iota(jnp.int32, (1, LANES), 1)
    keep = [(lane // head) == s for s in range(per)]

    def spread(x):
        return jnp.concatenate([jnp.where(m, x, jnp.zeros_like(x)) for m in keep], axis=0)

    def shard(d):
        times = times_all[d]
        times = jnp.concatenate([times] * per, axis=1)

        def pair(j, carry):
            at = pl.ds(pl.multiple_of(j * LANES, LANES), LANES)
            qs = spread(qc_all[d, 0, :, at])
            cs = spread(qc_all[d, 1, :, at])
            keys = kv_s[0, :, at]
            values = kv_s[1, :, at]
            scores = dot_nt(keys, qs) * (scale * math.log2(math.e)) + times
            d_attn = dot_nt(values, cs)
            e = jnp.exp2(scores - jnp.max(scores, axis=0, keepdims=True))
            attn = e * (1.0 / jnp.sum(e, axis=0, keepdims=True))
            ds = attn * (d_attn - jnp.sum(attn * d_attn, axis=0, keepdims=True)) * scale
            ds = ds.astype(BF16)
            attn = attn.astype(BF16)
            both = dot_nn(keys_t[j], ds).astype(BF16)
            dq = jnp.concatenate(
                [
                    both[s * head : (s + 1) * head, s * grid_dev : (s + 1) * grid_dev]
                    for s in range(per)
                ],
                axis=0,
            )
            dq_s[d, :, at] = dq.T
            dkv_acc[0, :, at] += dot_nn(ds, qs).astype(BF16).astype(F32)
            dkv_acc[1, :, at] += dot_nn(attn, cs).astype(BF16).astype(F32)
            return carry

        lax.fori_loop(0, hc // LANES, pair, 0, unroll=True)

    def await_shard(d):
        arrived(qc_all.at[d], qc_rs.at[d])

    shard(me)
    await_shard(mate)
    shard(mate)
    poll()
    for o in range(1, ny):
        for k in range(2):
            d = lax.rem(chip + ny - o, ny) * 2 + lax.rem(core + k, 2)
            await_shard(d)
            shard(d)
            if k == 0:
                poll()

    for k in range(nd):
        half, off = k // per_half, (k % per_half) * zc
        dkv_s[k] = dkv_acc[half, :, off : off + zc].astype(BF16)
    inward = 1 - 2 * lax.div(zd, nd // 2)
    far_first = []
    for o in range(nd - 1, 0, -1):
        for there in (zd + inward * o, zd - inward * o):
            far_first.append((lax.rem(there + nd, nd), (there >= 0) & (there < nd)))
    for there, here in far_first:
        send(
            dkv_s.at[there], dkv_all.at[zd, chip], sc_ss, sc_rs.at[zd, chip],
            dp=there, when=here,
        )
    dkv_all[zd, chip] = dkv_s[zd]

    def across(sample, when):
        block = dkv_all.at[sample, chip]
        for o in range(1, ny):
            there = lax.rem(chip + o, ny) * 2 + core
            send(block, block, scy_ss, sc_rs.at[sample, chip], mp=there, when=when)

    def gather_across(o):
        for sample, here in ((lax.rem(zd + nd - o, nd), zd >= o), (lax.rem(zd + o, nd), zd + o < nd)):

            @pl.when(here)
            def _():
                arrived(dkv_all.at[sample, chip], sc_rs.at[sample, chip])

            across(sample, here)

    across(zd, None)
    for o in range(1, n):
        there = peer_of(o)
        send(dq_s.at[there], dq_rows.at[:, own_cols], rq_ss, rq_rs, mp=there)
    dq_rows[:, own_cols] = dq_s[me]
    ret_kv[me] = dkv_s[:, pl.ds(pl.multiple_of(mine * nodes, nodes), nodes)]

    targets = [peer_of(o + 1) for o in range(n)]
    theirs = (1 - core) * ny + chip
    arrived(gf_all.at[theirs], gf_rs.at[theirs])

    def query_term(t, chips):
        cols = pl.ds(pl.multiple_of(t * hc, LANES), hc)
        left = [gf_all[c * ny + y, :, cols] for y in chips for c in range(2)]
        right = [dq_s[y * 2 + c] for y in chips for c in range(2)]
        return dot_tn(jnp.concatenate(left, axis=0), jnp.concatenate(right, axis=0))

    for t in targets:
        own_term[t] = query_term(t, [chip])
    poll()
    for o in range(1, ny):
        p = core * ny + lax.rem(chip + ny - o, ny)
        arrived(gf_all.at[p], gf_rs.at[p])
        send(gf_all.at[p], gf_all.at[p], gfm_ss, gf_rs.at[p], mp=mate)
    poll()
    for o in range(1, ny):
        p = (1 - core) * ny + lax.rem(chip + o, ny)
        arrived(gf_all.at[p], gf_rs.at[p])

    bits = [lax.rem(lax.div(zd, 1 << b), 2) for b in range(steps)]
    mates = [zd + (1 << b) * (1 - 2 * bits[b]) for b in range(steps)]

    def give(b, t):
        send(
            halves[b].at[t, :, 1 - bits[b]], gots[b].at[t], h_ss.at[b], h_rs.at[b, t],
            dp=mates[b],
        )

    others = [lax.rem(chip + o, ny) for o in range(1, ny)]
    for t in targets:
        term = (own_term[t] + query_term(t, others)) * wscale
        halves[0][t] = term.astype(BF16).reshape(per_half, 2, out_rows, hc)
        give(0, t)

    def column(m, k):
        return (k // per_half) * width + m * hc + (k % per_half) * zc

    def halve(b, i):
        t = targets[i]
        arrived(gots[b].at[t], h_rs.at[b, t])
        total = halves[b][t, :, bits[b]].astype(F32) + gots[b][t].astype(F32)
        total = total.astype(BF16)
        if b + 1 < steps:
            halves[b + 1][t] = total.reshape(halves[b + 1].shape[1:])
            give(b + 1, t)
        elif i < n - 1:
            fin_s[t] = total.reshape(out_rows, hc)
            send(fin_s.at[t], fin_q.at[me], fq_ss, fq_rs, mp=t)
        else:
            fin_q[me] = total.reshape(out_rows, hc)

    for o in range(1, nd):
        gather_across(o)
        poll()
    while links:
        poll()
    def keyval_block(i, y):
        k = lax.rem(core + 1 + i, 2)
        cols = pl.ds(pl.multiple_of(k * hc, LANES), hc)
        term = dot_tn(
            nf_part[:, :, :, cols].reshape(nd * all_nodes, hc),
            dkv_all[:, y].reshape(nd * all_nodes, zc),
        ) * wscale
        tkv[k, y] = term.astype(BF16).reshape(nd, out_rows, zc)

        def block_to(there, when):
            send(
                tkv.at[k, y, there], fin_kv.at[core * nd + zd, y], fk_ss,
                fk_rs, mp=chip * 2 + k, dp=there, when=when,
            )

        for there, here in far_first:
            block_to(there, here)
        if i == 0:
            block_to(zd, None)
        else:
            fin_kv[core * nd + zd, y] = tkv[k, y, zd]

    arrived(nf_part.at[0 : nd - 1, 0:ny], partm_rs)
    keyval_block(0, chip)
    keyval_block(1, chip)
    for o in range(1, n):
        there = peer_of(o)
        node_block = pl.ds(pl.multiple_of(place_of(there) * nodes, nodes), nodes)
        send(dkv_s.at[:, node_block], ret_kv.at[me], rkv_ss, rkv_rs, mp=there)
    inner = has_left & has_right
    halve(0, 0)

    @pl.when(inner)
    def _():
        for i in range(1, n // 2):
            halve(0, i)

    arrived(dq_s.at[0 : n - 1], rq_rs)
    dgrid[...] = dot_nt(dq_rows[...], wq[...]).astype(BF16)

    @pl.when(inner)
    def _():
        for i in range(n // 2, n):
            halve(0, i)

    for s in range(nd):
        for y in others:
            arrived(dkv_all.at[s, y], sc_rs.at[s, y])
    for i in range(2):
        for y in others:
            keyval_block(i, y)

    @pl.when(jnp.logical_not(inner))
    def _():
        for i in range(1, n):
            halve(0, i)

    arrived(ret_kv.at[0 : n - 1], rkv_rs)
    for m in range(n):
        for k in range(nd):
            dkv_rows[:, column(m, k) : column(m, k) + zc] = ret_kv[m, k]
    dnodes[...] = dot_nt(dkv_rows[...], wkv[...]).astype(BF16)
    for b in range(1, steps - 1):
        for i in range(n):
            halve(b, i)
    for i in range(n // 2):
        halve(steps - 1, i)
    for i in range(n // 2, n):
        halve(steps - 1, i)

    arrived(fin_q.at[0 : n - 1], fq_rs)
    for m in range(n):
        dwq[:, m * hc : (m + 1) * hc] = fin_q[m].astype(F32)
    arrived(fin_kv.at[0 : 2 * nd - 1], fk_rs)
    for c in range(2):
        for k in range(nd):
            for y in range(ny):
                at = column(y * 2 + c, k)
                dwkv[:, at : at + zc] = fin_kv[c * nd + k, y].astype(F32)
    for c, when in sent:
        pl.when(when)(c.wait_send)
    left_here(idx_all.at[0 : n - 1], idx_ss)
    left_here(nf_all.at[0 : ny - 1], nfy_ss)
    left_here(nf_all.at[0:ny], nfm_ss)
    left_here(nf_part.at[0 : nd - 1, 0:ny], partm_ss)
    left_here(q_s.at[0 : n - 1], cot_ss)
    left_here(q_s.at[0 : n - 1], q_ss)
    left_here(gf_all.at[0 : ny - 1], gfy_ss)
    left_here(gf_all.at[0:ny], gfm_ss)
    left_here(dkv_s.at[0 : nd - 1], sc_ss)
    left_here(dkv_all.at[:, 0 : ny - 1], scy_ss)
    left_here(dq_s.at[0 : n - 1], rq_ss)
    left_here(ret_kv.at[0 : n - 1], rkv_ss)
    for b in range(steps):
        left_here(gots[b], h_ss.at[b])
    left_here(fin_s.at[0 : n - 1], fq_ss)
    left_here(fin_kv.at[0 : 2 * nd - 1], fk_ss)


def copy_kernel(*refs):
    for i in range(len(refs) // 2):
        refs[len(refs) // 2 + i][...] = refs[i][...]


def heads_apart(grid_feat, node_feat, cotangent, w_query, w_keyval, neighbours, send_rows):
    n = lax.axis_size("mp")
    nd = lax.axis_size("dp")
    grid_dev, width = grid_feat.shape[1:]
    nodes = node_feat.shape[1]
    nbrs = neighbours.shape[1]
    cap = send_rows.shape[2]
    rows = n * cap + nodes
    hc = width // n
    zc = 2 * hc // nd
    ny = n // 2
    steps = nd.bit_length() - 1
    out_rows = width // (n * nd)
    wscale = 1.0 / math.sqrt(nd * grid_dev * n)
    idx_rows = nbrs + n
    idx_lanes = max(grid_dev, rows)
    vmem = pl.BlockSpec(memory_space=pltpu.VMEM)
    hbm = pl.BlockSpec(memory_space=pltpu.HBM)
    dma = pltpu.SemaphoreType.DMA
    one = dma(())
    outs = (
        jax.ShapeDtypeStruct((grid_dev, width), BF16),
        jax.ShapeDtypeStruct((nodes, width), BF16),
        jax.ShapeDtypeStruct((out_rows, width), F32),
        jax.ShapeDtypeStruct((out_rows, 2 * width), F32),
    )
    held = pl.pallas_call(
        functools.partial(heads_kernel, n, nd, wscale),
        out_shape=outs,
        in_specs=[hbm] * 7,
        out_specs=(vmem, vmem, vmem, vmem),
        scratch_shapes=[
            pltpu.VMEM((width, width), BF16),
            pltpu.VMEM((width, 2 * width), BF16),
            pltpu.VMEM((grid_dev, width), BF16),
            pltpu.VMEM((n, hc, hc), F32),
            pltpu.VMEM((nbrs, grid_dev), jnp.int32),
            pltpu.VMEM((n, cap), jnp.int32),
            pltpu.VMEM((n, n * nodes, grid_dev), F32),
            pltpu.VMEM((n, -(-idx_rows // 8) * 8, idx_lanes), jnp.int32),
            pltpu.VMEM((n, nodes, width), BF16),
            pltpu.VMEM((nd, n, nodes, width // ny), BF16),
            pltpu.VMEM((n, grid_dev, width), BF16),
            pltpu.VMEM((n, grid_dev, hc), BF16),
            pltpu.VMEM((n, 2, grid_dev, hc), BF16),
            pltpu.VMEM((2, n * nodes, hc), BF16),
            pltpu.VMEM((hc // LANES, LANES, n * nodes), BF16),
            pltpu.VMEM((2, n * nodes, hc), F32),
            pltpu.VMEM((n, grid_dev, hc), BF16),
            pltpu.VMEM((grid_dev, width), BF16),
            pltpu.VMEM((nd, n * nodes, zc), BF16),
            pltpu.VMEM((nd, ny, n * nodes, zc), BF16),
            pltpu.VMEM((n, nd, nodes, zc), BF16),
            pltpu.VMEM((nodes, 2 * width), BF16),
            pltpu.VMEM((n, out_rows, hc), BF16),
            pltpu.VMEM((n, out_rows, hc), BF16),
            pltpu.VMEM((2, ny, nd, out_rows, zc), BF16),
            pltpu.VMEM((2 * nd, ny, out_rows, zc), BF16),
        ] + [
            pltpu.VMEM((n, nd >> (b + 1), 2, out_rows, hc), BF16) for b in range(steps)
        ] + [
            pltpu.VMEM((n, nd >> (b + 1), out_rows, hc), BF16) for b in range(steps)
        ] + [
            dma((8,)), one, one,
            one, one, dma((n,)),
            dma((nd + 1, ny)), one, dma((nd, ny)), one,
            one, one, dma((n,)),
            one, one, dma((n,)),
            one, one, dma((nd, ny)),
            one, one, one, one,
            dma((steps,)), dma((steps, n)),
            one, one, one, one,
        ],
        compiler_params=pltpu.CompilerParams(
            collective_id=0, has_side_effects=True, vmem_limit_bytes=28 * 1024 * 1024
        ),
        name="heads_apart_grads",
    )(*(
        pltpu.with_memory_space_constraint(x, pltpu.HBM)
        for x in (
            grid_feat[0], node_feat[0], cotangent[0], w_query, w_keyval,
            neighbours.T, send_rows[0],
        )
    ))
    d_grid, d_nodes, dw_query, dw_keyval = pl.pallas_call(
        copy_kernel, out_shape=outs, in_specs=[vmem] * 4, out_specs=(vmem,) * 4,
        compiler_params=pltpu.CompilerParams(vmem_limit_bytes=4 * 1024 * 1024),
        name="results",
    )(*held)
    return d_grid[None], d_nodes[None], dw_query, dw_keyval


def per_device(*args):
    n = lax.axis_size("mp")
    nd = lax.axis_size("dp")
    samples_dev, grid_dev, width = args[0].shape
    hc = width // n
    apart = (
        samples_dev == 1
        and n % 2 == 0
        and nd >= 4
        and nd & (nd - 1) == 0
        and hc % LANES == 0
        and 2 * hc % (nd * LANES) == 0
        and grid_dev % LANES == 0
        and width % (HEADS * n) == 0
        and LANES % (width // HEADS) == 0
        and width % (n * nd * 16) == 0
        and args[6].shape[2] * n <= 256
        and args[1].shape[1] * n <= 256
    )
    return heads_apart(*args) if apart else rows_apart(*args)


def solution(mesh):
    in_specs = (
        P(("groups", "dp"), "mp", None),
        P(("groups", "dp"), "mp", None),
        P(("groups", "dp"), "mp", None),
        P(),
        P(),
        P("mp", None),
        P("mp", None, None),
    )
    out_specs = (
        P(("groups", "dp"), "mp", None),
        P(("groups", "dp"), "mp", None),
        P(("groups", "mp", "dp"), None),
        P(("groups", "mp", "dp"), None),
    )
    return jax.shard_map(
        per_device, mesh=mesh, in_specs=in_specs, out_specs=out_specs, check_vma=False
    )
```

```python
import functools
import math

import jax
import jax.numpy as jnp
from jax import lax
from jax.experimental import pallas as pl
from jax.experimental.pallas import tpu as pltpu
from jax.sharding import PartitionSpec as P

HEADS = 16
LANES = 128
MESH = pl.DeviceIdType.MESH
F32 = jnp.float32
BF16 = jnp.bfloat16


def dot_nn(x, y):
    return lax.dot_general(x, y, (((1,), (0,)), ((), ())), preferred_element_type=F32)


def dot_nt(x, y):
    return lax.dot_general(x, y, (((1,), (1,)), ((), ())), preferred_element_type=F32)


def dot_tn(x, y):
    return lax.dot_general(x, y, (((0,), (0,)), ((), ())), preferred_element_type=F32)


def kernel(
    n, nd, wscale,
    gf, nf, cot, wq_h, wkv_h, nbr, sr_col, sr_row,
    dgrid, dnodes, dwq, dwkv,
    wq, wkv, out_feat, tab, q_s, kv_s, count_s, gf_all, nf_all, dq_s, dq_all,
    part_s, ret_s, dkv_s, dkv_all, tq, tkv, rq, rkv, oq, okv, swq, swkv,
    local_sem, feat_ss, feat_rs, half_ss, half_rs, dq_ss, dq_rs, ret_ss, ret_rs,
    dkv_ss, dkv_rs, z_ss, z_rs, sw_ss, sw_rs,
):
    grid_dev, width = gf.shape
    nodes = nf.shape[0]
    slots = sr_col.shape[0]
    rows = slots + nodes
    cap = slots // n
    nbrs = nbr.shape[1]
    a = width // gf_all.shape[2]
    b = n // a
    high = width // a
    wide = width // b
    out_rows = dwq.shape[0]
    head = width // HEADS
    per = LANES // head
    scale = head ** (-0.5)
    me = lax.axis_index("mp")
    zd = lax.axis_index("dp")
    mine_i = me // b
    mine_j = lax.rem(me, b)

    def to_mp(src, dst, ssem, rsem, peer):
        return pltpu.make_async_remote_copy(
            src_ref=src, dst_ref=dst, send_sem=ssem, recv_sem=rsem,
            device_id={"mp": peer}, device_id_type=MESH,
        )

    def to_dp(src, dst, ssem, rsem, peer):
        return pltpu.make_async_remote_copy(
            src_ref=src, dst_ref=dst, send_sem=ssem, recv_sem=rsem,
            device_id={"dp": peer}, device_id_type=MESH,
        )

    def peer_of(o):
        return lax.rem(me + o, n)

    load_q = pltpu.make_async_copy(wq_h, wq, local_sem.at[0])
    load_kv = pltpu.make_async_copy(wkv_h, wkv, local_sem.at[1])
    load_q.start()
    load_kv.start()
    barrier = pltpu.get_barrier_semaphore()
    for o in range(1, n):
        pl.semaphore_signal(barrier, inc=1, device_id={"mp": peer_of(o)}, device_id_type=MESH)
    for o in range(1, nd):
        pl.semaphore_signal(
            barrier, inc=1, device_id={"dp": lax.rem(zd + o, nd)}, device_id_type=MESH
        )
    pick = (sr_col[...] == lax.broadcasted_iota(jnp.int32, (slots, nodes), 1)).astype(BF16)
    out_feat[...] = dot_nn(pick, nf[...]).astype(BF16)
    tab[pl.ds(slots, nodes), :] = nf[...]
    own_slots = pl.ds(pl.multiple_of(me * cap, cap), cap)
    tab[own_slots, :] = jnp.zeros((cap, width), BF16)
    for jb in range(b):
        ret_s[jb, own_slots, :] = jnp.zeros((cap, 2 * wide), BF16)
    pl.semaphore_wait(barrier, n - 1 + nd - 1)

    feat = []
    for o in range(1, n):
        there = pl.ds(pl.multiple_of(peer_of(o) * cap, cap), cap)
        feat.append(
            to_mp(out_feat.at[there], tab.at[own_slots], feat_ss.at[o], feat_rs.at[o], peer_of(o))
        )
        feat[-1].start()

    ids = nbr[...]
    row_id = lax.broadcasted_iota(jnp.int32, (grid_dev, rows), 1)
    count = jnp.zeros((grid_dev, rows), F32)
    for k in range(nbrs):
        count += (ids[:, k : k + 1] == row_id).astype(F32)
    for s in range(per):
        count_s[s * grid_dev : (s + 1) * grid_dev, :] = count
    half_cols = pl.ds(pl.multiple_of(mine_i * high, high), high)
    gf_all[me] = gf[:, half_cols]
    nf_all[me] = nf[:, half_cols]
    load_q.wait()
    q_s[...] = dot_nn(gf[...], wq[...]).astype(BF16)
    for c in feat:
        c.wait_recv()
    half = []
    for o in range(1, n):
        there = pl.ds(pl.multiple_of((peer_of(o) // b) * high, high), high)
        half.append(
            to_mp(nf.at[:, there], nf_all.at[me], half_ss.at[0, o], half_rs.at[0, o], peer_of(o))
        )
        half.append(
            to_mp(gf.at[:, there], gf_all.at[me], half_ss.at[1, o], half_rs.at[1, o], peer_of(o))
        )
    for c in half:
        c.start()
    load_kv.wait()
    kv_s[...] = dot_nn(tab[...], wkv[...]).astype(BF16)

    lane = lax.broadcasted_iota(jnp.int32, (1, LANES), 1)
    keep = [(lane // head) == s for s in range(per)]

    def spread(x):
        return jnp.concatenate([jnp.where(m, x, jnp.zeros_like(x)) for m in keep], axis=0)

    dq_copies = []
    ret_copies = []
    for jb in range(b):

        def one(blk, carry):
            off = pl.multiple_of(jb * wide + blk * LANES, LANES)
            at = pl.ds(off, LANES)
            at_v = pl.ds(pl.multiple_of(width + off, LANES), LANES)
            here = pl.ds(pl.multiple_of(blk * LANES, LANES), LANES)
            here_v = pl.ds(pl.multiple_of(wide + blk * LANES, LANES), LANES)
            qs = spread(q_s[:, at])
            cs = spread(cot[:, at])
            keys = kv_s[:, at]
            values = kv_s[:, at_v]
            times = count_s[...]
            scores = dot_nt(qs, keys) * scale
            d_attn = dot_nt(cs, values)
            top = jnp.max(
                jnp.where(times > 0, scores, -jnp.inf), axis=1, keepdims=True
            )
            e = jnp.where(times > 0, times * jnp.exp(jnp.minimum(scores - top, 0.0)), 0.0)
            attn = e / jnp.sum(e, axis=1, keepdims=True)
            ds = attn * (d_attn - jnp.sum(attn * d_attn, axis=1, keepdims=True)) * scale
            ds = ds.astype(BF16)
            attn = attn.astype(BF16)
            dq = None
            for s in range(per):
                term = dot_nn(
                    ds[s * grid_dev : (s + 1) * grid_dev],
                    jnp.where(keep[s], keys, jnp.zeros_like(keys)),
                )
                dq = term if dq is None else dq + term
            dq_s[jb, :, here] = dq.astype(BF16)
            part_s[jb, :, here] = dot_tn(ds, qs).astype(BF16)
            part_s[jb, :, here_v] = dot_tn(attn, cs).astype(BF16)
            return carry

        lax.fori_loop(0, wide // LANES, one, 0)
        for o in range(1, n):
            peer = peer_of(o)
            c = to_mp(dq_s.at[jb], dq_all.at[me], dq_ss.at[o], dq_rs.at[o], peer)

            @pl.when(lax.rem(peer, b) == jb)
            def _():
                c.start()

        for o in range(1, n):
            there = pl.ds(pl.multiple_of(peer_of(o) * cap, cap), cap)
            c = to_mp(
                part_s.at[jb, there], ret_s.at[jb, own_slots],
                ret_ss.at[jb, o], ret_rs.at[jb, o], peer_of(o),
            )
            c.start()
            ret_copies.append(c)

    dq_all[me] = dq_s[mine_j]
    acc = None
    for jb in range(b):
        term = dot_nt(dq_s[jb], wq[:, jb * wide : (jb + 1) * wide])
        acc = term if acc is None else acc + term
    dgrid[...] = acc.astype(BF16)

    place = (sr_row[...] == lax.broadcasted_iota(jnp.int32, (nodes, slots), 0)).astype(BF16)
    for jb in range(b):
        for o in range(1, n):
            ret_copies[jb * (n - 1) + o - 1].wait_recv()
        dkv = part_s[jb, slots:, :].astype(F32) + dot_nn(place, ret_s[jb])
        dkv_s[jb] = dkv.astype(BF16)
        for o in range(1, n):
            peer = peer_of(o)
            c = to_mp(dkv_s.at[jb], dkv_all.at[me], dkv_ss.at[o], dkv_rs.at[o], peer)

            @pl.when(lax.rem(peer, b) == jb)
            def _():
                c.start()

    dkv_all[me] = dkv_s[mine_j]

    def got(src, dst, ssem, rsem):
        return to_mp(src, dst, ssem, rsem, peer_of(1))

    for c in half:
        c.wait_recv()
    for o in range(1, n):
        got(dq_s.at[0], dq_all.at[me], dq_ss.at[o], dq_rs.at[o]).wait_recv()
    term_q = dot_tn(
        gf_all[...].reshape(n * grid_dev, high), dq_all[...].reshape(n * grid_dev, wide)
    ) * wscale
    term_q = term_q.astype(BF16).reshape(b, nd, out_rows, wide)
    for d in range(nd):
        tq[d] = term_q[:, d]
    z_copies = []
    for o in range(1, nd):
        peer = lax.rem(zd + o, nd)
        z_copies.append(to_dp(tq.at[peer], rq.at[o], z_ss.at[0, o], z_rs.at[0, o], peer))
        z_copies[-1].start()

    acc = None
    for jb in range(b):
        for k in range(2):
            term = dot_nt(
                dkv_s[jb, :, k * wide : (k + 1) * wide],
                wkv[:, k * width + jb * wide : k * width + (jb + 1) * wide],
            )
            acc = term if acc is None else acc + term
    dnodes[...] = acc.astype(BF16)

    for o in range(1, n):
        got(dkv_s.at[0], dkv_all.at[me], dkv_ss.at[o], dkv_rs.at[o]).wait_recv()
    term_kv = dot_tn(
        nf_all[...].reshape(n * nodes, high), dkv_all[...].reshape(n * nodes, 2 * wide)
    ) * wscale
    term_kv = term_kv.astype(BF16).reshape(b, nd, out_rows, 2 * wide)
    for d in range(nd):
        tkv[d] = term_kv[:, d]
    for o in range(1, nd):
        peer = lax.rem(zd + o, nd)
        z_copies.append(to_dp(tkv.at[peer], rkv.at[o], z_ss.at[1, o], z_rs.at[1, o], peer))
        z_copies[-1].start()

    def finish(which, t, r, out, sw, width_out):
        total = t[zd].astype(F32)
        for o in range(1, nd):
            z_copies[which * (nd - 1) + o - 1].wait_recv()
            total += r[o].astype(F32)
        out[...] = total.astype(BF16)
        sent = []
        for o in range(1, b):
            mate = lax.rem(mine_j + o, b)
            c = to_mp(
                out.at[mate], sw.at[o], sw_ss.at[which, o], sw_rs.at[which, o],
                mine_i * b + mate,
            )
            c.start()
            sent.append(c)
        return sent

    sent_q = finish(0, tq, rq, oq, swq, wide)
    sent_kv = finish(1, tkv, rkv, okv, swkv, 2 * wide)

    def columns(j, k):
        return pl.ds(pl.multiple_of(k * width + j * wide, LANES), wide)

    dwq[:, columns(mine_j, 0)] = oq[mine_j].astype(F32)
    for o in range(1, b):
        source = lax.rem(mine_j + b - o, b)
        sent_q[o - 1].wait_recv()
        dwq[:, columns(source, 0)] = swq[o].astype(F32)
    for k in range(2):
        dwkv[:, columns(mine_j, k)] = okv[mine_j][:, k * wide : (k + 1) * wide].astype(F32)
    for o in range(1, b):
        source = lax.rem(mine_j + b - o, b)
        sent_kv[o - 1].wait_recv()
        for k in range(2):
            dwkv[:, columns(source, k)] = swkv[o][:, k * wide : (k + 1) * wide].astype(F32)

    for c in feat + half + ret_copies + z_copies + sent_q + sent_kv:
        c.wait_send()
    for o in range(1, n):
        got(dq_s.at[0], dq_all.at[me], dq_ss.at[o], dq_rs.at[o]).wait_send()
        got(dkv_s.at[0], dkv_all.at[me], dkv_ss.at[o], dkv_rs.at[o]).wait_send()


def rows_apart(grid_feat, node_feat, cotangent, w_query, w_keyval, neighbours, send_rows):
    n = lax.axis_size("mp")
    nd = lax.axis_size("dp")
    samples_dev, grid_dev, width = grid_feat.shape
    nodes = node_feat.shape[1]
    cap = send_rows.shape[2]
    slots = n * cap
    rows = slots + nodes
    a = 2
    b = n // a
    high = width // a
    wide = width // b
    out_rows = width // (n * nd)
    per = LANES * HEADS // width
    wscale = 1.0 / math.sqrt(samples_dev * nd * grid_dev * n)
    vmem = pl.BlockSpec(memory_space=pltpu.VMEM)
    anywhere = pl.BlockSpec(memory_space=pl.ANY)
    dma = pltpu.SemaphoreType.DMA
    d_grid, d_nodes, dw_query, dw_keyval = pl.pallas_call(
        functools.partial(kernel, n, nd, wscale),
        out_shape=(
            jax.ShapeDtypeStruct((grid_dev, width), BF16),
            jax.ShapeDtypeStruct((nodes, width), BF16),
            jax.ShapeDtypeStruct((out_rows, width), F32),
            jax.ShapeDtypeStruct((out_rows, 2 * width), F32),
        ),
        in_specs=[vmem, vmem, vmem, anywhere, anywhere, vmem, vmem, vmem],
        out_specs=(vmem, vmem, vmem, vmem),
        scratch_shapes=[
            pltpu.VMEM((width, width), BF16),
            pltpu.VMEM((width, 2 * width), BF16),
            pltpu.VMEM((slots, width), BF16),
            pltpu.VMEM((rows, width), BF16),
            pltpu.VMEM((grid_dev, width), BF16),
            pltpu.VMEM((rows, 2 * width), BF16),
            pltpu.VMEM((per * grid_dev, rows), F32),
            pltpu.VMEM((n, grid_dev, high), BF16),
            pltpu.VMEM((n, nodes, high), BF16),
            pltpu.VMEM((b, grid_dev, wide), BF16),
            pltpu.VMEM((n, grid_dev, wide), BF16),
            pltpu.VMEM((b, rows, 2 * wide), BF16),
            pltpu.VMEM((b, slots, 2 * wide), BF16),
            pltpu.VMEM((b, nodes, 2 * wide), BF16),
            pltpu.VMEM((n, nodes, 2 * wide), BF16),
            pltpu.VMEM((nd, b, out_rows, wide), BF16),
            pltpu.VMEM((nd, b, out_rows, 2 * wide), BF16),
            pltpu.VMEM((nd, b, out_rows, wide), BF16),
            pltpu.VMEM((nd, b, out_rows, 2 * wide), BF16),
            pltpu.VMEM((b, out_rows, wide), BF16),
            pltpu.VMEM((b, out_rows, 2 * wide), BF16),
            pltpu.VMEM((b, out_rows, wide), BF16),
            pltpu.VMEM((b, out_rows, 2 * wide), BF16),
            dma((2,)),
            dma((n,)), dma((n,)),
            dma((2, n)), dma((2, n)),
            dma((n,)), dma((n,)),
            dma((b, n)), dma((b, n)),
            dma((n,)), dma((n,)),
            dma((2, nd)), dma((2, nd)),
            dma((2, b)), dma((2, b)),
        ],
        compiler_params=pltpu.CompilerParams(
            collective_id=0, has_side_effects=True, vmem_limit_bytes=56 * 1024 * 1024
        ),
        name="graph_attention_grads",
    )(
        grid_feat[0], node_feat[0], cotangent[0], w_query, w_keyval, neighbours,
        send_rows.reshape(slots, 1), send_rows.reshape(1, slots),
    )
    return d_grid[None], d_nodes[None], dw_query, dw_keyval


def heads_kernel(
    n, nd, wscale,
    gf_h, nf_h, cot_h, wq_h, wkv_h, nbr_h, sr_h,
    dgrid, dnodes, dwq, dwkv,
    wq, wkv, cot, own_term, nbr_t, sr, times_all, idx_all, nf_all, nf_part, gf_all, q_s, qc_all, kv_s, dkv_acc, dq_s, dq_rows,
    dkv_s, dkv_all, ret_kv, dkv_rows, fin_s, fin_q, tkv, fin_kv, *rest,
):
    steps = nd.bit_length() - 1
    halves, rest = rest[: steps], rest[steps:]
    gots, rest = rest[: steps], rest[steps:]
    (
        local_sem, idx_ss, idx_rs, nfy_ss, nfm_ss, nf_rs, part_ss, partm_ss, part_rs, partm_rs,
        cot_ss, q_ss, qc_rs, gfy_ss, gfm_ss, gf_rs, sc_ss, scy_ss, sc_rs, rq_ss, rq_rs,
        rkv_ss, rkv_rs, h_ss, h_rs, fq_ss, fq_rs, fk_ss, fk_rs,
    ) = rest
    grid_dev, width = gf_h.shape
    nodes = nf_h.shape[0]
    nbrs = nbr_t.shape[0]
    cap = sr.shape[1]
    slots = n * cap
    rows = slots + nodes
    all_nodes = n * nodes
    hc = width // n
    zc = 2 * hc // nd
    per_half = nd // 2
    out_rows = dwq.shape[0]
    head = width // HEADS
    per = LANES // head
    scale = head ** (-0.5)
    ny = n // 2
    wy = width // ny
    sr_at = idx_all.shape[1] - n
    me = lax.axis_index("mp")
    zd = lax.axis_index("dp")
    core = lax.rem(me, 2)
    chip = lax.div(me, 2)
    mate = me + 1 - 2 * core

    def place_of(m):
        return lax.rem(m, 2) * ny + lax.div(m, 2)

    mine = place_of(me)
    sent = []

    def send(src, dst, ssem, rsem, mp=None, dp=None, when=None):
        device = {}
        if mp is not None:
            device["mp"] = mp
        if dp is not None:
            device["dp"] = dp
        c = pltpu.make_async_remote_copy(
            src_ref=src, dst_ref=dst, send_sem=ssem, recv_sem=rsem,
            device_id=device, device_id_type=MESH,
        )
        if when is None:
            c.start()
        else:
            pl.when(when)(c.start)
        return c

    def left_here(block, ssem):
        pltpu.make_async_remote_copy(
            src_ref=block, dst_ref=block, send_sem=ssem, recv_sem=ssem,
            device_id={"mp": mate}, device_id_type=MESH,
        ).wait_send()

    def arrived(dst, rsem):
        pltpu.make_async_remote_copy(
            src_ref=dst, dst_ref=dst, send_sem=rsem, recv_sem=rsem,
            device_id={"mp": mate}, device_id_type=MESH,
        ).wait_recv()

    def peer_of(o):
        return lax.rem(me + o, n)

    barrier = pltpu.get_barrier_semaphore()
    for o in range(n):
        for k in range(nd):
            if o or k:
                pl.semaphore_signal(
                    barrier, inc=1,
                    device_id={"mp": peer_of(o), "dp": lax.rem(zd + k, nd)}, device_id_type=MESH,
                )
    own_cols = pl.ds(pl.multiple_of(me * hc, hc), hc)
    half_cols = pl.ds(pl.multiple_of(chip * wy, LANES), wy)

    def load(i, src, dst):
        c = pltpu.make_async_copy(src, dst, local_sem.at[i])
        c.start()
        return c

    load_nbr = load(0, nbr_h, nbr_t)
    load_sr = load(1, sr_h, sr)
    load_nf = load(2, nf_h, nf_all.at[mine])
    load_part = load(3, nf_h.at[:, half_cols], nf_part.at[zd, mine])
    load_gf = load(5, gf_h, gf_all.at[mine])
    load_q = load(6, wq_h, wq)
    load_cot = load(4, cot_h, cot)
    load_kv = load(7, wkv_h, wkv)

    load_nbr.wait()
    load_sr.wait()
    lane_slot = lax.broadcasted_iota(jnp.int32, (cap, rows), 1)
    tile = (lax.rem(lane_slot, cap) == lax.broadcasted_iota(jnp.int32, (cap, rows), 0)).astype(BF16)
    spread_rows = dot_nn(sr[...].astype(F32).astype(BF16), tile).astype(jnp.int32) + mine * nodes
    lane_row = lax.broadcasted_iota(jnp.int32, (n, rows), 1)
    own_lane = (lane_row >= me * cap) & (lane_row < me * cap + cap)
    idx_all[me] = jnp.zeros(idx_all.shape[1:], jnp.int32)
    idx_all[me, 0:nbrs, 0:grid_dev] = nbr_t[...]
    idx_all[me, sr_at : sr_at + n, 0:rows] = jnp.where(own_lane, spread_rows, 0)
    load_nf.wait()
    load_part.wait()
    pl.semaphore_wait(barrier, n * nd - 1)

    for o in range(1, n):
        send(idx_all.at[me], idx_all.at[me], idx_ss, idx_rs, mp=peer_of(o))

    has_right = zd + 1 < nd
    has_left = zd > 0

    def pass_on(sample, y, to_right, to_left, when):
        block = nf_part.at[sample, core * ny + y]
        rsem = part_rs.at[sample, y]
        for step, go, at in ((1, to_right, sample), (nd - 1, to_left, sample if when is not None else nd)):
            if go is not None:
                c = send(block, block, part_ss.at[at, y], rsem, dp=lax.rem(zd + step, nd), when=go)
                sent.append((c, go))
        if when is not None:
            send(block, block, partm_ss, partm_rs, mp=mate, when=when)

    for o in range(1, ny):
        there = lax.rem(chip + o, ny) * 2 + core
        send(nf_all.at[mine], nf_all.at[mine], nfy_ss, nf_rs.at[mine], mp=there)
    send(nf_all.at[mine], nf_all.at[mine], nfm_ss, nf_rs.at[mine], mp=mate)
    pass_on(zd, chip, has_right, has_left, None)
    readers = [lax.rem(chip + o, ny) * 2 + lax.rem(core + k, 2) for k in range(2) for o in range(ny)]
    readers = readers[1:ny] + [readers[ny]] + readers[ny + 1 :]

    def send_cot(i):
        there = readers[i]
        cols = pl.ds(pl.multiple_of(there * hc, hc), hc)
        send(cot.at[:, cols], qc_all.at[me, 1], cot_ss, qc_rs.at[me], mp=there)

    load_cot.wait()
    for i in range(ny):
        send_cot(i)
    qc_all[me, 1] = cot[:, own_cols]
    load_gf.wait()
    load_q.wait()
    query = dot_nn(gf_all[mine], wq[...]).astype(BF16)
    for k in range(n):
        q_s[k] = query[:, k * hc : (k + 1) * hc]
    for i in range(n - 1):
        there = readers[i]
        if i >= ny:
            send_cot(i)
        send(q_s.at[there], qc_all.at[me, 0], q_ss, qc_rs.at[me], mp=there)
    qc_all[me, 0] = q_s[me]
    for o in range(1, ny):
        there = lax.rem(chip + o, ny) * 2 + core
        send(gf_all.at[mine], gf_all.at[mine], gfy_ss, gf_rs.at[mine], mp=there)
    send(gf_all.at[mine], gf_all.at[mine], gfm_ss, gf_rs.at[mine], mp=mate)

    arrived(idx_all.at[0 : n - 1], idx_rs)
    plan = None
    for m in range(n):
        part = idx_all[m, sr_at : sr_at + n, 0:rows]
        plan = part if plan is None else plan + part
    own_rows = lax.broadcasted_iota(jnp.int32, (1, rows), 1)
    node_iota = lax.broadcasted_iota(jnp.int32, (all_nodes, rows), 0)
    row_iota = lax.broadcasted_iota(jnp.int32, (rows, grid_dev), 0)
    reader = lax.broadcasted_iota(jnp.int32, (n, rows), 0)

    def count_shard(d, carry):
        ids = idx_all[d, 0:nbrs, 0:grid_dev]
        count = jnp.zeros((rows, grid_dev), F32)
        for k in range(nbrs):
            count += (ids[k : k + 1, :] == row_iota).astype(F32)
        remote = jnp.sum(jnp.where(reader == d, plan, 0), axis=0, keepdims=True)
        target = jnp.where(own_rows < slots, remote, place_of(d) * nodes + own_rows - slots)
        named = (node_iota == target).astype(BF16)
        times_all[d] = dot_nn(named, count.astype(BF16))
        return carry

    lax.fori_loop(0, n, count_shard, 0)
    dkv_acc[...] = jnp.zeros_like(dkv_acc)
    def chain(o, k):
        y = lax.rem(chip + k, ny)
        from_left = zd >= o
        from_right = zd + o < nd
        left_sample = lax.rem(zd + nd - o, nd)
        right_sample = lax.rem(zd + o, nd)

        @pl.when(from_left)
        def _():
            arrived(nf_part.at[left_sample, core * ny + y], part_rs.at[left_sample, y])

        pass_on(left_sample, y, from_left & has_right, None, from_left)

        @pl.when(from_right)
        def _():
            arrived(nf_part.at[right_sample, core * ny + y], part_rs.at[right_sample, y])

        pass_on(right_sample, y, None, from_right & has_left, from_right)

    links = [(o, y) for o in range(1, nd) for y in range(ny)]
    links.sort(key=lambda link: 2 * link[0] + 3 * (link[1] > 0))

    def poll():
        if links:
            chain(*links.pop(0))

    poll()
    for o in range(1, ny):
        y = lax.rem(chip + ny - o, ny)
        p = core * ny + y
        arrived(nf_all.at[p], nf_rs.at[p])
        send(nf_all.at[p], nf_all.at[p], nfm_ss, nf_rs.at[p], mp=mate)
        nf_part[zd, p] = nf_all[p, :, half_cols]
        pass_on(zd, y, has_right, has_left, None)
    for o in range(ny):
        p = (1 - core) * ny + lax.rem(chip + o, ny)
        arrived(nf_all.at[p], nf_rs.at[p])
        nf_part[zd, p] = nf_all[p, :, half_cols]
    load_kv.wait()
    node_rows = nf_all[...].reshape(all_nodes, width)
    for k in range(2):
        cols = pl.ds(pl.multiple_of(k * width + me * hc, LANES), hc)
        kv_s[k] = dot_nn(node_rows, wkv[:, cols]).astype(BF16)
    lane = lax.broadcasted_iota(jnp.int32, (1, LANES), 1)
    keep = [(lane // head) == s for s in range(per)]

    def spread(x):
        return jnp.concatenate([jnp.where(m, x, jnp.zeros_like(x)) for m in keep], axis=0)

    def shard(d):
        times = times_all[d]
        times = jnp.concatenate([times] * per, axis=1)

        def pair(j, carry):
            at = pl.ds(pl.multiple_of(j * LANES, LANES), LANES)
            qs = spread(qc_all[d, 0, :, at])
            cs = spread(qc_all[d, 1, :, at])
            keys = kv_s[0, :, at]
            values = kv_s[1, :, at]
            scores = dot_nt(keys, qs) * scale
            d_attn = dot_nt(values, cs)
            scores = jnp.where(times > 0, scores, -jnp.inf)
            e = times * jnp.exp(scores - jnp.max(scores, axis=0, keepdims=True))
            attn = e * (1.0 / jnp.sum(e, axis=0, keepdims=True))
            ds = attn * (d_attn - jnp.sum(attn * d_attn, axis=0, keepdims=True)) * scale
            ds = ds.astype(BF16)
            attn = attn.astype(BF16)
            both = dot_tn(ds, keys)
            dq = both[:grid_dev]
            for s in range(1, per):
                dq = jnp.where(keep[s], both[s * grid_dev : (s + 1) * grid_dev], dq)
            dq_s[d, :, at] = dq.astype(BF16)
            dkv_acc[0, :, at] += dot_nn(ds, qs).astype(BF16).astype(F32)
            dkv_acc[1, :, at] += dot_nn(attn, cs).astype(BF16).astype(F32)
            return carry

        lax.fori_loop(0, hc // LANES, pair, 0, unroll=True)

    def await_shard(d):
        arrived(qc_all.at[d], qc_rs.at[d])

    shard(me)
    await_shard(mate)
    shard(mate)
    poll()
    poll()
    for o in range(1, ny):
        for k in range(2):
            d = lax.rem(chip + ny - o, ny) * 2 + lax.rem(core + k, 2)
            await_shard(d)
            shard(d)

    for k in range(nd):
        half, off = k // per_half, (k % per_half) * zc
        dkv_s[k] = dkv_acc[half, :, off : off + zc].astype(BF16)
    inward = 1 - 2 * lax.div(zd, nd // 2)
    far_first = []
    for o in range(nd - 1, 0, -1):
        for there in (zd + inward * o, zd - inward * o):
            far_first.append((lax.rem(there + nd, nd), (there >= 0) & (there < nd)))
    for there, here in far_first:
        send(
            dkv_s.at[there], dkv_all.at[zd, chip], sc_ss, sc_rs.at[zd, chip],
            dp=there, when=here,
        )
    dkv_all[zd, chip] = dkv_s[zd]

    def across(sample, when):
        block = dkv_all.at[sample, chip]
        for o in range(1, ny):
            there = lax.rem(chip + o, ny) * 2 + core
            send(block, block, scy_ss, sc_rs.at[sample, chip], mp=there, when=when)

    def gather_across(o):
        for sample, here in ((lax.rem(zd + nd - o, nd), zd >= o), (lax.rem(zd + o, nd), zd + o < nd)):

            @pl.when(here)
            def _():
                arrived(dkv_all.at[sample, chip], sc_rs.at[sample, chip])

            across(sample, here)

    across(zd, None)
    for o in range(1, n):
        there = peer_of(o)
        send(dq_s.at[there], dq_rows.at[:, own_cols], rq_ss, rq_rs, mp=there)
    dq_rows[:, own_cols] = dq_s[me]
    ret_kv[me] = dkv_s[:, pl.ds(pl.multiple_of(mine * nodes, nodes), nodes)]

    targets = [peer_of(o + 1) for o in range(n)]
    theirs = (1 - core) * ny + chip
    arrived(gf_all.at[theirs], gf_rs.at[theirs])

    def query_term(t, chips):
        cols = pl.ds(pl.multiple_of(t * hc, LANES), hc)
        left = [gf_all[c * ny + y, :, cols] for y in chips for c in range(2)]
        right = [dq_s[y * 2 + c] for y in chips for c in range(2)]
        return dot_tn(jnp.concatenate(left, axis=0), jnp.concatenate(right, axis=0))

    for t in targets:
        own_term[t] = query_term(t, [chip])
    poll()
    for o in range(1, ny):
        p = core * ny + lax.rem(chip + ny - o, ny)
        arrived(gf_all.at[p], gf_rs.at[p])
        send(gf_all.at[p], gf_all.at[p], gfm_ss, gf_rs.at[p], mp=mate)
    poll()
    for o in range(1, ny):
        p = (1 - core) * ny + lax.rem(chip + o, ny)
        arrived(gf_all.at[p], gf_rs.at[p])

    bits = [lax.rem(lax.div(zd, 1 << b), 2) for b in range(steps)]
    mates = [zd + (1 << b) * (1 - 2 * bits[b]) for b in range(steps)]

    def give(b, t):
        send(
            halves[b].at[t, :, 1 - bits[b]], gots[b].at[t], h_ss.at[b], h_rs.at[b, t],
            dp=mates[b],
        )

    others = [lax.rem(chip + o, ny) for o in range(1, ny)]
    for t in targets:
        term = (own_term[t] + query_term(t, others)) * wscale
        halves[0][t] = term.astype(BF16).reshape(per_half, 2, out_rows, hc)
        give(0, t)

    def column(m, k):
        return (k // per_half) * width + m * hc + (k % per_half) * zc

    def halve(b, i):
        t = targets[i]
        arrived(gots[b].at[t], h_rs.at[b, t])
        total = halves[b][t, :, bits[b]].astype(F32) + gots[b][t].astype(F32)
        total = total.astype(BF16)
        if b + 1 < steps:
            halves[b + 1][t] = total.reshape(halves[b + 1].shape[1:])
            give(b + 1, t)
        elif i < n - 1:
            fin_s[t] = total.reshape(out_rows, hc)
            send(fin_s.at[t], fin_q.at[me], fq_ss, fq_rs, mp=t)
        else:
            fin_q[me] = total.reshape(out_rows, hc)

    for o in range(1, nd):
        gather_across(o)
        poll()
    while links:
        poll()
    def keyval_block(i, y):
        k = lax.rem(core + 1 + i, 2)
        cols = pl.ds(pl.multiple_of(k * hc, LANES), hc)
        term = dot_tn(
            nf_part[:, :, :, cols].reshape(nd * all_nodes, hc),
            dkv_all[:, y].reshape(nd * all_nodes, zc),
        ) * wscale
        tkv[k, y] = term.astype(BF16).reshape(nd, out_rows, zc)

        def block_to(there, when):
            send(
                tkv.at[k, y, there], fin_kv.at[core * nd + zd, y], fk_ss,
                fk_rs, mp=chip * 2 + k, dp=there, when=when,
            )

        for there, here in far_first:
            block_to(there, here)
        if i == 0:
            block_to(zd, None)
        else:
            fin_kv[core * nd + zd, y] = tkv[k, y, zd]

    arrived(nf_part.at[0 : nd - 1, 0:ny], partm_rs)
    keyval_block(0, chip)
    keyval_block(1, chip)
    for o in range(1, n):
        there = peer_of(o)
        node_block = pl.ds(pl.multiple_of(place_of(there) * nodes, nodes), nodes)
        send(dkv_s.at[:, node_block], ret_kv.at[me], rkv_ss, rkv_rs, mp=there)
    for i in range(n // 2):
        halve(0, i)
    arrived(dq_s.at[0 : n - 1], rq_rs)
    dgrid[...] = dot_nt(dq_rows[...], wq[...]).astype(BF16)
    for i in range(n // 2, n - 1):
        halve(0, i)
    for s in range(nd):
        for y in others:
            arrived(dkv_all.at[s, y], sc_rs.at[s, y])
    for i in range(2):
        for y in others:
            keyval_block(i, y)
    halve(0, n - 1)
    for b in range(1, steps - 1):
        for i in range(n):
            halve(b, i)
    for i in range(n // 2):
        halve(steps - 1, i)
    arrived(ret_kv.at[0 : n - 1], rkv_rs)
    for m in range(n):
        for k in range(nd):
            dkv_rows[:, column(m, k) : column(m, k) + zc] = ret_kv[m, k]
    dnodes[...] = dot_nt(dkv_rows[...], wkv[...]).astype(BF16)
    for i in range(n // 2, n):
        halve(steps - 1, i)

    arrived(fin_q.at[0 : n - 1], fq_rs)
    for m in range(n):
        dwq[:, m * hc : (m + 1) * hc] = fin_q[m].astype(F32)
    arrived(fin_kv.at[0 : 2 * nd - 1], fk_rs)
    for c in range(2):
        for k in range(nd):
            for y in range(ny):
                at = column(y * 2 + c, k)
                dwkv[:, at : at + zc] = fin_kv[c * nd + k, y].astype(F32)
    for c, when in sent:
        pl.when(when)(c.wait_send)
    left_here(idx_all.at[0 : n - 1], idx_ss)
    left_here(nf_all.at[0 : ny - 1], nfy_ss)
    left_here(nf_all.at[0:ny], nfm_ss)
    left_here(nf_part.at[0 : nd - 1, 0:ny], partm_ss)
    left_here(q_s.at[0 : n - 1], cot_ss)
    left_here(q_s.at[0 : n - 1], q_ss)
    left_here(gf_all.at[0 : ny - 1], gfy_ss)
    left_here(gf_all.at[0:ny], gfm_ss)
    left_here(dkv_s.at[0 : nd - 1], sc_ss)
    left_here(dkv_all.at[:, 0 : ny - 1], scy_ss)
    left_here(dq_s.at[0 : n - 1], rq_ss)
    left_here(ret_kv.at[0 : n - 1], rkv_ss)
    for b in range(steps):
        left_here(gots[b], h_ss.at[b])
    left_here(fin_s.at[0 : n - 1], fq_ss)
    left_here(fin_kv.at[0 : 2 * nd - 1], fk_ss)


def copy_kernel(*refs):
    for i in range(len(refs) // 2):
        refs[len(refs) // 2 + i][...] = refs[i][...]


def heads_apart(grid_feat, node_feat, cotangent, w_query, w_keyval, neighbours, send_rows):
    n = lax.axis_size("mp")
    nd = lax.axis_size("dp")
    grid_dev, width = grid_feat.shape[1:]
    nodes = node_feat.shape[1]
    nbrs = neighbours.shape[1]
    cap = send_rows.shape[2]
    rows = n * cap + nodes
    hc = width // n
    zc = 2 * hc // nd
    ny = n // 2
    steps = nd.bit_length() - 1
    out_rows = width // (n * nd)
    wscale = 1.0 / math.sqrt(nd * grid_dev * n)
    idx_rows = -(-nbrs // 8) * 8 + n
    idx_lanes = max(grid_dev, rows)
    vmem = pl.BlockSpec(memory_space=pltpu.VMEM)
    hbm = pl.BlockSpec(memory_space=pltpu.HBM)
    dma = pltpu.SemaphoreType.DMA
    one = dma(())
    outs = (
        jax.ShapeDtypeStruct((grid_dev, width), BF16),
        jax.ShapeDtypeStruct((nodes, width), BF16),
        jax.ShapeDtypeStruct((out_rows, width), F32),
        jax.ShapeDtypeStruct((out_rows, 2 * width), F32),
    )
    held = pl.pallas_call(
        functools.partial(heads_kernel, n, nd, wscale),
        out_shape=outs,
        in_specs=[hbm] * 7,
        out_specs=(vmem, vmem, vmem, vmem),
        scratch_shapes=[
            pltpu.VMEM((width, width), BF16),
            pltpu.VMEM((width, 2 * width), BF16),
            pltpu.VMEM((grid_dev, width), BF16),
            pltpu.VMEM((n, hc, hc), F32),
            pltpu.VMEM((nbrs, grid_dev), jnp.int32),
            pltpu.VMEM((n, cap), jnp.int32),
            pltpu.VMEM((n, n * nodes, grid_dev), F32),
            pltpu.VMEM((n, -(-idx_rows // 8) * 8, idx_lanes), jnp.int32),
            pltpu.VMEM((n, nodes, width), BF16),
            pltpu.VMEM((nd, n, nodes, width // ny), BF16),
            pltpu.VMEM((n, grid_dev, width), BF16),
            pltpu.VMEM((n, grid_dev, hc), BF16),
            pltpu.VMEM((n, 2, grid_dev, hc), BF16),
            pltpu.VMEM((2, n * nodes, hc), BF16),
            pltpu.VMEM((2, n * nodes, hc), F32),
            pltpu.VMEM((n, grid_dev, hc), BF16),
            pltpu.VMEM((grid_dev, width), BF16),
            pltpu.VMEM((nd, n * nodes, zc), BF16),
            pltpu.VMEM((nd, ny, n * nodes, zc), BF16),
            pltpu.VMEM((n, nd, nodes, zc), BF16),
            pltpu.VMEM((nodes, 2 * width), BF16),
            pltpu.VMEM((n, out_rows, hc), BF16),
            pltpu.VMEM((n, out_rows, hc), BF16),
            pltpu.VMEM((2, ny, nd, out_rows, zc), BF16),
            pltpu.VMEM((2 * nd, ny, out_rows, zc), BF16),
        ] + [
            pltpu.VMEM((n, nd >> (b + 1), 2, out_rows, hc), BF16) for b in range(steps)
        ] + [
            pltpu.VMEM((n, nd >> (b + 1), out_rows, hc), BF16) for b in range(steps)
        ] + [
            dma((8,)), one, one,
            one, one, dma((n,)),
            dma((nd + 1, ny)), one, dma((nd, ny)), one,
            one, one, dma((n,)),
            one, one, dma((n,)),
            one, one, dma((nd, ny)),
            one, one, one, one,
            dma((steps,)), dma((steps, n)),
            one, one, one, one,
        ],
        compiler_params=pltpu.CompilerParams(
            collective_id=0, has_side_effects=True, vmem_limit_bytes=28 * 1024 * 1024
        ),
        name="heads_apart_grads",
    )(*(
        pltpu.with_memory_space_constraint(x, pltpu.HBM)
        for x in (
            grid_feat[0], node_feat[0], cotangent[0], w_query, w_keyval,
            neighbours.T, send_rows[0],
        )
    ))
    d_grid, d_nodes, dw_query, dw_keyval = pl.pallas_call(
        copy_kernel, out_shape=outs, in_specs=[vmem] * 4, out_specs=(vmem,) * 4,
        compiler_params=pltpu.CompilerParams(vmem_limit_bytes=4 * 1024 * 1024),
        name="results",
    )(*held)
    return d_grid[None], d_nodes[None], dw_query, dw_keyval


def per_device(*args):
    n = lax.axis_size("mp")
    nd = lax.axis_size("dp")
    samples_dev, grid_dev, width = args[0].shape
    hc = width // n
    apart = (
        samples_dev == 1
        and n % 2 == 0
        and nd >= 4
        and nd & (nd - 1) == 0
        and hc % LANES == 0
        and 2 * hc % (nd * LANES) == 0
        and grid_dev % LANES == 0
        and width % (HEADS * n) == 0
        and LANES % (width // HEADS) == 0
        and width % (n * nd * 16) == 0
        and args[6].shape[2] * n <= 256
        and args[1].shape[1] * n <= 256
    )
    return heads_apart(*args) if apart else rows_apart(*args)


def solution(mesh):
    in_specs = (
        P(("groups", "dp"), "mp", None),
        P(("groups", "dp"), "mp", None),
        P(("groups", "dp"), "mp", None),
        P(),
        P(),
        P("mp", None),
        P("mp", None, None),
    )
    out_specs = (
        P(("groups", "dp"), "mp", None),
        P(("groups", "dp"), "mp", None),
        P(("groups", "mp", "dp"), None),
        P(("groups", "mp", "dp"), None),
    )
    return jax.shard_map(
        per_device, mesh=mesh, in_specs=in_specs, out_specs=out_specs, check_vma=False
    )
```
